128 devices in a mesh: region: 4 (over x), space: 32 (over z, y, core).
Axes of the slice: x: 4, y: 4, z: 4, core: 2. Of those that a mesh axis runs over, the one named last changes fastest.
Arguments:
- features: bfloat16 [2048, 64, 512], P(('region', 'space')), may hold values from -6 to 6
- fine_weight: bfloat16 [7, 64, 64], replicated, may hold values from -0.25 to 0.25
- down_weight: bfloat16 [8, 64, 128], replicated, may hold values from -0.25 to 0.25
- coarse_weight: bfloat16 [128, 128], replicated, may hold values from -0.5 to 0.5
- cotangent: bfloat16 [1024, 512, 128], P(('region', 'space')), may hold values from -6 to 6
- face_source: int32 [2048, 6], P(('region', 'space')), may hold values from -1 to 119, as said below
- face_requests: int32 [128, 24], P(('region', 'space')), may hold values from -1 to 95, as said below
- child_slot: int32 [2048], P(('region', 'space')), may hold values from 0 to 63, as said below
- parent_octant: int32 [128, 64], P(('region', 'space')), may hold values from -1 to 63, as said below
Outputs:
- grad_in: bfloat16 [2048, 64, 512], P(('region', 'space'))
- coarse_out: bfloat16 [1024, 512, 128], P(('region', 'space'))
- grad_fine: float32 [7, 64, 64], replicated
- grad_down: float32 [8, 64, 128], replicated
- grad_coarse: float32 [128, 128], replicated
The draws below stay inside these ranges and needn't reach their ends.
Inputs may be any that keep to these rules, and one draw needn't show every extreme that they name: `face_source`: -1 marks a face without neighbour. A code c below 96 names brick c // 6 of the same device and its face c % 6; a larger code names received slot c - 96 = k * 4 + s, slot s of what the device whose neighbour in direction k is this device sends in direction k. The face named is always the opposite face, d with its lowest bit flipped. Each used received slot is named by exactly one (brick, direction) of its receiver. face_requests[h, k * 4 + s] is brick * 6 + face of device h that h sends in slot s to its neighbour in direction k, or -1; in each (h, k) the used slots come first; slots toward a missing neighbour are -1; it agrees with face_source of the receiver; in every draw one device receives 4 faces from each of its neighbours. `child_slot`: owner * 2 + slot, owner counted within the sender's region; distinct on each device; in every region one owner receives 2 children from every device of the region. parent_octant[q, x * 2 + u] is parent * 8 + octant on device q for the child that device x of q's region sends in slot u to q, or -1 where none is sent; distinct on each device; some parents and octants receive no child.
All inputs are finite; a program needn't handle non-finite values.
Results may differ from the reference program's by a relative error of at most 0.0069.
Values may be sent and summed in bfloat16 or wider, within the bound.
A program may use at most 192 MiB of HBM per device.

```python
import math
import jax
import jax.numpy as jnp
import numpy as np
from jax import lax

EDGE = 8
CH_FINE = 64
CH_COARSE = 128
BRICK_DEV = 16
VOLUME = 512
HSLOT = 4
CSLOT = 2
PARENT_DEV = 8
BRICKS = 2048
PARENTS = 1024
N_REGION = 4
N_SPACE = 32


def halo_lists(key):
    peer_count = N_REGION * N_SPACE
    face_count = BRICK_DEV * 6
    far_step = N_SPACE // 4
    key_list = jax.random.split(jax.random.fold_in(key, 11), 6)
    device_ids = jnp.arange(peer_count)
    row_region = device_ids // N_SPACE
    row_space = device_ids % N_SPACE
    move_region = jnp.array([1, -1, 0, 0, 0, 0])
    move_space = jnp.array([0, 0, 1, -1, far_step, -far_step])
    from_region = row_region[:, None] - move_region[None, :]
    from_space = row_space[:, None] - move_space[None, :]
    inside = (from_region >= 0) & (from_region < N_REGION) & (from_space >= 0) & (from_space < N_SPACE)
    sender_ids = from_region * N_SPACE + from_space
    counts = jax.random.randint(key_list[0], (peer_count, 6), HSLOT // 2, HSLOT + 1)
    busiest = jax.random.randint(key_list[1], (), 0, peer_count)
    counts = jnp.where(device_ids[:, None] == busiest, HSLOT, counts)
    counts = jnp.where(inside, counts, 0)
    used_slot = (jnp.arange(HSLOT)[None, None, :] < counts[:, :, None]).reshape(peer_count, 6 * HSLOT)
    slot_rank = jnp.cumsum(used_slot.astype(jnp.int32), axis=1) - 1
    orders = jax.vmap(lambda sub_key: jax.random.permutation(sub_key, face_count))(jax.random.split(key_list[2], peer_count))
    pair_index = jnp.take_along_axis(orders, jnp.clip(slot_rank, 0, face_count - 1), axis=1)
    pair_index = jnp.where(used_slot, pair_index, face_count)
    directions = jnp.arange(face_count) % 6
    bricks_here = jnp.arange(face_count) // 6
    offsets = jax.random.randint(key_list[3], (peer_count, face_count), 1, BRICK_DEV)
    local_codes = (bricks_here[None, :] + offsets) % BRICK_DEV * 6 + (directions[None, :] ^ 1)
    empty_face = jax.random.randint(key_list[4], (peer_count, face_count), 0, 4) == 0
    local_codes = jnp.where(empty_face, -1, local_codes)
    remote_codes = face_count + jnp.arange(6 * HSLOT)

    def place_codes(code_row, target_row):
        return code_row.at[target_row].set(remote_codes, mode='drop')
    code_table = jax.vmap(place_codes)(local_codes, pair_index)
    sender_brick = jax.random.randint(key_list[5], (peer_count, 6 * HSLOT), 0, BRICK_DEV)
    send_codes = jnp.where(used_slot, sender_brick * 6 + (pair_index % 6 ^ 1), -1).reshape(peer_count, 6, HSLOT)
    target_rows = jnp.where(inside, sender_ids, peer_count)[:, :, None] + jnp.zeros((1, 1, HSLOT), jnp.int32)
    direction_cols = jnp.arange(6)[None, :, None]
    slot_cols = jnp.arange(HSLOT)[None, None, :]
    requests = jnp.full((peer_count, 6, HSLOT), -1, jnp.int32).at[target_rows, direction_cols, slot_cols].set(send_codes, mode='drop')
    return (code_table.reshape(peer_count * BRICK_DEV, 6).astype(jnp.int32), requests.reshape(peer_count, 6 * HSLOT).astype(jnp.int32))


def child_lists(key):
    peer_count = N_REGION * N_SPACE
    slot_count = N_SPACE * CSLOT
    key_list = jax.random.split(jax.random.fold_in(key, 23), 4)
    busiest = jax.random.randint(key_list[0], (N_REGION,), 0, N_SPACE)
    owner_of_slot = jnp.arange(slot_count) // CSLOT
    region_of = jnp.arange(peer_count) // N_SPACE
    shuffled = jax.vmap(lambda sub_key: jax.random.permutation(sub_key, slot_count))(jax.random.split(key_list[1], peer_count))
    scores = shuffled + jnp.where(owner_of_slot[None, :] == busiest[region_of][:, None], slot_count, 0)
    chosen = jnp.argsort(-scores, axis=1)[:, :BRICK_DEV]
    mixing = jax.vmap(lambda sub_key: jax.random.permutation(sub_key, BRICK_DEV))(jax.random.split(key_list[2], peer_count))
    slot_table = jnp.take_along_axis(chosen, mixing, axis=1)
    filled = jax.vmap(lambda slot_row: jnp.zeros((slot_count,), jnp.int32).at[slot_row].set(1))(chosen)
    incoming = filled.reshape(N_REGION, N_SPACE, N_SPACE, CSLOT).transpose(0, 2, 1, 3).reshape(peer_count, slot_count)
    slot_rank = jnp.cumsum(incoming, axis=1) - 1
    octant_order = jax.vmap(lambda sub_key: jax.random.permutation(sub_key, PARENT_DEV * 8))(jax.random.split(key_list[3], peer_count))
    octant_codes = jnp.take_along_axis(octant_order, jnp.clip(slot_rank, 0, PARENT_DEV * 8 - 1), axis=1)
    octant_table = jnp.where(incoming > 0, octant_codes, -1)
    return (slot_table.reshape(peer_count * BRICK_DEV).astype(jnp.int32), octant_table.astype(jnp.int32))


def draw_face_source(key, part):
    return halo_lists(key)[0]


def draw_face_requests(key, part):
    return halo_lists(key)[1]


def draw_child_slot(key, part):
    return child_lists(key)[0]


def draw_parent_octant(key, part):
    return child_lists(key)[1]


def block_levels(stream_key, shape, shards, low, largest):
    gain = 1.0
    for dim, parts in shards:
        heights = jax.random.uniform(jax.random.fold_in(jax.random.fold_in(stream_key, 6), dim), (parts,), jnp.float32, low / len(shards), largest / len(shards))
        gain = gain * jnp.repeat(jnp.exp(heights), shape[dim] // parts).reshape((-1,) + (1,) * (len(shape) - 1 - dim))
    return gain


def noise(own_key, extent, deviation, bound, cuts=(), held_as=jnp.bfloat16):
    entries = deviation * jax.random.normal(own_key, extent, jnp.float32)
    if cuts:
        entries = entries * block_levels(own_key, extent, cuts, -0.22, 0.18)
    return jnp.clip(entries, -bound, bound).astype(held_as)


def setup_inputs(seed: int = 0) -> dict:
    keys = jax.random.split(jax.random.key(seed), 10)
    features = noise(keys[0], (BRICKS, CH_FINE, VOLUME), 1.0, 6.0, ((0, 128),))
    fine_weight = noise(keys[1], (7, CH_FINE, CH_FINE), (7 * CH_FINE) ** -0.5, 0.25)
    down_weight = noise(keys[2], (8, CH_FINE, CH_COARSE), (8 * CH_FINE) ** -0.5, 0.25)
    coarse_weight = noise(keys[3], (CH_COARSE, CH_COARSE), CH_COARSE ** -0.5, 0.5)
    cotangent = noise(keys[4], (PARENTS, VOLUME, CH_COARSE), 1.0, 6.0, ((0, 128),))
    face_source = draw_face_source(jax.random.fold_in(keys[9], 71), 0)
    face_requests = draw_face_requests(jax.random.fold_in(keys[9], 71), 0)
    child_slot = draw_child_slot(jax.random.fold_in(keys[9], 71), 0)
    parent_octant = draw_parent_octant(jax.random.fold_in(keys[9], 71), 0)
    return {"features": features, "fine_weight": fine_weight, "down_weight": down_weight, "coarse_weight": coarse_weight, "cotangent": cotangent, "face_source": face_source, "face_requests": face_requests, "child_slot": child_slot, "parent_octant": parent_octant}


def silu_slope(values):
    sigma = jax.nn.sigmoid(values)
    return sigma * (1.0 + values * (1.0 - sigma))

def face_voxels(brick_edge):
    voxels = np.arange(brick_edge ** 3)
    position = np.stack([voxels // (brick_edge * brick_edge), voxels // brick_edge % brick_edge, voxels % brick_edge])
    listing = []
    for face_index in range(6):
        wanted = 0 if face_index % 2 == 0 else brick_edge - 1
        listing.append(voxels[position[face_index // 2] == wanted])
    return listing

def tap_sources(brick_edge):
    volume = brick_edge ** 3
    listing = face_voxels(brick_edge)
    sources = []
    for face_index in range(6):
        stride = brick_edge ** (2 - face_index // 2)
        moving = -stride if face_index % 2 == 0 else stride
        source = np.arange(volume) + moving
        source[listing[face_index]] = volume + np.arange(brick_edge * brick_edge)
        sources.append(source)
    return sources

def octant_voxels(brick_edge):
    half_edge = brick_edge // 2
    grid_index = np.arange(half_edge ** 3)
    inner_pos = np.stack([grid_index // (half_edge * half_edge), grid_index // half_edge % half_edge, grid_index % half_edge])
    row_list = []
    for octant in range(8):
        corner = [octant // 4, octant // 2 % 2, octant % 2]
        row_list.append((2 * inner_pos[0] + corner[0]) * brick_edge * brick_edge + (2 * inner_pos[1] + corner[1]) * brick_edge + 2 * inner_pos[2] + corner[2])
    return np.stack(row_list)

def neighbour_tables(regions, owners):
    far_step = owners // 4
    move_list = [(1, 0), (-1, 0), (0, 1), (0, -1), (0, far_step), (0, -far_step)]
    device_ids = np.arange(regions * owners)
    row_region = device_ids // owners
    row_space = device_ids % owners
    senders = []
    sender_ok = []
    receivers = []
    receiver_ok = []
    for move_region, move_space in move_list:
        for direction_sign, target_list, flag_list in ((-1, senders, sender_ok), (1, receivers, receiver_ok)):
            other_region = row_region + direction_sign * move_region
            other_space = row_space + direction_sign * move_space
            inside = (other_region >= 0) & (other_region < regions) & (other_space >= 0) & (other_space < owners)
            target_list.append(np.where(inside, other_region * owners + other_space, 0))
            flag_list.append(inside)
    return (np.stack(senders, axis=1), np.stack(sender_ok, axis=1), np.stack(receivers, axis=1), np.stack(receiver_ok, axis=1))

def reference(features, fine_weight, down_weight, coarse_weight, cotangent, face_source, face_requests, child_slot, parent_octant):
    peer_count = N_REGION * N_SPACE
    channels = CH_FINE
    volume = EDGE ** 3
    plane_size = EDGE * EDGE
    face_count = BRICK_DEV * 6
    face_width = channels * plane_size
    octant_size = volume // 8
    slot_total = N_SPACE * CSLOT
    listing = face_voxels(EDGE)
    sources = tap_sources(EDGE)
    octants = octant_voxels(EDGE)
    inverse_octants = np.argsort(octants.reshape(-1))
    senders, sender_ok, receivers, receiver_ok = neighbour_tables(N_REGION, N_SPACE)
    fine32 = fine_weight.astype(jnp.float32)
    down32 = down_weight.astype(jnp.float32)
    coarse32 = coarse_weight.astype(jnp.float32)
    per_device = features.reshape(peer_count, BRICK_DEV, channels, volume)
    codes_all = face_source.reshape(peer_count, face_count)

    def faces_of(own):
        stacked = jnp.stack([own[:, :, listing[face_index]] for face_index in range(6)], axis=1)
        return stacked.reshape(face_count, face_width)

    def outgoing(item):
        own, wanted = item
        table = jnp.concatenate([faces_of(own), jnp.zeros((1, face_width), own.dtype)], axis=0)
        return table[jnp.where(wanted >= 0, wanted, face_count)]

    def arriving(table, source_rows, allowed):
        part_list = []
        for direction in range(6):
            piece = table[source_rows[:, direction], direction]
            part_list.append(jnp.where(jnp.asarray(allowed[:, direction])[:, None, None], piece, jnp.zeros_like(piece)))
        return jnp.stack(part_list, axis=1).reshape(peer_count, 6 * HSLOT, face_width)
    sent = lax.map(outgoing, (per_device, face_requests)).reshape(peer_count, 6, HSLOT, face_width)
    received = arriving(sent, senders, sender_ok)

    def tap_stack(own, arrived, face_codes):
        table = jnp.concatenate([faces_of(own), arrived, jnp.zeros((1, face_width), own.dtype)], axis=0)
        picked = table[jnp.where(face_codes >= 0, face_codes, table.shape[0] - 1)]
        picked = picked.reshape(BRICK_DEV, 6, channels, plane_size)
        tap_list = [own]
        for face_index in range(6):
            extended = jnp.concatenate([own, picked[:, face_index]], axis=-1)
            tap_list.append(extended[:, :, sources[face_index]])
        return jnp.stack(tap_list, axis=1)

    def forward_fine(item):
        own, arrived, face_codes = item
        tap_values = tap_stack(own, arrived, face_codes).astype(jnp.float32)
        hidden = jnp.einsum('btcv,tco->bov', tap_values, fine32)
        active = jax.nn.silu(hidden).astype(jnp.bfloat16)
        corners = active[:, :, octants].astype(jnp.float32)
        return jnp.einsum('bcts,tco->bso', corners, down32).astype(jnp.bfloat16)
    reduced = lax.map(forward_fine, (per_device, received, codes_all))
    slot_rows = child_slot.reshape(peer_count, BRICK_DEV)

    def fill_slots(values, slot_row):
        return jnp.zeros((slot_total, octant_size, CH_COARSE), jnp.bfloat16).at[slot_row].set(values)

    def to_owner(buffer):
        shaped = buffer.reshape(N_REGION, N_SPACE, N_SPACE, CSLOT, octant_size, CH_COARSE)
        return shaped.transpose(0, 2, 1, 3, 4, 5).reshape(peer_count, slot_total, octant_size, CH_COARSE)
    arrived_children = to_owner(jax.vmap(fill_slots)(reduced, slot_rows))
    placed = jnp.where(parent_octant >= 0, parent_octant, PARENT_DEV * 8)

    def assemble(values, target_row):
        return jnp.zeros((PARENT_DEV * 8, octant_size, CH_COARSE), jnp.bfloat16).at[target_row].set(values, mode='drop')
    coarse_in = jax.vmap(assemble)(arrived_children, placed).reshape(PARENTS, volume, CH_COARSE)
    coarse_in32 = coarse_in.astype(jnp.float32)
    coarse_pre = jnp.einsum('pvc,co->pvo', coarse_in32, coarse32)
    coarse_out = jax.nn.silu(coarse_pre).astype(jnp.bfloat16)
    coarse_grad = (cotangent.astype(jnp.float32) * silu_slope(coarse_pre)).astype(jnp.bfloat16)
    grad_coarse = jnp.einsum('pvc,pvo->co', coarse_in32, coarse_grad.astype(jnp.float32)) / math.sqrt(PARENTS * volume)
    back_coarse = jnp.einsum('pvo,co->pvc', coarse_grad.astype(jnp.float32), coarse32).astype(jnp.bfloat16)
    back_table = jnp.concatenate([back_coarse.reshape(peer_count, PARENT_DEV * 8, octant_size, CH_COARSE), jnp.zeros((peer_count, 1, octant_size, CH_COARSE), jnp.bfloat16)], axis=1)
    back_slots = jax.vmap(lambda table_row, target_row: table_row[target_row])(back_table, placed)
    returned = to_owner(back_slots)
    child_grads = jax.vmap(lambda table_row, slot_row: table_row[slot_row])(returned, slot_rows)

    def backward_fine(item):
        own, arrived, face_codes, child_grad = item
        tap_values = tap_stack(own, arrived, face_codes).astype(jnp.float32)
        hidden = jnp.einsum('btcv,tco->bov', tap_values, fine32)
        active = jax.nn.silu(hidden).astype(jnp.bfloat16)
        corners = active[:, :, octants].astype(jnp.float32)
        child32 = child_grad.astype(jnp.float32)
        grad_down = jnp.einsum('bcts,bso->tco', corners, child32)
        grad_corners = jnp.einsum('bso,tco->bcts', child32, down32)
        grad_active = grad_corners.reshape(BRICK_DEV, channels, volume)[:, :, inverse_octants]
        grad_hidden = (grad_active * silu_slope(hidden)).astype(jnp.bfloat16).astype(jnp.float32)
        grad_fine = jnp.einsum('btcv,bov->tco', tap_values, grad_hidden)
        tap_grad = jnp.einsum('tco,bov->btcv', fine32, grad_hidden)
        grad_sum = tap_grad[:, 0]
        plane_list = []
        for face_index in range(6):
            source = sources[face_index]
            own_part = source < volume
            grad_sum = grad_sum.at[:, :, source[own_part]].add(tap_grad[:, face_index + 1][:, :, own_part])
            plane_list.append(tap_grad[:, face_index + 1][:, :, listing[face_index]])
        plane_grad = jnp.stack(plane_list, axis=1).astype(jnp.bfloat16).reshape(face_count, face_width)
        return (grad_down, grad_fine, grad_sum, plane_grad)
    down_parts, fine_parts, grad_sums, plane_grads = lax.map(backward_fine, (per_device, received, codes_all, child_grads))
    remote_index = jnp.where(codes_all >= face_count, codes_all - face_count, 6 * HSLOT)

    def slot_fill(values, index_row):
        return jnp.zeros((6 * HSLOT, face_width), jnp.bfloat16).at[index_row].set(values, mode='drop')
    back_faces = jax.vmap(slot_fill)(plane_grads, remote_index).reshape(peer_count, 6, HSLOT, face_width)
    answered = arriving(back_faces, receivers, receiver_ok)

    def finish(item):
        grad_sum, plane_grad, face_codes, wanted, answers = item
        local_index = jnp.where((face_codes >= 0) & (face_codes < face_count), face_codes, face_count)
        request_index = jnp.where(wanted >= 0, wanted, face_count)
        face_grad = jnp.zeros((face_count + 1, face_width), jnp.float32)
        face_grad = face_grad.at[local_index].add(plane_grad.astype(jnp.float32))
        face_grad = face_grad.at[request_index].add(answers.astype(jnp.float32))
        face_grad = face_grad[:face_count].reshape(BRICK_DEV, 6, channels, plane_size)
        for face_index in range(6):
            grad_sum = grad_sum.at[:, :, listing[face_index]].add(face_grad[:, face_index])
        return grad_sum.astype(jnp.bfloat16)
    grad_in = lax.map(finish, (grad_sums, plane_grads, codes_all, face_requests, answered)).reshape(BRICKS, channels, volume)
    grad_fine = lax.optimization_barrier(jnp.sum(fine_parts, axis=0)) / math.sqrt(BRICKS * volume)
    grad_down = lax.optimization_barrier(jnp.sum(down_parts, axis=0)) / math.sqrt(BRICKS * volume)
    return (grad_in, coarse_out, grad_fine, grad_down, grad_coarse)
```

```python
import functools
import math

import jax
import jax.numpy as jnp
import numpy as np
from jax import lax
from jax.experimental import pallas as pl
from jax.experimental.pallas import tpu as pltpu
from jax.sharding import PartitionSpec as P

EDGE = 8
BF = jnp.bfloat16
F32 = jnp.float32
MESH = pl.DeviceIdType.MESH
NT = (((1,), (1,)), ((), ()))
TN = (((0,), (0,)), ((), ()))
VMEM_SPEC = pl.BlockSpec(memory_space=pltpu.VMEM)
SMEM_SPEC = pl.BlockSpec(memory_space=pltpu.SMEM)
ANY_SPEC = pl.BlockSpec(memory_space=pl.ANY)
ROWS = 128
LANES = 256
CHUNK = 8


def row_of(i, j, k):
    return i * 16 + j * 4 + k


def make_tables():
    order = np.zeros((512, 512), np.float32)
    for i in range(8):
        for j in range(8):
            for k in range(8):
                q = (j % 2) * 2 + k % 2
                order[q * 128 + row_of(i, j // 2, k // 2), i * 64 + j * 8 + k] = 1
    face = np.zeros((128, 128), np.float32)
    shift = np.zeros((4, 128, 192), np.float32)
    for i in range(8):
        for m in range(4):
            face[i * 4 + m, row_of(i, 0, m)] = 1
            face[32 + i * 4 + m, row_of(i, 3, m)] = 1
            face[64 + i * 4 + m, row_of(i, m, 0)] = 1
            face[96 + i * 4 + m, row_of(i, m, 3)] = 1
            for n in range(4):
                r = row_of(i, m, n)
                shift[0, r, row_of(i, m + 1, n) if m < 3 else 128 + i * 4 + n] = 1
                shift[1, r, row_of(i, m - 1, n) if m > 0 else 128 + i * 4 + n] = 1
                shift[2, r, row_of(i, m, n + 1) if n < 3 else 160 + i * 4 + m] = 1
                shift[3, r, row_of(i, m, n - 1) if n > 0 else 160 + i * 4 + m] = 1
    back = np.zeros((4, 160, 128), np.float32)
    back[:, :128] = shift[:, :, :128]
    back[0, 128:] = face[0:32]
    back[1, 128:] = face[32:64]
    back[2, 128:] = face[64:96]
    back[3, 128:] = face[96:128]
    spread = np.zeros((2, 128, 192), np.float32)
    for half in range(2):
        j_face = face[0:32] if half == 0 else face[32:64]
        parts = [j_face, j_face, face[64:96], face[64:96], face[96:128], face[96:128]]
        spread[half] = np.concatenate(parts, axis=0).T
    cast = lambda a: np.asarray(a, dtype=BF)
    return cast(order), cast(face), cast(shift), cast(back), cast(spread)


ORDER, FACE, SHIFT, BACK, SPREAD = make_tables()


def dot(a, b, dims=(((1,), (0,)), ((), ()))):
    return lax.dot_general(a, b, dims, preferred_element_type=F32)


def first_kernel(req_ref, slot_ref, feat_ref, cot_ref, order_ref, face_ref,
                 x_ref, table_ref, out_ref, cots_ref):
    def gather_cot(s, carry):
        cots_ref[s] = cot_ref[jnp.maximum(slot_ref[0, s], 0)]
        return carry

    lax.fori_loop(0, 64, gather_cot, 0, unroll=4)

    def four(g, carry):
        block = feat_ref[pl.ds(g * 4, 4)].reshape(256, 512)
        turned = dot(order_ref[...], block, NT).astype(BF)
        for n in range(4):
            b = g * 4 + n
            x = jnp.concatenate(
                [turned[q * 128:(q + 1) * 128, n * 64:(n + 1) * 64] for q in range(4)], axis=1
            )
            x_ref[b] = x
            f = dot(face_ref[...], x).astype(BF)
            base = b * 6
            table_ref[base] = jnp.concatenate([x[0:16, 0:128], x[0:16, 128:256]], axis=0)
            table_ref[base + 1] = jnp.concatenate([x[112:128, 0:128], x[112:128, 128:256]], axis=0)
            table_ref[base + 2] = f[0:32, 0:128]
            table_ref[base + 3] = f[32:64, 128:256]
            table_ref[base + 4] = jnp.concatenate([f[64:96, 0:64], f[64:96, 128:192]], axis=1)
            table_ref[base + 5] = jnp.concatenate([f[96:128, 64:128], f[96:128, 192:256]], axis=1)
        return carry

    lax.fori_loop(0, 4, four, 0)

    def gather_face(s, carry):
        out_ref[s] = table_ref[jnp.maximum(req_ref[0, s], 0)]
        return carry

    lax.fori_loop(0, 24, gather_face, 0, unroll=4)


def neighbours(regions, owners):
    far = owners // 4
    return [(1, 0), (-1, 0), (0, 1), (0, -1), (0, far), (0, -far)]


def face_moves(regions, owners, my_r, my_s, backward):
    sign = -1 if backward else 1
    for k, (dr, ds) in enumerate(neighbours(regions, owners)):
        to_r, to_s = my_r + sign * dr, my_s + sign * ds
        from_r, from_s = my_r - sign * dr, my_s - sign * ds
        can_send = (to_r >= 0) & (to_r < regions) & (to_s >= 0) & (to_s < owners)
        can_take = (from_r >= 0) & (from_r < regions) & (from_s >= 0) & (from_s < owners)
        yield k, (to_r, to_s), can_send, can_take


def greet_region(regions, owners, my_r, my_s):
    barrier = pltpu.get_barrier_semaphore()

    def greet(step, carry):
        peer = lax.rem(my_s + step, owners)
        pl.semaphore_signal(barrier, inc=1, device_id=(my_r, peer), device_id_type=MESH)
        return carry

    lax.fori_loop(1, owners, greet, 0)

    @pl.when(my_r > 0)
    def _():
        pl.semaphore_signal(barrier, inc=1, device_id=(my_r - 1, my_s), device_id_type=MESH)

    @pl.when(my_r < regions - 1)
    def _():
        pl.semaphore_signal(barrier, inc=1, device_id=(my_r + 1, my_s), device_id_type=MESH)

    lower = jnp.where(my_r > 0, 1, 0)
    upper = jnp.where(my_r < regions - 1, 1, 0)
    pl.semaphore_wait(barrier, owners - 1 + lower + upper)


def send_faces(regions, owners, my_r, my_s, backward, src, dst, send_sem, recv_sem):
    for k, target, can_send, can_take in face_moves(regions, owners, my_r, my_s, backward):
        copy = pltpu.make_async_remote_copy(
            src_ref=src.at[k], dst_ref=dst.at[k], send_sem=send_sem.at[k],
            recv_sem=recv_sem.at[k], device_id=target, device_id_type=MESH)

        @pl.when(can_send)
        def _():
            copy.start()


def wait_faces(regions, owners, my_r, my_s, backward, src, dst, send_sem, recv_sem):
    for k, target, can_send, can_take in face_moves(regions, owners, my_r, my_s, backward):
        copy = pltpu.make_async_remote_copy(
            src_ref=src.at[k], dst_ref=dst.at[k], send_sem=send_sem.at[k],
            recv_sem=recv_sem.at[k], device_id=target, device_id_type=MESH)

        @pl.when(can_send)
        def _():
            copy.wait_send()

        @pl.when(can_take)
        def _():
            copy.wait_recv()


def start_blocks(owners, my_r, my_s, src, dst, send_sem, recv_sem):
    def start(step, carry):
        peer = lax.rem(my_s + step, owners)
        pltpu.make_async_remote_copy(
            src_ref=src.at[peer], dst_ref=dst.at[my_s], send_sem=send_sem.at[peer],
            recv_sem=recv_sem.at[my_s], device_id=(my_r, peer), device_id_type=MESH).start()
        return carry

    lax.fori_loop(1, owners, start, 0)


def wait_blocks(owners, my_r, my_s, src, dst, send_sem, recv_sem):
    def wait(step, carry):
        peer = lax.rem(my_s + step, owners)
        copy = pltpu.make_async_remote_copy(
            src_ref=src.at[peer], dst_ref=dst.at[peer], send_sem=send_sem.at[peer],
            recv_sem=recv_sem.at[peer], device_id=(my_r, peer), device_id_type=MESH)
        copy.wait_send()
        copy.wait_recv()
        return carry

    lax.fori_loop(1, owners, wait, 0)


def exchange_kernel(regions, owners, face_ref, cots_ref, got_face_ref, got_cot_ref,
                    own, fsend, frecv, bsend, brecv, lsem):
    my_r = lax.axis_index("region")
    my_s = lax.axis_index("space")
    greet_region(regions, owners, my_r, my_s)
    send_faces(regions, owners, my_r, my_s, False, face_ref, got_face_ref, fsend, frecv)
    start_blocks(owners, my_r, my_s, cots_ref, got_cot_ref, bsend, brecv)
    take = pltpu.make_async_copy(cots_ref.at[my_s], own, lsem.at[0])
    take.start()
    take.wait()
    put = pltpu.make_async_copy(own, got_cot_ref.at[my_s], lsem.at[1])
    put.start()
    put.wait()
    wait_faces(regions, owners, my_r, my_s, False, face_ref, got_face_ref, fsend, frecv)
    wait_blocks(owners, my_r, my_s, cots_ref, got_cot_ref, bsend, brecv)


def silu_parts(v):
    s = 1.0 / (1.0 + jnp.exp(-v))
    return v * s, s * (1.0 + v * (1.0 - s))


def place(w_ref, base, q_in, q_out, block):
    w_ref[base + q_in * 64:base + q_in * 64 + 64, q_out * 64:q_out * 64 + 64] = block


def fill_weights(fine_ref, w_ref, wt_ref):
    w_ref[...] = jnp.zeros_like(w_ref)
    wt_ref[...] = jnp.zeros_like(wt_ref)
    same = [(q, q) for q in range(4)]
    up_j = [(0, 2), (1, 3)]
    down_j = [(2, 0), (3, 1)]
    up_k = [(0, 1), (2, 3)]
    down_k = [(1, 0), (3, 2)]
    plan = [
        (0, 0, 0, same), (1, 1, 2, same), (2, 2, 1, same),
        (3, 0, 0, up_j), (3, 3, 3, down_j), (4, 0, 0, down_j), (4, 3, 3, up_j),
        (5, 0, 0, up_k), (5, 4, 4, down_k), (6, 0, 0, down_k), (6, 4, 4, up_k),
    ]
    for tap, fwd, bwd, pairs in plan:
        w = fine_ref[tap]
        wt = w.astype(F32).T.astype(BF)
        for q_in, q_out in pairs:
            place(w_ref, fwd * 256, q_in, q_out, w)
            place(wt_ref, bwd * 256, q_out, q_in, wt)
    return plan


def compute_kernel(scale_fine, scale_coarse, code_ref, slot_ref, x_ref, table_ref, inf_ref,
                   cot_ref, fine_ref, down_ref, coarse_ref, shift_ref, back_ref,
                   gin_ref, fg_ref, bf_ref, co_ref, grad_ref,
                   w_ref, wt_ref, taps_ref, act_ref, gh_ref, red_ref, cg_ref, ch_ref):
    plan = fill_weights(fine_ref, w_ref, wt_ref)
    fg_ref[...] = jnp.zeros_like(fg_ref)
    bf_ref[...] = jnp.zeros_like(bf_ref)
    lane = lax.broadcasted_iota(jnp.int32, (ROWS, LANES), 1)
    k_low = (lane % 128) < 64
    k_low32 = k_low[0:32]
    face_total = table_ref.shape[0]

    def halo(b, d):
        code = code_ref[b, d]
        own = table_ref[jnp.clip(code, 0, face_total - 1)]
        got = inf_ref[jnp.clip(code - face_total, 0, inf_ref.shape[0] - 1)]
        picked = jnp.where(code >= face_total, got, own)
        return jnp.where(code >= 0, picked, jnp.zeros_like(picked))

    def one(b, carry):
        x = x_ref[b]
        h = [halo(b, d) for d in range(6)]
        hi_m = jnp.concatenate([h[0][0:16], h[0][16:32]], axis=1)
        hi_p = jnp.concatenate([h[1][0:16], h[1][16:32]], axis=1)
        hj = jnp.concatenate([h[3], h[2]], axis=1)
        hk = jnp.concatenate(
            [h[5][:, 0:64], h[4][:, 0:64], h[5][:, 64:128], h[4][:, 64:128]], axis=1)
        ext = jnp.concatenate([x, hj, hk], axis=0)
        tj = jnp.concatenate(
            [dot(shift_ref[0], ext[:, 0:128]), dot(shift_ref[1], ext[:, 128:256])], axis=1)
        tk = jnp.where(k_low, dot(shift_ref[2], ext), dot(shift_ref[3], ext))
        taps = jnp.concatenate([
            x,
            jnp.concatenate([hi_m, x[0:112]], axis=0),
            jnp.concatenate([x[16:128], hi_p], axis=0),
            tj.astype(BF), tk.astype(BF)], axis=1)
        row = pl.multiple_of(b * ROWS, ROWS)
        taps_ref[pl.ds(row, ROWS), :] = taps
        hidden = dot(taps, w_ref[...])
        act, slope = silu_parts(hidden)
        act = act.astype(BF)
        even = jnp.concatenate([act[32 * n:32 * n + 16] for n in range(4)], axis=0)
        odd = jnp.concatenate([act[32 * n + 16:32 * n + 32] for n in range(4)], axis=0)
        pair = jnp.concatenate([even, odd], axis=1)
        half = pl.multiple_of(b * 64, 64)
        act_ref[pl.ds(half, 64), :] = pair
        reduced = dot(pair, down_ref[...]).astype(BF)
        red_ref[pl.ds(half, 64), :] = reduced
        slot = slot_ref[b]
        c_out, c_slope = silu_parts(dot(reduced, coarse_ref[...]))
        co_ref[slot] = c_out.astype(BF)
        c_grad = (cot_ref[slot].astype(F32) * c_slope).astype(BF)
        cg_ref[pl.ds(half, 64), :] = c_grad
        child = dot(c_grad, coarse_ref[...], NT).astype(BF)
        ch_ref[pl.ds(half, 64), :] = child
        ga = dot(child, down_ref[...], NT)
        pieces = []
        for n in range(4):
            pieces += [ga[16 * n:16 * n + 16, 0:256], ga[16 * n:16 * n + 16, 256:512]]
        gh = (jnp.concatenate(pieces, axis=0) * slope).astype(BF)
        gh_ref[pl.ds(row, ROWS), :] = gh
        gj = jnp.concatenate(
            [dot(back_ref[0], gh[:, 0:128]), dot(back_ref[1], gh[:, 128:256])], axis=1).astype(BF)
        gk_low = dot(back_ref[2], gh)
        gk_high = dot(back_ref[3], gh)
        gk = jnp.where(k_low, gk_low[0:128], gk_high[0:128]).astype(BF)
        gkf = jnp.where(k_low32, gk_low[128:160], gk_high[128:160]).astype(BF)
        blank = jnp.zeros((16, LANES), BF)
        bwd = jnp.concatenate([
            gh,
            jnp.concatenate([blank, gh[0:112]], axis=0),
            jnp.concatenate([gh[16:128], blank], axis=0),
            gj[0:128], gk], axis=1)
        gin_ref[b] = dot(bwd, wt_ref[...])
        p0 = dot(gh[0:16], wt_ref[512:768, :]).astype(BF)
        p1 = dot(gh[112:128], wt_ref[256:512, :]).astype(BF)
        pj = dot(gj[128:160], wt_ref[768:1024, :]).astype(BF)
        pk = dot(gkf, wt_ref[1024:1280, :]).astype(BF)
        planes = [
            jnp.concatenate([p0[:, 0:128], p0[:, 128:256]], axis=0),
            jnp.concatenate([p1[:, 0:128], p1[:, 128:256]], axis=0),
            pj[:, 128:256],
            pj[:, 0:128],
            jnp.concatenate([pk[:, 64:128], pk[:, 192:256]], axis=1),
            jnp.concatenate([pk[:, 0:64], pk[:, 128:192]], axis=1),
        ]
        for d in range(6):
            code = code_ref[b, d]
            plane = planes[d]

            @pl.when(code >= face_total)
            def _():
                bf_ref[code - face_total] = plane

            @pl.when((code >= 0) & (code < face_total))
            def _():
                fg_ref[code] += plane.astype(F32)
        return carry

    lax.fori_loop(0, x_ref.shape[0], one, 0)
    fine = dot(taps_ref[...], gh_ref[...], TN) * scale_fine
    sums = [None] * 7
    for tap, fwd, bwd, pairs in plan:
        for q_in, q_out in pairs:
            part = fine[fwd * 256 + q_in * 64:fwd * 256 + q_in * 64 + 64,
                        q_out * 64:q_out * 64 + 64]
            sums[tap] = part if sums[tap] is None else sums[tap] + part
    sums.append(jnp.zeros_like(sums[0]))
    for n in range(4):
        grad_ref[n * 64:n * 64 + 64, :] = jnp.concatenate([sums[2 * n], sums[2 * n + 1]], axis=1)
    grad_ref[256:768, :] = dot(act_ref[...], ch_ref[...], TN) * scale_fine
    grad_ref[768:896, :] = dot(red_ref[...], cg_ref[...], TN) * scale_coarse


def greet_all(regions, owners, my_r, my_s):
    barrier = pltpu.get_barrier_semaphore()
    count = regions * owners
    me = my_r * owners + my_s

    def greet(step, carry):
        peer = lax.rem(me + step, count)
        pl.semaphore_signal(barrier, inc=1, device_id=(peer // owners, lax.rem(peer, owners)),
                            device_id_type=MESH)
        return carry

    lax.fori_loop(1, count, greet, 0)
    pl.semaphore_wait(barrier, count - 1)


def answer_kernel(regions, owners, face_ref, blocks_ref, grad_ref, got_face_ref, got_block_ref,
                  total_ref, own, parts, mine, fsend, frecv, bsend, brecv, lsem,
                  rsend, rrecv, gsend, grecv):
    my_r = lax.axis_index("region")
    my_s = lax.axis_index("space")
    count = regions * owners
    me = my_r * owners + my_s
    chunks = grad_ref.shape[0]
    greet_all(regions, owners, my_r, my_s)
    send_faces(regions, owners, my_r, my_s, True, face_ref, got_face_ref, fsend, frecv)

    def spot(peer):
        return (peer // owners, lax.rem(peer, owners))

    def reduce_copy(slot, peer):
        return pltpu.make_async_remote_copy(
            src_ref=grad_ref.at[jnp.minimum(peer, chunks - 1)], dst_ref=parts.at[slot],
            send_sem=rsend.at[peer], recv_sem=rrecv.at[slot], device_id=spot(peer),
            device_id_type=MESH)

    def gather_copy(chunk, peer):
        return pltpu.make_async_remote_copy(
            src_ref=mine, dst_ref=total_ref.at[jnp.minimum(chunk, chunks - 1)],
            send_sem=gsend.at[peer], recv_sem=grecv.at[chunk], device_id=spot(peer),
            device_id_type=MESH)

    def start_reduce(step, carry):
        peer = lax.rem(me + step, count)

        @pl.when(peer < chunks)
        def _():
            reduce_copy(me, peer).start()
        return carry

    lax.fori_loop(1, count, start_reduce, 0)
    start_blocks(owners, my_r, my_s, blocks_ref, got_block_ref, bsend, brecv)
    take = pltpu.make_async_copy(blocks_ref.at[my_s], own, lsem.at[0])
    take.start()

    def end_reduce(step, carry):
        peer = lax.rem(me + step, count)

        @pl.when(peer < chunks)
        def _():
            reduce_copy(me, peer).wait_send()

        @pl.when(me < chunks)
        def _():
            reduce_copy(peer, peer).wait_recv()
        return carry

    @pl.when(me < chunks)
    def _():
        keep = pltpu.make_async_copy(grad_ref.at[jnp.minimum(me, chunks - 1)], parts.at[me], lsem.at[2])
        keep.start()
        keep.wait()

    lax.fori_loop(1, count, end_reduce, 0)

    @pl.when(me < chunks)
    def _():
        mine[...] = lax.fori_loop(
            0, count, lambda n, acc: acc + parts[n], jnp.zeros_like(mine))

        def start_gather(step, carry):
            gather_copy(me, lax.rem(me + step, count)).start()
            return carry

        lax.fori_loop(1, count, start_gather, 0)
        total_ref[jnp.minimum(me, chunks - 1)] = mine[...]

    take.wait()
    put = pltpu.make_async_copy(own, got_block_ref.at[my_s], lsem.at[1])
    put.start()
    wait_faces(regions, owners, my_r, my_s, True, face_ref, got_face_ref, fsend, frecv)
    put.wait()

    def end_gather(step, carry):
        peer = lax.rem(me + step, count)

        @pl.when(me < chunks)
        def _():
            gather_copy(me, peer).wait_send()

        @pl.when(peer < chunks)
        def _():
            gather_copy(peer, peer).wait_recv()
        return carry

    lax.fori_loop(1, count, end_gather, 0)
    wait_blocks(owners, my_r, my_s, blocks_ref, got_block_ref, bsend, brecv)


def last_kernel(req_ref, slot_ref, gin_ref, fg_ref, ans_ref, arr_ref, order_ref, spread_ref,
                grad_ref, out_ref, fg_acc):
    fg_acc[...] = fg_ref[...]
    for s in range(24):
        want = req_ref[0, s]

        @pl.when(want >= 0)
        def _():
            fg_acc[want] += ans_ref[s].astype(F32)

    out_ref[...] = jnp.zeros_like(out_ref)

    def put_block(s, carry):
        spot = slot_ref[0, s]

        @pl.when(spot >= 0)
        def _():
            out_ref[spot] = arr_ref[s]
        return carry

    lax.fori_loop(0, 64, put_block, 0)
    lane = lax.broadcasted_iota(jnp.int32, (32, LANES), 1)
    k_low = (lane % 128) < 64

    def split(v):
        high = v.astype(BF)
        return high, (v - high.astype(F32)).astype(BF)

    def one(b, carry):
        base = b * 6
        f = [fg_acc[base + n] for n in range(6)]
        j_sum = jnp.concatenate([f[2], f[3]], axis=1)
        k_sum = jnp.concatenate(
            [f[4][:, 0:64], f[5][:, 0:64], f[4][:, 64:128], f[5][:, 64:128]], axis=1)
        zero = jnp.zeros_like(k_sum)
        parts = split(j_sum) + split(jnp.where(k_low, k_sum, zero)) + split(
            jnp.where(k_low, zero, k_sum))
        stack = jnp.concatenate(parts, axis=0)
        spread = jnp.concatenate(
            [dot(spread_ref[0], stack[:, 0:128]), dot(spread_ref[1], stack[:, 128:256])], axis=1)
        total = gin_ref[b] + spread
        low = jnp.concatenate([f[0][0:16], f[0][16:32]], axis=1)
        high = jnp.concatenate([f[1][0:16], f[1][16:32]], axis=1)
        total = jnp.concatenate(
            [total[0:16] + low, total[16:112], total[112:128] + high], axis=0)
        turned = total.T.astype(BF)
        wide = jnp.concatenate([turned[q * 64:q * 64 + 64] for q in range(4)], axis=1)
        grad_ref[b] = dot(wide, order_ref[...]).astype(BF)
        return carry

    lax.fori_loop(0, gin_ref.shape[0], one, 0)


def on_device(features, fine_weight, down_weight, coarse_weight, cotangent, face_source,
              face_requests, child_slot, parent_octant):
    regions = lax.axis_size("region")
    owners = lax.axis_size("space")
    count = regions * owners
    bricks, channels, volume = features.shape
    faces = bricks * 6
    parents, _, wide = cotangent.shape
    octant = volume // 8
    slots = parent_octant.shape[1]
    shape = jax.ShapeDtypeStruct
    big = pltpu.CompilerParams(vmem_limit_bytes=60 * 2**20)
    x, table, out_faces, out_cots = pl.pallas_call(
        first_kernel,
        out_shape=(shape((bricks, ROWS, LANES), BF), shape((faces, 32, 128), BF),
                   shape((24, 32, 128), BF), shape((slots, octant, wide), BF)),
        in_specs=[SMEM_SPEC] * 2 + [VMEM_SPEC] * 4,
        out_specs=(VMEM_SPEC,) * 4,
        compiler_params=big,
        name="first",
    )(face_requests, parent_octant, features, cotangent.reshape(parents * 8, octant, wide),
      jnp.asarray(ORDER), jnp.asarray(FACE))
    pair = slots // owners
    dma = pltpu.SemaphoreType.DMA
    in_faces, in_cots = pl.pallas_call(
        functools.partial(exchange_kernel, regions, owners),
        out_shape=(shape((6, 4, 32, 128), BF), shape((owners, pair, octant, wide), BF)),
        in_specs=[ANY_SPEC] * 2,
        out_specs=(ANY_SPEC,) * 2,
        scratch_shapes=[pltpu.VMEM((pair, octant, wide), BF), dma((6,)), dma((6,)),
                        dma((owners,)), dma((owners,)), dma((2,))],
        compiler_params=pltpu.CompilerParams(collective_id=0, has_side_effects=True),
        name="exchange",
    )(out_faces.reshape(6, 4, 32, 128), out_cots.reshape(owners, pair, octant, wide))
    scale_fine = 1.0 / math.sqrt(bricks * count * volume)
    scale_coarse = 1.0 / math.sqrt(parents * count * volume)
    gin, fg, back, co, grads = pl.pallas_call(
        functools.partial(compute_kernel, scale_fine, scale_coarse),
        out_shape=(shape((bricks, ROWS, LANES), F32), shape((faces, 32, 128), F32),
                   shape((24, 32, 128), BF), shape((slots, octant, wide), BF),
                   shape((896, 128), F32)),
        in_specs=[SMEM_SPEC] * 2 + [VMEM_SPEC] * 9,
        out_specs=(VMEM_SPEC,) * 5,
        scratch_shapes=[
            pltpu.VMEM((1280, LANES), BF), pltpu.VMEM((1280, LANES), BF),
            pltpu.VMEM((bricks * ROWS, 1280), BF), pltpu.VMEM((bricks * 64, 512), BF),
            pltpu.VMEM((bricks * ROWS, LANES), BF), pltpu.VMEM((bricks * 64, wide), BF),
            pltpu.VMEM((bricks * 64, wide), BF), pltpu.VMEM((bricks * 64, wide), BF)],
        compiler_params=big,
        name="compute",
    )(face_source, child_slot, x, table, in_faces.reshape(24, 32, 128),
      in_cots.reshape(slots, octant, wide), fine_weight,
      down_weight.reshape(8 * channels, wide), coarse_weight,
      jnp.asarray(SHIFT), jnp.asarray(BACK))
    chunk = max(CHUNK, 896 // count)
    chunks = 896 // chunk
    answers, arrived, totals = pl.pallas_call(
        functools.partial(answer_kernel, regions, owners),
        out_shape=(shape((6, 4, 32, 128), BF), shape((owners, pair, octant, wide), BF),
                   shape((chunks, chunk, 128), F32)),
        in_specs=[ANY_SPEC, ANY_SPEC, VMEM_SPEC],
        out_specs=(ANY_SPEC, ANY_SPEC, VMEM_SPEC),
        scratch_shapes=[pltpu.VMEM((pair, octant, wide), BF),
                        pltpu.VMEM((count, chunk, 128), F32), pltpu.VMEM((chunk, 128), F32),
                        dma((6,)), dma((6,)), dma((owners,)), dma((owners,)), dma((3,)),
                        dma((count,)), dma((count,)), dma((count,)), dma((count,))],
        compiler_params=pltpu.CompilerParams(collective_id=1, has_side_effects=True),
        name="answer",
    )(back.reshape(6, 4, 32, 128), co.reshape(owners, pair, octant, wide),
      grads.reshape(chunks, chunk, 128))
    grad_in, coarse_out = pl.pallas_call(
        last_kernel,
        out_shape=(shape((bricks, channels, volume), BF), shape((parents * 8, octant, wide), BF)),
        in_specs=[SMEM_SPEC] * 2 + [VMEM_SPEC] * 6,
        out_specs=(VMEM_SPEC,) * 2,
        scratch_shapes=[pltpu.VMEM((faces, 32, 128), F32)],
        compiler_params=big,
        name="last",
    )(face_requests, parent_octant, gin, fg, answers.reshape(24, 32, 128),
      arrived.reshape(slots, octant, wide), jnp.asarray(ORDER), jnp.asarray(SPREAD))
    totals = totals.reshape(896, 128)
    fine = totals[0:256].reshape(4, 64, 2, 64).transpose(0, 2, 1, 3).reshape(8, 64, 64)[0:7]
    return (grad_in, coarse_out.reshape(parents, volume, wide), fine,
            totals[256:768].reshape(8, channels, wide), totals[768:896])


def solution(mesh):
    both = ("region", "space")
    return jax.shard_map(
        on_device,
        mesh=mesh,
        in_specs=(P(both, None, None), P(), P(), P(), P(both, None, None), P(both, None),
                  P(both, None), P(both), P(both, None)),
        out_specs=(P(both, None, None), P(both, None, None), P(), P(), P()),
        check_vma=False,
    )
```

```python
import functools
import math

import jax
import jax.numpy as jnp
import numpy as np
from jax import lax
from jax.experimental import pallas as pl
from jax.experimental.pallas import tpu as pltpu
from jax.sharding import PartitionSpec as P

EDGE = 8
BF = jnp.bfloat16
F32 = jnp.float32
MESH = pl.DeviceIdType.MESH
NT = (((1,), (1,)), ((), ()))
TN = (((0,), (0,)), ((), ()))
VMEM_SPEC = pl.BlockSpec(memory_space=pltpu.VMEM)
SMEM_SPEC = pl.BlockSpec(memory_space=pltpu.SMEM)
ANY_SPEC = pl.BlockSpec(memory_space=pl.ANY)
ROWS = 128
LANES = 256
GROUP = 4


def row_of(i, j, k):
    return i * 16 + j * 4 + k


def make_tables():
    order = np.zeros((512, 512), np.float32)
    for i in range(8):
        for j in range(8):
            for k in range(8):
                q = (j % 2) * 2 + k % 2
                order[q * 128 + row_of(i, j // 2, k // 2), i * 64 + j * 8 + k] = 1
    face = np.zeros((128, 128), np.float32)
    for i in range(8):
        for m in range(4):
            face[i * 4 + m, row_of(i, 0, m)] = 1
            face[32 + i * 4 + m, row_of(i, 3, m)] = 1
            face[64 + i * 4 + m, row_of(i, m, 0)] = 1
            face[96 + i * 4 + m, row_of(i, m, 3)] = 1
    spread = np.zeros((2, 128, 192), np.float32)
    for half in range(2):
        j_face = face[0:32] if half == 0 else face[32:64]
        parts = [j_face, j_face, face[64:96], face[64:96], face[96:128], face[96:128]]
        spread[half] = np.concatenate(parts, axis=0).T
    cast = lambda a: np.asarray(a, dtype=BF)
    return cast(order), cast(face), cast(spread)


ORDER, FACE, SPREAD = make_tables()


def dot(a, b, dims=(((1,), (0,)), ((), ()))):
    return lax.dot_general(a, b, dims, preferred_element_type=F32)


def neighbours(regions, owners):
    far = owners // 4
    return [(1, 0), (-1, 0), (0, 1), (0, -1), (0, far), (0, -far)]


def face_moves(regions, owners, my_r, my_s, backward):
    sign = -1 if backward else 1
    for k, (dr, ds) in enumerate(neighbours(regions, owners)):
        to_r, to_s = my_r + sign * dr, my_s + sign * ds
        from_r, from_s = my_r - sign * dr, my_s - sign * ds
        can_send = (to_r >= 0) & (to_r < regions) & (to_s >= 0) & (to_s < owners)
        can_take = (from_r >= 0) & (from_r < regions) & (from_s >= 0) & (from_s < owners)
        yield k, (to_r, to_s), can_send, can_take


def send_faces(regions, owners, my_r, my_s, backward, src, dst, send_sem, recv_sem):
    for k, target, can_send, can_take in face_moves(regions, owners, my_r, my_s, backward):
        copy = pltpu.make_async_remote_copy(
            src_ref=src.at[k], dst_ref=dst.at[k], send_sem=send_sem.at[k],
            recv_sem=recv_sem.at[k], device_id=target, device_id_type=MESH)

        @pl.when(can_send)
        def _():
            copy.start()


def wait_faces(regions, owners, my_r, my_s, backward, src, dst, send_sem, recv_sem):
    for k, target, can_send, can_take in face_moves(regions, owners, my_r, my_s, backward):
        copy = pltpu.make_async_remote_copy(
            src_ref=src.at[k], dst_ref=dst.at[k], send_sem=send_sem.at[k],
            recv_sem=recv_sem.at[k], device_id=target, device_id_type=MESH)

        @pl.when(can_send)
        def _():
            copy.wait_send()

        @pl.when(can_take)
        def _():
            copy.wait_recv()


def block_copy(my_r, peer, pair, take, land, src, dst, send_sem, recv_sem):
    return pltpu.make_async_remote_copy(
        src_ref=src.at[pl.ds(take * pair, pair)], dst_ref=dst.at[pl.ds(land * pair, pair)],
        send_sem=send_sem.at[take], recv_sem=recv_sem.at[land], device_id=(my_r, peer),
        device_id_type=MESH)


def start_blocks(owners, my_r, my_s, pair, src, dst, send_sem, recv_sem):
    def start(step, carry):
        peer = lax.rem(my_s + step, owners)
        block_copy(my_r, peer, pair, peer, my_s, src, dst, send_sem, recv_sem).start()
        return carry

    lax.fori_loop(1, owners, start, 0)


def wait_blocks(owners, my_r, my_s, pair, src, dst, send_sem, recv_sem):
    def wait(step, carry):
        peer = lax.rem(my_s + step, owners)
        copy = block_copy(my_r, peer, pair, peer, peer, src, dst, send_sem, recv_sem)
        copy.wait_send()
        copy.wait_recv()
        return carry

    lax.fori_loop(1, owners, wait, 0)


def silu_parts(v):
    s = 1.0 / (1.0 + jnp.exp(-v))
    return v * s, s * (1.0 + v * (1.0 - s))


def place(w_ref, base, q_in, q_out, block):
    w_ref[base + q_in * 64:base + q_in * 64 + 64, q_out * 64:q_out * 64 + 64] = block


def fill_weights(fine_ref, w_ref, wt_ref):
    w_ref[...] = jnp.zeros_like(w_ref)
    wt_ref[...] = jnp.zeros_like(wt_ref)
    same = [(q, q) for q in range(4)]
    up_j = [(0, 2), (1, 3)]
    down_j = [(2, 0), (3, 1)]
    up_k = [(0, 1), (2, 3)]
    down_k = [(1, 0), (3, 2)]
    plan = [
        (0, 0, 0, same), (1, 1, 2, same), (2, 2, 1, same),
        (3, 0, 0, up_j), (3, 3, 3, down_j), (4, 0, 0, down_j), (4, 3, 3, up_j),
        (5, 0, 0, up_k), (5, 4, 4, down_k), (6, 0, 0, down_k), (6, 4, 4, up_k),
    ]
    for tap, fwd, bwd, pairs in plan:
        w = fine_ref[tap]
        wt = w.astype(F32).T.astype(BF)
        for q_in, q_out in pairs:
            place(w_ref, fwd * 256, q_in, q_out, w)
            place(wt_ref, bwd * 256, q_out, q_in, wt)
    return plan


def index_kernel(code_ref, slot_ref, child_ref, face_ref):
    for s in range(child_ref.shape[0]):
        child_ref[s] = 0
    for s in range(face_ref.shape[0]):
        face_ref[s] = 0
    for b in range(slot_ref.shape[0]):
        child_ref[slot_ref[b]] = b
    total = code_ref.shape[0]

    def mark(n, carry):
        code = code_ref[n]

        @pl.when(code >= total)
        def _():
            face_ref[code - total] = n
        return carry

    lax.fori_loop(0, total, mark, 0, unroll=8)


def signal_peers(regions, owners, my_r, my_s):
    barrier = pltpu.get_barrier_semaphore()
    core = lax.rem(my_s, 2)
    half = owners // 2

    def greet(step, carry):
        peer = lax.rem(my_s + step, owners)
        pl.semaphore_signal(barrier, inc=1, device_id=(my_r, peer), device_id_type=MESH)
        return carry

    lax.fori_loop(1, owners, greet, 0)

    def greet_far(step, carry):
        far_r = lax.rem(my_r + 1 + step // half, regions)
        far_s = 2 * lax.rem(step, half) + core
        pl.semaphore_signal(barrier, inc=1, device_id=(far_r, far_s), device_id_type=MESH)
        return carry

    lax.fori_loop(0, (regions - 1) * half, greet_far, 0)


def wait_peers(regions, owners):
    barrier = pltpu.get_barrier_semaphore()
    pl.semaphore_wait(barrier, owners - 1 + (regions - 1) * (owners // 2))


def row_roll(v, by):
    return pltpu.roll(v, by % v.shape[0], 0)


def pieces8(v, start, step, count):
    return jnp.concatenate([v[start + n * step:start + n * step + 8] for n in range(count)], axis=0)


def main_kernel(regions, owners, scale_fine, scale_coarse,
                code_ref, slot_ref, req_ref, po_ref, child_inv, face_inv,
                feat_hbm, cot_hbm, order_hbm, face_ref, fine_ref, down_ref, coarse_ref,
                gin_ref, plane_ref, ans_ref, blocks_out, total_ref,
                feat, cot, order, x_ref, table, out_face, in_face, cots, got_cots,
                w_ref, wt_ref, taps_ref, act_ref, gh_ref, red_ref, cg_ref, ch_ref,
                co_ref, co_slots, slope_ref, cslope_ref, back_face, halo_scr, g_scr,
                grads, pair_got, half_sum, parts, mine,
                load, fsend, frecv, bsend, brecv, hsend, hrecv, csend, crecv, osem,
                psend, precv, rsend, rrecv, gsend, grecv):
    my_r = lax.axis_index("region")
    my_s = lax.axis_index("space")
    bricks = feat.shape[0]
    face_total = table.shape[0]
    slots = cots.shape[0]
    pair = slots // owners
    loads = [pltpu.make_async_copy(src, dst, load.at[n]) for n, (src, dst) in enumerate(
        [(feat_hbm, feat), (order_hbm, order), (cot_hbm, cot)])]
    for copy in loads:
        copy.start()
    signal_peers(regions, owners, my_r, my_s)
    plan = fill_weights(fine_ref, w_ref, wt_ref)
    loads[0].wait()
    loads[1].wait()

    def turn(g, carry):
        block = feat[pl.ds(g * GROUP, GROUP)].reshape(GROUP * 64, 512)
        turned = dot(order[...], block, NT).astype(BF)
        for n in range(GROUP):
            b = g * GROUP + n
            x = jnp.concatenate(
                [turned[q * 128:(q + 1) * 128, n * 64:(n + 1) * 64] for q in range(4)], axis=1
            )
            x_ref[pl.ds(b * ROWS, ROWS), :] = x
            f = dot(face_ref[...], x).astype(BF)
            base = b * 6
            table[base] = jnp.concatenate([x[0:16, 0:128], x[0:16, 128:256]], axis=0)
            table[base + 1] = jnp.concatenate([x[112:128, 0:128], x[112:128, 128:256]], axis=0)
            table[base + 2] = f[0:32, 0:128]
            table[base + 3] = f[32:64, 128:256]
            table[base + 4] = jnp.concatenate([f[64:96, 0:64], f[64:96, 128:192]], axis=1)
            table[base + 5] = jnp.concatenate([f[96:128, 64:128], f[96:128, 192:256]], axis=1)
        return carry

    lax.fori_loop(0, bricks // GROUP, turn, 0)
    for s in range(24):
        out_face[s // 4, s % 4] = table[jnp.maximum(req_ref[s], 0)]
    loads[2].wait()

    def gather_cot(s, carry):
        cots[s] = cot[jnp.maximum(po_ref[s], 0)]
        return carry

    lax.fori_loop(0, slots, gather_cot, 0, unroll=8)
    wait_peers(regions, owners)
    send_faces(regions, owners, my_r, my_s, False, out_face, in_face, fsend, frecv)
    start_blocks(owners, my_r, my_s, pair, cots, got_cots, bsend, brecv)
    for u in range(pair):
        got_cots[my_s * pair + u] = cots[my_s * pair + u]
    wait_faces(regions, owners, my_r, my_s, False, out_face, in_face, fsend, frecv)

    row8 = lax.broadcasted_iota(jnp.int32, (ROWS, 128), 0)
    first_j = lax.rem(row8, 16) < 4
    last_j = lax.rem(row8, 16) >= 12
    row_w = lax.broadcasted_iota(jnp.int32, (ROWS, LANES), 0)
    lane_w = lax.broadcasted_iota(jnp.int32, (ROWS, LANES), 1)
    k_low = lax.rem(lane_w, 128) < 64
    edge_k = lax.rem(row_w, 4) == jnp.where(k_low, 3, 0)
    low4 = lax.rem(lax.broadcasted_iota(jnp.int32, (32, 128), 0), 8) < 4

    def halo(b, d):
        code = code_ref[b * 6 + d]
        own = table[jnp.clip(code, 0, face_total - 1)]
        slot = jnp.clip(code - face_total, 0, 23)
        got = in_face[slot // 4, lax.rem(slot, 4)]
        picked = jnp.where(code >= face_total, got, own)
        return jnp.where(code >= 0, picked, jnp.zeros_like(picked))

    def shift_j(low, high):
        return row_roll(low, -4), row_roll(high, 4)

    def shift_k(v):
        return jnp.where(k_low, row_roll(v, -1), row_roll(v, 1))

    def forward_taps(b):
        row = pl.multiple_of(b * ROWS, ROWS)
        x = x_ref[pl.ds(row, ROWS), :]
        h = [halo(b, d) for d in range(6)]
        x32 = x.astype(F32)
        up, down = h[3].astype(F32), h[2].astype(F32)
        up_r, down_r = row_roll(up, 4), row_roll(down, -4)
        h_up, h_down = [], []
        for i in range(8):
            n = (i // 2) * 8
            a = (up_r if i % 2 == 0 else up)[n:n + 8]
            c = (down if i % 2 == 0 else down_r)[n:n + 8]
            h_up += [a, a]
            h_down += [c, c]
        low, high = shift_j(x32[:, 0:128], x32[:, 128:256])
        tj = jnp.concatenate([
            jnp.where(last_j, jnp.concatenate(h_up, axis=0), low),
            jnp.where(first_j, jnp.concatenate(h_down, axis=0), high)], axis=1)
        k5, k4 = h[5].astype(F32), h[4].astype(F32)
        k5r, k4r = pltpu.roll(k5, 64, 1), pltpu.roll(k4, 64, 1)
        halo_scr[0, pl.ds(3, 32, stride=4), :] = k5
        halo_scr[1, pl.ds(3, 32, stride=4), :] = k5r
        halo_scr[0, pl.ds(0, 32, stride=4), :] = k4r
        halo_scr[1, pl.ds(0, 32, stride=4), :] = k4
        hk = jnp.concatenate([halo_scr[0], halo_scr[1]], axis=1)
        tk = jnp.where(edge_k, hk, shift_k(x32))
        hi_m = jnp.concatenate([h[0][0:16], h[0][16:32]], axis=1)
        hi_p = jnp.concatenate([h[1][0:16], h[1][16:32]], axis=1)
        taps_ref[pl.ds(row, ROWS), :] = jnp.concatenate([
            x,
            jnp.concatenate([hi_m, x[0:112]], axis=0),
            jnp.concatenate([x[16:128], hi_p], axis=0),
            tj.astype(BF), tk.astype(BF)], axis=1)

    def forward(g, carry):
        for n in range(GROUP):
            forward_taps(g * GROUP + n)
        row = pl.multiple_of(g * GROUP * ROWS, GROUP * ROWS)
        half = pl.multiple_of(g * GROUP * 64, GROUP * 64)
        hidden = dot(taps_ref[pl.ds(row, GROUP * ROWS), :], w_ref[...])
        act, slope = silu_parts(hidden)
        slope_ref[pl.ds(row, GROUP * ROWS), :] = slope
        act = act.astype(BF)
        count = GROUP * 4
        even = jnp.concatenate([act[32 * n:32 * n + 16] for n in range(count)], axis=0)
        odd = jnp.concatenate([act[32 * n + 16:32 * n + 32] for n in range(count)], axis=0)
        both = jnp.concatenate([even, odd], axis=1)
        act_ref[pl.ds(half, GROUP * 64), :] = both
        reduced = dot(both, down_ref[...]).astype(BF)
        red_ref[pl.ds(half, GROUP * 64), :] = reduced
        c_out, c_slope = silu_parts(dot(reduced, coarse_ref[...]))
        co_ref[pl.ds(g * GROUP, GROUP)] = c_out.astype(BF).reshape(GROUP, 64, 128)
        cslope_ref[pl.ds(half, GROUP * 64), :] = c_slope
        return carry

    lax.fori_loop(0, bricks // GROUP, forward, 0)

    def gather_out(s, carry):
        co_slots[s] = co_ref[child_inv[s]]
        return carry

    lax.fori_loop(0, slots, gather_out, 0, unroll=8)
    wait_blocks(owners, my_r, my_s, pair, cots, got_cots, bsend, brecv)
    start_blocks(owners, my_r, my_s, pair, co_slots, blocks_out, csend, crecv)
    keep = pltpu.make_async_copy(co_slots.at[pl.ds(my_s * pair, pair)],
                                 blocks_out.at[pl.ds(my_s * pair, pair)], osem)
    keep.start()

    def backward(g, carry):
        row = pl.multiple_of(g * GROUP * ROWS, GROUP * ROWS)
        half = pl.multiple_of(g * GROUP * 64, GROUP * 64)
        cot_rows = jnp.concatenate(
            [got_cots[slot_ref[g * GROUP + n]] for n in range(GROUP)], axis=0).astype(F32)
        c_grad = (cot_rows * cslope_ref[pl.ds(half, GROUP * 64), :]).astype(BF)
        cg_ref[pl.ds(half, GROUP * 64), :] = c_grad
        child = dot(c_grad, coarse_ref[...], NT).astype(BF)
        ch_ref[pl.ds(half, GROUP * 64), :] = child
        ga = dot(child, down_ref[...], NT)
        rows = []
        for n in range(GROUP * 4):
            rows += [ga[16 * n:16 * n + 16, 0:256], ga[16 * n:16 * n + 16, 256:512]]
        all_gh = (jnp.concatenate(rows, axis=0) * slope_ref[pl.ds(row, GROUP * ROWS), :]).astype(BF)
        gh_ref[pl.ds(row, GROUP * ROWS), :] = all_gh
        bwd, f0, f1, fj, fk = [], [], [], [], []
        for n in range(GROUP):
            gh = all_gh[n * ROWS:(n + 1) * ROWS]
            g32 = gh.astype(F32)
            low, high = shift_j(g32[:, 0:128], g32[:, 128:256])
            zero = jnp.zeros_like(low)
            gj = jnp.concatenate(
                [jnp.where(last_j, zero, low), jnp.where(first_j, zero, high)], axis=1)
            gk = jnp.where(edge_k, jnp.zeros_like(g32), shift_k(g32))
            blank = jnp.zeros((16, LANES), BF)
            bwd.append(jnp.concatenate([
                gh,
                jnp.concatenate([blank, gh[0:112]], axis=0),
                jnp.concatenate([gh[16:128], blank], axis=0),
                gj.astype(BF), gk.astype(BF)], axis=1))
            f0.append(gh[0:16])
            f1.append(gh[112:128])
            j0 = jnp.where(low4, pieces8(g32[:, 0:128], 0, 32, 4),
                           row_roll(pieces8(g32[:, 0:128], 16, 32, 4), 4))
            j3 = jnp.where(low4, row_roll(pieces8(g32[:, 128:256], 8, 32, 4), -4),
                           pieces8(g32[:, 128:256], 24, 32, 4))
            fj.append(jnp.concatenate([j0, j3], axis=1).astype(BF))
            g_scr[0] = g32[:, 0:128]
            g_scr[1] = g32[:, 128:256]
            sides = []
            for side in range(2):
                sides.append(jnp.where(
                    k_low[0:32, 0:128], g_scr[side, pl.ds(0, 32, stride=4), :],
                    g_scr[side, pl.ds(3, 32, stride=4), :]))
            fk.append(jnp.concatenate(sides, axis=1).astype(BF))
        gin_ref[pl.ds(row, GROUP * ROWS), :] = dot(jnp.concatenate(bwd, axis=0), wt_ref[...])
        p0 = dot(jnp.concatenate(f0, axis=0), wt_ref[512:768, :]).astype(BF)
        p1 = dot(jnp.concatenate(f1, axis=0), wt_ref[256:512, :]).astype(BF)
        pj = dot(jnp.concatenate(fj, axis=0), wt_ref[768:1024, :]).astype(BF)
        pk = dot(jnp.concatenate(fk, axis=0), wt_ref[1024:1280, :]).astype(BF)
        for n in range(GROUP):
            base = (g * GROUP + n) * 6
            a, c = p0[n * 16:n * 16 + 16], p1[n * 16:n * 16 + 16]
            j, k = pj[n * 32:n * 32 + 32], pk[n * 32:n * 32 + 32]
            plane_ref[base] = jnp.concatenate([a[:, 0:128], a[:, 128:256]], axis=0)
            plane_ref[base + 1] = jnp.concatenate([c[:, 0:128], c[:, 128:256]], axis=0)
            plane_ref[base + 2] = j[:, 128:256]
            plane_ref[base + 3] = j[:, 0:128]
            plane_ref[base + 4] = jnp.concatenate([k[:, 64:128], k[:, 192:256]], axis=1)
            plane_ref[base + 5] = jnp.concatenate([k[:, 0:64], k[:, 128:192]], axis=1)
        return carry

    lax.fori_loop(0, bricks // GROUP, backward, 0)
    for s in range(24):
        back_face[s // 4, s % 4] = plane_ref[face_inv[s]]
    fine = dot(taps_ref[...], gh_ref[...], TN) * scale_fine
    send_faces(regions, owners, my_r, my_s, True, back_face, ans_ref, hsend, hrecv)
    sums = [None] * 7
    for tap, fwd, bwd, pairs in plan:
        for q_in, q_out in pairs:
            part = fine[fwd * 256 + q_in * 64:fwd * 256 + q_in * 64 + 64,
                        q_out * 64:q_out * 64 + 64]
            sums[tap] = part if sums[tap] is None else sums[tap] + part
    sums.append(jnp.zeros_like(sums[0]))

    def put_rows(start, value):
        count = value.shape[0] // 8
        grads[start // 8:start // 8 + count] = value.reshape(count, 8, 128)

    for n in range(4):
        put_rows(n * 64, jnp.concatenate([sums[2 * n], sums[2 * n + 1]], axis=1))
    put_rows(256, dot(act_ref[...], ch_ref[...], TN) * scale_fine)
    put_rows(768, dot(red_ref[...], cg_ref[...], TN) * scale_coarse)
    reduce_all(regions, owners, my_r, my_s, grads, pair_got, half_sum, parts, mine, total_ref,
               psend, precv, rsend, rrecv, gsend, grecv)
    wait_faces(regions, owners, my_r, my_s, True, back_face, ans_ref, hsend, hrecv)
    keep.wait()
    wait_blocks(owners, my_r, my_s, pair, co_slots, blocks_out, csend, crecv)


def reduce_all(regions, owners, my_r, my_s, grads, pair_got, half_sum, parts, mine, total_ref,
               psend, precv, rsend, rrecv, gsend, grecv):
    core = lax.rem(my_s, 2)
    other = 1 - core
    half = pair_got.shape[0]
    chips = parts.shape[0]
    width = owners // 2
    chip = my_r * width + my_s // 2
    rows = half_sum.shape[1]
    used = half_sum.shape[0]
    partner = (my_r, my_s + 1 - 2 * core)
    swap = pltpu.make_async_remote_copy(
        src_ref=grads.at[pl.ds(other * half, half)], dst_ref=pair_got, send_sem=psend.at[0],
        recv_sem=precv.at[0], device_id=partner, device_id_type=MESH)
    swap.start()
    swap.wait()
    half_sum[...] = (grads[pl.ds(core * half, half)] + pair_got[...]).reshape(half_sum.shape)

    def spot(peer):
        return (peer // width, 2 * lax.rem(peer, width) + core)

    def reduce_copy(slot, peer):
        return pltpu.make_async_remote_copy(
            src_ref=half_sum.at[jnp.minimum(peer, used - 1)], dst_ref=parts.at[slot],
            send_sem=rsend.at[peer], recv_sem=rrecv.at[slot], device_id=spot(peer),
            device_id_type=MESH)

    def gather_copy(chunk, peer):
        return pltpu.make_async_remote_copy(
            src_ref=mine, dst_ref=total_ref.at[core * used + jnp.minimum(chunk, used - 1)],
            send_sem=gsend.at[peer], recv_sem=grecv.at[chunk], device_id=spot(peer),
            device_id_type=MESH)

    def loop(body):
        def step(n, carry):
            body(lax.rem(chip + n, chips))
            return carry
        lax.fori_loop(1, chips, step, 0)

    def start_reduce(peer):
        @pl.when(peer < used)
        def _():
            reduce_copy(chip, peer).start()

    def end_reduce(peer):
        @pl.when(peer < used)
        def _():
            reduce_copy(chip, peer).wait_send()

        @pl.when(chip < used)
        def _():
            reduce_copy(peer, peer).wait_recv()

    def end_gather(peer):
        @pl.when(chip < used)
        def _():
            gather_copy(chip, peer).wait_send()

        @pl.when(peer < used)
        def _():
            gather_copy(peer, peer).wait_recv()

    loop(start_reduce)

    @pl.when(chip < used)
    def _():
        parts[chip] = half_sum[jnp.minimum(chip, used - 1)]

    loop(end_reduce)

    @pl.when(chip < used)
    def _():
        total = parts[0]
        for n in range(1, chips):
            total = total + parts[n]
        mine[...] = total
        total_ref[core * used + jnp.minimum(chip, used - 1)] = total
        loop(lambda peer: gather_copy(chip, peer).start())

    loop(end_gather)
    share = pltpu.make_async_remote_copy(
        src_ref=total_ref.at[pl.ds(core * used, used)],
        dst_ref=total_ref.at[pl.ds(core * used, used)],
        send_sem=psend.at[1], recv_sem=precv.at[1], device_id=partner, device_id_type=MESH)
    share.start()
    share.wait_send()
    pltpu.make_async_remote_copy(
        src_ref=total_ref.at[pl.ds(other * used, used)],
        dst_ref=total_ref.at[pl.ds(other * used, used)],
        send_sem=psend.at[1], recv_sem=precv.at[1], device_id=partner,
        device_id_type=MESH).wait_recv()


def last_kernel(code_ref, req_ref, slot_ref, gin_ref, plane_ref, ans_ref, arr_ref, order_ref,
                spread_ref, grad_ref, out_ref, fg_acc):
    fg_acc[...] = jnp.zeros_like(fg_acc)
    face_total = plane_ref.shape[0]

    def add_plane(n, carry):
        code = code_ref[n]

        @pl.when((code >= 0) & (code < face_total))
        def _():
            fg_acc[code] += plane_ref[n].astype(F32)
        return carry

    lax.fori_loop(0, face_total, add_plane, 0, unroll=4)
    for s in range(24):
        want = req_ref[s]

        @pl.when(want >= 0)
        def _():
            fg_acc[want] += ans_ref[s].astype(F32)

    out_ref[...] = jnp.zeros_like(out_ref)

    def put_block(s, carry):
        spot = slot_ref[s]

        @pl.when(spot >= 0)
        def _():
            out_ref[spot] = arr_ref[s]
        return carry

    lax.fori_loop(0, 64, put_block, 0)
    lane = lax.broadcasted_iota(jnp.int32, (32, LANES), 1)
    k_low = (lane % 128) < 64

    def split(v):
        high = v.astype(BF)
        return high, (v - high.astype(F32)).astype(BF)

    def one(b, carry):
        base = b * 6
        f = [fg_acc[base + n] for n in range(6)]
        j_sum = jnp.concatenate([f[2], f[3]], axis=1)
        k_sum = jnp.concatenate(
            [f[4][:, 0:64], f[5][:, 0:64], f[4][:, 64:128], f[5][:, 64:128]], axis=1)
        zero = jnp.zeros_like(k_sum)
        parts = split(j_sum) + split(jnp.where(k_low, k_sum, zero)) + split(
            jnp.where(k_low, zero, k_sum))
        stack = jnp.concatenate(parts, axis=0)
        spread = jnp.concatenate(
            [dot(spread_ref[0], stack[:, 0:128]), dot(spread_ref[1], stack[:, 128:256])], axis=1)
        total = gin_ref[pl.ds(b * ROWS, ROWS), :] + spread
        low = jnp.concatenate([f[0][0:16], f[0][16:32]], axis=1)
        high = jnp.concatenate([f[1][0:16], f[1][16:32]], axis=1)
        total = jnp.concatenate(
            [total[0:16] + low, total[16:112], total[112:128] + high], axis=0)
        turned = total.T.astype(BF)
        wide = jnp.concatenate([turned[q * 64:q * 64 + 64] for q in range(4)], axis=1)
        grad_ref[b] = dot(wide, order_ref[...]).astype(BF)
        return carry

    lax.fori_loop(0, grad_ref.shape[0], one, 0)


def on_device(features, fine_weight, down_weight, coarse_weight, cotangent, face_source,
              face_requests, child_slot, parent_octant):
    regions = lax.axis_size("region")
    owners = lax.axis_size("space")
    count = regions * owners
    bricks, channels, volume = features.shape
    faces = bricks * 6
    parents, _, wide = cotangent.shape
    octant = volume // 8
    slots = parent_octant.shape[1]
    shape = jax.ShapeDtypeStruct
    vm = pltpu.VMEM
    dma = pltpu.SemaphoreType.DMA
    codes = face_source.reshape(faces)
    requests = face_requests.reshape(24)
    targets = parent_octant.reshape(slots)
    child_inv, face_inv = pl.pallas_call(
        index_kernel,
        out_shape=(shape((slots,), jnp.int32), shape((24,), jnp.int32)),
        in_specs=[SMEM_SPEC] * 2,
        out_specs=(SMEM_SPEC,) * 2,
        name="index",
    )(codes, child_slot)
    scale_fine = 1.0 / math.sqrt(bricks * count * volume)
    scale_coarse = 1.0 / math.sqrt(parents * count * volume)
    chips = count // 2
    chunk = max(8, 448 // chips)
    used = 448 // chunk
    big = bricks * ROWS
    small = bricks * octant
    gin, planes, answers, arrived, totals = pl.pallas_call(
        functools.partial(main_kernel, regions, owners, scale_fine, scale_coarse),
        out_shape=(shape((big, LANES), F32), shape((faces, 32, 128), BF),
                   shape((6, 4, 32, 128), BF), shape((slots, octant, wide), BF),
                   shape((2 * used, chunk, 128), F32)),
        in_specs=[SMEM_SPEC] * 6 + [ANY_SPEC] * 3 + [VMEM_SPEC] * 4,
        out_specs=(VMEM_SPEC,) * 3 + (ANY_SPEC, VMEM_SPEC),
        scratch_shapes=[
            vm((bricks, channels, volume), BF), vm((slots, octant, wide), BF), vm((512, 512), BF),
            vm((big, LANES), BF), vm((faces, 32, 128), BF), vm((6, 4, 32, 128), BF),
            vm((6, 4, 32, 128), BF), vm((slots, octant, wide), BF), vm((slots, octant, wide), BF),
            vm((1280, LANES), BF), vm((1280, LANES), BF), vm((big, 1280), BF),
            vm((small, 512), BF), vm((big, LANES), BF), vm((small, wide), BF),
            vm((small, wide), BF), vm((small, wide), BF),
            vm((bricks, octant, wide), BF), vm((slots, octant, wide), BF), vm((big, LANES), F32),
            vm((small, wide), F32), vm((6, 4, 32, 128), BF), vm((2, ROWS, 128), F32),
            vm((2, ROWS, 128), F32), vm((112, 8, 128), F32), vm((56, 8, 128), F32),
            vm((used, chunk, 128), F32), vm((chips, chunk, 128), F32), vm((chunk, 128), F32),
            dma((3,)), dma((6,)), dma((6,)), dma((owners,)), dma((owners,)), dma((6,)), dma((6,)),
            dma((owners,)), dma((owners,)), dma, dma((2,)), dma((2,)), dma((chips,)),
            dma((chips,)), dma((chips,)), dma((chips,))],
        compiler_params=pltpu.CompilerParams(
            collective_id=0, has_side_effects=True, vmem_limit_bytes=60 * 2**20),
        name="main",
    )(codes, child_slot, requests, targets, child_inv, face_inv, features,
      cotangent.reshape(parents * 8, octant, wide), jnp.asarray(ORDER), jnp.asarray(FACE),
      fine_weight, down_weight.reshape(8 * channels, wide), coarse_weight)
    grad_in, coarse_out = pl.pallas_call(
        last_kernel,
        out_shape=(shape((bricks, channels, volume), BF), shape((parents * 8, octant, wide), BF)),
        in_specs=[SMEM_SPEC] * 3 + [VMEM_SPEC] * 6,
        out_specs=(VMEM_SPEC,) * 2,
        scratch_shapes=[vm((faces, 32, 128), F32)],
        compiler_params=pltpu.CompilerParams(vmem_limit_bytes=60 * 2**20),
        name="last",
    )(codes, requests, targets, gin, planes, answers.reshape(24, 32, 128), arrived,
      jnp.asarray(ORDER), jnp.asarray(SPREAD))
    totals = totals.reshape(896, 128)
    fine = totals[0:256].reshape(4, 64, 2, 64).transpose(0, 2, 1, 3).reshape(8, 64, 64)[0:7]
    return (grad_in, coarse_out.reshape(parents, volume, wide), fine,
            totals[256:768].reshape(8, channels, wide), totals[768:896])


def solution(mesh):
    both = ("region", "space")
    return jax.shard_map(
        on_device,
        mesh=mesh,
        in_specs=(P(both, None, None), P(), P(), P(), P(both, None, None), P(both, None),
                  P(both, None), P(both), P(both, None)),
        out_specs=(P(both, None, None), P(both, None, None), P(), P(), P()),
        check_vma=False,
    )
```

```python
import functools
import math

import jax
import jax.numpy as jnp
import numpy as np
from jax import lax
from jax.experimental import pallas as pl
from jax.experimental.pallas import tpu as pltpu
from jax.sharding import PartitionSpec as P

EDGE = 8
BF = jnp.bfloat16
F32 = jnp.float32
MESH = pl.DeviceIdType.MESH
NT = (((1,), (1,)), ((), ()))
TN = (((0,), (0,)), ((), ()))
VMEM_SPEC = pl.BlockSpec(memory_space=pltpu.VMEM)
SMEM_SPEC = pl.BlockSpec(memory_space=pltpu.SMEM)
ANY_SPEC = pl.BlockSpec(memory_space=pl.ANY)
ROWS = 128
LANES = 256
GROUP = 4


def row_of(i, j, k):
    return i * 16 + j * 4 + k


def make_tables():
    order = np.zeros((512, 512), np.float32)
    for i in range(8):
        for j in range(8):
            for k in range(8):
                q = (j % 2) * 2 + k % 2
                order[q * 128 + row_of(i, j // 2, k // 2), i * 64 + j * 8 + k] = 1
    face = np.zeros((128, 128), np.float32)
    for i in range(8):
        for m in range(4):
            face[i * 4 + m, row_of(i, 0, m)] = 1
            face[32 + i * 4 + m, row_of(i, 3, m)] = 1
            face[64 + i * 4 + m, row_of(i, m, 0)] = 1
            face[96 + i * 4 + m, row_of(i, m, 3)] = 1
    cast = lambda a: np.asarray(a, dtype=BF)
    return cast(order), cast(order.T), cast(face)


ORDER, ORDER_T, FACE = make_tables()


def dot(a, b, dims=(((1,), (0,)), ((), ()))):
    return lax.dot_general(a, b, dims, preferred_element_type=F32)


def neighbours(regions, owners):
    far = owners // 4
    return [(1, 0), (-1, 0), (0, 1), (0, -1), (0, far), (0, -far)]


def face_moves(regions, owners, my_r, my_s, backward):
    sign = -1 if backward else 1
    for k, (dr, ds) in enumerate(neighbours(regions, owners)):
        to_r, to_s = my_r + sign * dr, my_s + sign * ds
        from_r, from_s = my_r - sign * dr, my_s - sign * ds
        can_send = (to_r >= 0) & (to_r < regions) & (to_s >= 0) & (to_s < owners)
        can_take = (from_r >= 0) & (from_r < regions) & (from_s >= 0) & (from_s < owners)
        yield k, (to_r, to_s), can_send, can_take


def send_faces(regions, owners, my_r, my_s, backward, src, dst, send_sem, recv_sem):
    for k, target, can_send, can_take in face_moves(regions, owners, my_r, my_s, backward):
        copy = pltpu.make_async_remote_copy(
            src_ref=src.at[k], dst_ref=dst.at[k], send_sem=send_sem.at[k],
            recv_sem=recv_sem.at[k], device_id=target, device_id_type=MESH)

        @pl.when(can_send)
        def _():
            copy.start()


def wait_faces(regions, owners, my_r, my_s, backward, src, dst, send_sem, recv_sem):
    for k, target, can_send, can_take in face_moves(regions, owners, my_r, my_s, backward):
        copy = pltpu.make_async_remote_copy(
            src_ref=src.at[k], dst_ref=dst.at[k], send_sem=send_sem.at[k],
            recv_sem=recv_sem.at[k], device_id=target, device_id_type=MESH)

        @pl.when(can_send)
        def _():
            copy.wait_send()

        @pl.when(can_take)
        def _():
            copy.wait_recv()


def block_copy(my_r, peer, pair, take, land, src, dst, send_sem, recv_sem):
    return pltpu.make_async_remote_copy(
        src_ref=src.at[pl.ds(take * pair, pair)], dst_ref=dst.at[pl.ds(land * pair, pair)],
        send_sem=send_sem, recv_sem=recv_sem, device_id=(my_r, peer),
        device_id_type=MESH)


def start_blocks(owners, my_r, my_s, pair, src, dst, send_sem, recv_sem):
    def start(step, carry):
        peer = lax.rem(my_s + step, owners)
        block_copy(my_r, peer, pair, peer, my_s, src, dst, send_sem, recv_sem).start()
        return carry

    lax.fori_loop(1, owners, start, 0)


def wait_blocks(owners, my_r, my_s, pair, src, dst, send_sem, recv_sem):
    count = (owners - 1) * pair
    copy = pltpu.make_async_remote_copy(
        src_ref=src.at[pl.ds(0, count)], dst_ref=dst.at[pl.ds(0, count)], send_sem=send_sem,
        recv_sem=recv_sem, device_id=(my_r, lax.rem(my_s + 1, owners)), device_id_type=MESH)
    copy.wait_send()
    copy.wait_recv()


def silu_parts(v):
    s = 1.0 / (1.0 + jnp.exp(-v))
    return v * s, s * (1.0 + v * (1.0 - s))


def place(w_ref, base, q_in, q_out, block):
    w_ref[base + q_in * 64:base + q_in * 64 + 64, q_out * 64:q_out * 64 + 64] = block


SWAP = (0, 2, 1, 3)


def fill_weights(fine_ref, w_ref, wt_ref):
    w_ref[...] = jnp.zeros_like(w_ref)
    wt_ref[...] = jnp.zeros_like(wt_ref)
    same = [(q, q) for q in range(4)]
    up_j = [(0, 2), (1, 3)]
    down_j = [(2, 0), (3, 1)]
    up_k = [(0, 1), (2, 3)]
    down_k = [(1, 0), (3, 2)]
    plan = [
        (0, 0, 0, same), (1, 1, 2, same), (2, 2, 1, same),
        (3, 0, 0, up_j), (3, 3, 3, down_j), (4, 0, 0, down_j), (4, 3, 3, up_j),
        (5, 0, 0, up_k), (5, 4, 4, down_k), (6, 0, 0, down_k), (6, 4, 4, up_k),
    ]
    for tap, fwd, bwd, pairs in plan:
        w = fine_ref[tap]
        wt = w.astype(F32).T.astype(BF)
        for q_in, q_out in pairs:
            place(w_ref, fwd * 256, SWAP[q_in] if fwd == 4 else q_in, q_out, w)
            place(wt_ref, bwd * 256, SWAP[q_out] if bwd == 4 else q_out, q_in, wt)
    return plan


def index_kernel(code_ref, slot_ref, req_ref, child_ref, face_ref, prev_ref, last_ref):
    total = code_ref.shape[0]
    none = prev_ref.shape[0]
    for s in range(child_ref.shape[0]):
        child_ref[s] = 0
    for s in range(face_ref.shape[0]):
        face_ref[s] = 0
    for f in range(total):
        last_ref[f] = none
    for b in range(slot_ref.shape[0]):
        child_ref[slot_ref[b]] = b

    def mark(n, carry):
        code = code_ref[n]

        @pl.when(code >= total)
        def _():
            face_ref[code - total] = n

        @pl.when((code >= 0) & (code < total))
        def _():
            prev_ref[n] = last_ref[code]
            last_ref[code] = n

        @pl.when((code < 0) | (code >= total))
        def _():
            prev_ref[n] = none
        return carry

    lax.fori_loop(0, total, mark, 0)

    def answer(s, carry):
        want = req_ref[s]

        @pl.when(want >= 0)
        def _():
            prev_ref[total + s] = last_ref[want]
            last_ref[want] = total + s

        @pl.when(want < 0)
        def _():
            prev_ref[total + s] = none
        return carry

    lax.fori_loop(0, req_ref.shape[0], answer, 0)


def signal_peers(regions, owners, my_r, my_s):
    barrier = pltpu.get_barrier_semaphore()

    def greet(step, carry):
        peer = lax.rem(my_s + step, owners)
        pl.semaphore_signal(barrier, inc=1, device_id=(my_r, peer), device_id_type=MESH)
        return carry

    lax.fori_loop(1, owners, greet, 0)

    for step in range(1, regions):
        far_r = lax.rem(my_r + step, regions)
        pl.semaphore_signal(barrier, inc=1, device_id=(far_r, my_s), device_id_type=MESH)


def wait_peers(regions, owners):
    barrier = pltpu.get_barrier_semaphore()
    pl.semaphore_wait(barrier, owners - 1 + regions - 1)


def row_roll(v, by):
    return pltpu.roll(v, by % v.shape[0], 0)


def pieces8(v, start, step, count):
    return jnp.concatenate([v[start + n * step:start + n * step + 8] for n in range(count)], axis=0)


def main_kernel(regions, owners, scale_fine, scale_coarse,
                code_ref, slot_ref, req_ref, po_ref, child_inv, face_inv, prev_ref, last_ref,
                feat_hbm, cot_hbm, order_t_hbm, order_hbm, face_ref, fine_ref, down_ref,
                coarse_ref,
                grad_ref, blocks_out, total_ref,
                feat, cot, order_t, order, x_ref, xk_ref, table, out_face, in_face, cots,
                got_cots, w_ref, wt_ref, taps_ref, act_ref, gh_ref, red_ref, cg_ref, ch_ref,
                co_ref, co_slots, slope_ref, cslope_ref, gin_ref, plane_ref, back_face, ans_ref,
                chain, halo_scr, g_scr,
                grads, pair_got, half_sum, part_x, x_sum, part_p, mine,
                load, fsend, frecv, hsend, hrecv, osem, bsem, csem, rsem):
    my_r = lax.axis_index("region")
    my_s = lax.axis_index("space")
    bricks = feat.shape[0]
    face_total = table.shape[0]
    slots = cots.shape[0]
    pair = slots // owners
    groups = bricks // GROUP
    wide_rows = GROUP * ROWS
    half_rows = GROUP * 64
    loads = [pltpu.make_async_copy(src, dst, load.at[n]) for n, (src, dst) in enumerate(
        [(feat_hbm, feat), (order_t_hbm, order_t), (cot_hbm, cot), (order_hbm, order)])]
    for copy in loads:
        copy.start()
    signal_peers(regions, owners, my_r, my_s)
    loads[2].wait()

    def gather_cot(s, carry):
        cots[s] = cot[jnp.maximum(po_ref[s], 0)]
        return carry

    lax.fori_loop(0, slots, gather_cot, 0, unroll=8)
    loads[0].wait()
    loads[1].wait()

    def turn(g, carry):
        block = feat[pl.ds(g * GROUP, GROUP)].reshape(half_rows, 512)
        moved = dot(block, order_t[...]).astype(BF)
        for n in range(GROUP):
            b = g * GROUP + n
            row = pl.multiple_of(b * ROWS, ROWS)
            part = moved[n * 64:(n + 1) * 64]
            q = [part[:, m * 128:(m + 1) * 128] for m in range(4)]
            x = jnp.concatenate(q, axis=0).T
            x_ref[pl.ds(row, ROWS), :] = x
            xk = jnp.concatenate([q[m] for m in SWAP], axis=0).T
            xk_ref[pl.ds(row, ROWS), :] = xk
            fj = dot(face_ref[0:64], x).astype(BF)
            fk = dot(face_ref[64:128], xk).astype(BF)
            base = b * 6
            table[base] = jnp.concatenate([x[0:16, 0:128], x[0:16, 128:256]], axis=0)
            table[base + 1] = jnp.concatenate([x[112:128, 0:128], x[112:128, 128:256]], axis=0)
            table[base + 2] = fj[0:32, 0:128]
            table[base + 3] = fj[32:64, 128:256]
            table[base + 4] = fk[0:32, 0:128]
            table[base + 5] = fk[32:64, 128:256]
        return carry

    lax.fori_loop(0, groups, turn, 0)
    for s in range(24):
        out_face[s // 4, s % 4] = table[jnp.maximum(req_ref[s], 0)]
    wait_peers(regions, owners)
    send_faces(regions, owners, my_r, my_s, False, out_face, in_face, fsend, frecv)
    start_blocks(owners, my_r, my_s, pair, cots, got_cots, bsem.at[0], bsem.at[1])
    plan = fill_weights(fine_ref, w_ref, wt_ref)
    wait_faces(regions, owners, my_r, my_s, False, out_face, in_face, fsend, frecv)

    row8 = lax.broadcasted_iota(jnp.int32, (ROWS, 128), 0)
    first_j = lax.rem(row8, 16) < 4
    last_j = lax.rem(row8, 16) >= 12
    first_k = lax.rem(row8, 4) == 0
    last_k = lax.rem(row8, 4) == 3
    low4 = lax.rem(lax.broadcasted_iota(jnp.int32, (32, 128), 0), 8) < 4

    def halo(b, d):
        code = code_ref[b * 6 + d]
        own = table[jnp.clip(code, 0, face_total - 1)]
        slot = jnp.clip(code - face_total, 0, 23)
        got = in_face[slot // 4, lax.rem(slot, 4)]
        picked = jnp.where(code >= face_total, got, own)
        return jnp.where(code >= 0, picked, jnp.zeros_like(picked))

    def spread_j(slab, to_last):
        if to_last:
            even, odd = row_roll(slab, 4), slab
        else:
            even, odd = slab, row_roll(slab, -4)
        rows = []
        for i in range(8):
            piece = (even if i % 2 == 0 else odd)[(i // 2) * 8:(i // 2) * 8 + 8]
            rows += [piece, piece]
        return jnp.concatenate(rows, axis=0)

    def pick_j(values, from_last):
        if from_last:
            return jnp.where(low4, row_roll(pieces8(values, 8, 32, 4), -4),
                             pieces8(values, 24, 32, 4))
        return jnp.where(low4, pieces8(values, 0, 32, 4),
                         row_roll(pieces8(values, 16, 32, 4), 4))

    def forward_taps(b, n):
        row = pl.multiple_of(b * ROWS, ROWS)
        x = x_ref[pl.ds(row, ROWS), :]
        xk = xk_ref[pl.ds(row, ROWS), :].astype(F32)
        x32 = x.astype(F32)
        h = [halo(b, d) for d in range(6)]
        halo_scr[n, pl.ds(3, 32, stride=4), :] = h[5].astype(F32)
        halo_scr[n, pl.ds(0, 32, stride=4), :] = h[4].astype(F32)
        edge = halo_scr[n]
        out = pl.ds(row, ROWS)
        taps_ref[out, 0:256] = x
        taps_ref[out, 256:512] = jnp.concatenate(
            [jnp.concatenate([h[0][0:16], h[0][16:32]], axis=1), x[0:112]], axis=0)
        taps_ref[out, 512:768] = jnp.concatenate(
            [x[16:128], jnp.concatenate([h[1][0:16], h[1][16:32]], axis=1)], axis=0)
        taps_ref[out, 768:896] = jnp.where(
            last_j, spread_j(h[3].astype(F32), True), row_roll(x32[:, 0:128], -4)).astype(BF)
        taps_ref[out, 896:1024] = jnp.where(
            first_j, spread_j(h[2].astype(F32), False), row_roll(x32[:, 128:256], 4)).astype(BF)
        taps_ref[out, 1024:1152] = jnp.where(
            last_k, edge, row_roll(xk[:, 0:128], -1)).astype(BF)
        taps_ref[out, 1152:1280] = jnp.where(
            first_k, edge, row_roll(xk[:, 128:256], 1)).astype(BF)

    def forward(g, carry):
        for n in range(GROUP):
            forward_taps(g * GROUP + n, n)
        row = pl.multiple_of(g * wide_rows, wide_rows)
        half = pl.multiple_of(g * half_rows, half_rows)
        for n in range(GROUP):
            part = pl.ds(pl.multiple_of(row + n * ROWS, ROWS), ROWS)
            hidden = dot(taps_ref[part, :], w_ref[...])
            act, slope = silu_parts(hidden)
            slope_ref[part, :] = slope
            act = act.astype(BF)
            dst = pl.ds(pl.multiple_of(half + n * 64, 64), 64)
            act_ref[dst, 0:256] = jnp.concatenate(
                [act[32 * m:32 * m + 16] for m in range(4)], axis=0)
            act_ref[dst, 256:512] = jnp.concatenate(
                [act[32 * m + 16:32 * m + 32] for m in range(4)], axis=0)
        out = pl.ds(half, half_rows)
        reduced = dot(act_ref[out, :], down_ref[...]).astype(BF)
        red_ref[out, :] = reduced
        c_out, c_slope = silu_parts(dot(reduced, coarse_ref[...]))
        co_ref[pl.ds(g * GROUP, GROUP)] = c_out.astype(BF).reshape(GROUP, 64, 128)
        cslope_ref[out, :] = c_slope
        return carry

    lax.fori_loop(0, groups, forward, 0)

    def gather_out(s, carry):
        co_slots[s] = co_ref[child_inv[s]]
        return carry

    lax.fori_loop(0, slots, gather_out, 0, unroll=8)
    wait_blocks(owners, my_r, my_s, pair, cots, got_cots, bsem.at[0], bsem.at[1])
    for u in range(pair):
        got_cots[my_s * pair + u] = cots[my_s * pair + u]
    start_blocks(owners, my_r, my_s, pair, co_slots, blocks_out, csem.at[0], csem.at[1])
    keep = pltpu.make_async_copy(co_slots.at[pl.ds(my_s * pair, pair)],
                                 blocks_out.at[pl.ds(my_s * pair, pair)], osem)
    keep.start()

    def coarse_back(g, carry):
        row = pl.multiple_of(g * wide_rows, wide_rows)
        half = pl.multiple_of(g * half_rows, half_rows)
        out = pl.ds(half, half_rows)
        cot_rows = jnp.concatenate(
            [got_cots[slot_ref[g * GROUP + n]] for n in range(GROUP)], axis=0).astype(F32)
        c_grad = (cot_rows * cslope_ref[out, :]).astype(BF)
        cg_ref[out, :] = c_grad
        child = dot(c_grad, coarse_ref[...], NT).astype(BF)
        ch_ref[out, :] = child
        ga = dot(child, down_ref[...], NT)
        for n in range(GROUP * 4):
            for a in range(2):
                part = pl.ds(pl.multiple_of(row + n * 32 + a * 16, 16), 16)
                gh_ref[part, :] = (ga[16 * n:16 * n + 16, a * 256:a * 256 + 256]
                                   * slope_ref[part, :]).astype(BF)
        return carry

    lax.fori_loop(0, groups, coarse_back, 0)

    def put_rows(start, value):
        count = value.shape[0] // 8
        grads[start // 8:start // 8 + count] = value.reshape(count, 8, 128)

    turned = dot(gh_ref[...], taps_ref[...], TN) * scale_fine
    sums = [None] * 7
    for tap, fwd, bwd, pairs in plan:
        for q_in, q_out in pairs:
            spot = fwd * 256 + (SWAP[q_in] if fwd == 4 else q_in) * 64
            part = turned[q_out * 64:q_out * 64 + 64, spot:spot + 64]
            sums[tap] = part if sums[tap] is None else sums[tap] + part
    sums.append(jnp.zeros_like(sums[0]))
    for n in range(4):
        put_rows(n * 64, jnp.concatenate([sums[2 * n], sums[2 * n + 1]], axis=0).T)
    put_rows(256, dot(act_ref[...], ch_ref[...], TN) * scale_fine)
    put_rows(768, dot(red_ref[...], cg_ref[...], TN) * scale_coarse)
    phases = sum_phases(regions, owners, my_r, my_s, grads, pair_got, half_sum, part_x, x_sum,
                        part_p, mine, total_ref, rsem)
    next(phases)

    def backward(g):
        row = g * wide_rows
        bwd, f0, f1, fj, fk = [], [], [], [], []
        for n in range(GROUP):
            gh = gh_ref[row + n * ROWS:row + (n + 1) * ROWS, :]
            g32 = gh.astype(F32)
            low, high = g32[:, 0:128], g32[:, 128:256]
            zero = jnp.zeros_like(low)
            swapped = jnp.concatenate([gh[:, 0:64], gh[:, 128:192], gh[:, 64:128], gh[:, 192:256]],
                                      axis=1).astype(F32)
            k_low, k_high = swapped[:, 0:128], swapped[:, 128:256]
            blank = jnp.zeros((16, LANES), BF)
            bwd.append(jnp.concatenate([
                gh,
                jnp.concatenate([blank, gh[0:112]], axis=0),
                jnp.concatenate([gh[16:128], blank], axis=0),
                jnp.where(last_j, zero, row_roll(low, -4)).astype(BF),
                jnp.where(first_j, zero, row_roll(high, 4)).astype(BF),
                jnp.where(last_k, zero, row_roll(k_low, -1)).astype(BF),
                jnp.where(first_k, zero, row_roll(k_high, 1)).astype(BF)], axis=1))
            f0.append(gh[0:16])
            f1.append(gh[112:128])
            fj.append(jnp.concatenate([pick_j(low, False), pick_j(high, True)], axis=1).astype(BF))
            g_scr[2 * n] = k_low
            g_scr[2 * n + 1] = k_high
            fk.append(jnp.concatenate([g_scr[2 * n, pl.ds(0, 32, stride=4), :],
                                       g_scr[2 * n + 1, pl.ds(3, 32, stride=4), :]],
                                      axis=1).astype(BF))
        for n in range(GROUP):
            gin_ref[row + n * ROWS:row + (n + 1) * ROWS, :] = dot(bwd[n], wt_ref[...])
        p0 = dot(jnp.concatenate(f0, axis=0), wt_ref[512:768, :]).astype(BF)
        p1 = dot(jnp.concatenate(f1, axis=0), wt_ref[256:512, :]).astype(BF)
        pj = dot(jnp.concatenate(fj, axis=0), wt_ref[768:1024, :]).astype(BF)
        pk = dot(jnp.concatenate(fk, axis=0), wt_ref[1024:1280, :]).astype(BF)
        for n in range(GROUP):
            base = (g * GROUP + n) * 6
            a, c = p0[n * 16:n * 16 + 16], p1[n * 16:n * 16 + 16]
            j, k = pj[n * 32:n * 32 + 32], pk[n * 32:n * 32 + 32]
            plane_ref[base] = jnp.concatenate([a[:, 0:128], a[:, 128:256]], axis=0)
            plane_ref[base + 1] = jnp.concatenate([c[:, 0:128], c[:, 128:256]], axis=0)
            plane_ref[base + 2] = j[:, 128:256]
            plane_ref[base + 3] = j[:, 0:128]
            plane_ref[base + 4] = jnp.concatenate([k[:, 64:128], k[:, 192:256]], axis=1)
            plane_ref[base + 5] = jnp.concatenate([k[:, 0:64], k[:, 128:192]], axis=1)

    for g in range(groups):
        backward(g)
        if g == 0 or g == 2:
            next(phases)
    for s in range(24):
        back_face[s // 4, s % 4] = plane_ref[face_inv[s]]
    chain[face_total + 24] = jnp.zeros((32, 128), F32)
    send_faces(regions, owners, my_r, my_s, True, back_face, ans_ref, hsend, hrecv)

    def add_plane(n, carry):
        chain[n] = chain[prev_ref[n]] + plane_ref[n].astype(F32)
        return carry

    lax.fori_loop(0, face_total, add_plane, 0, unroll=4)
    next(phases)
    wait_faces(regions, owners, my_r, my_s, True, back_face, ans_ref, hsend, hrecv)
    for s in range(24):
        chain[face_total + s] = (chain[prev_ref[face_total + s]]
                                 + ans_ref[s // 4, s % 4].astype(F32))
    loads[3].wait()
    lane = lax.broadcasted_iota(jnp.int32, (ROWS, LANES), 1)
    edge_k = lax.rem(lax.broadcasted_iota(jnp.int32, (ROWS, LANES), 0), 4) == jnp.where(
        lax.rem(lane, 128) < 64, 0, 3)

    def finish(g, carry):
        wides = []
        for n in range(GROUP):
            b = g * GROUP + n
            f = [chain[last_ref[b * 6 + d]] for d in range(6)]
            zero = jnp.zeros((ROWS, 128), F32)
            add_j = jnp.concatenate([jnp.where(first_j, spread_j(f[2], False), zero),
                                     jnp.where(last_j, spread_j(f[3], True), zero)], axis=1)
            for side in range(2):
                k0 = f[4] if side == 0 else pltpu.roll(f[4], 64, 1)
                k3 = f[5] if side == 1 else pltpu.roll(f[5], 64, 1)
                g_scr[2 * n + side, pl.ds(0, 32, stride=4), :] = k0
                g_scr[2 * n + side, pl.ds(3, 32, stride=4), :] = k3
            add_k = jnp.where(edge_k, jnp.concatenate([g_scr[2 * n], g_scr[2 * n + 1]], axis=1),
                              jnp.zeros((ROWS, LANES), F32))
            total = gin_ref[pl.ds(pl.multiple_of(b * ROWS, ROWS), ROWS), :] + add_j + add_k
            low = jnp.concatenate([f[0][0:16], f[0][16:32]], axis=1)
            high = jnp.concatenate([f[1][0:16], f[1][16:32]], axis=1)
            total = jnp.concatenate(
                [total[0:16] + low, total[16:112], total[112:128] + high], axis=0).astype(BF)
            flipped = total.T
            wides.append(jnp.concatenate([flipped[q * 64:q * 64 + 64] for q in range(4)], axis=1))
        out = dot(jnp.concatenate(wides, axis=0), order[...]).astype(BF)
        grad_ref[pl.ds(g * GROUP, GROUP)] = out.reshape(GROUP, 64, 512)
        return carry

    lax.fori_loop(0, groups, finish, 0)
    for _ in phases:
        pass
    keep.wait()
    wait_blocks(owners, my_r, my_s, pair, co_slots, blocks_out, csem.at[0], csem.at[1])


def sum_phases(regions, owners, my_r, my_s, grads, pair_got, half_sum, part_x, x_sum, part_p, mine,
               total_ref, sem):
    core = lax.rem(my_s, 2)
    other = 1 - core
    place_ = my_s // 2
    places = owners // 2
    half = pair_got.shape[0]
    per_r = half // regions
    unit = mine.shape[0]
    used = per_r // unit
    partner = (my_r, my_s + 1 - 2 * core)

    def remote(src, dst, n, target):
        return pltpu.make_async_remote_copy(
            src_ref=src, dst_ref=dst, send_sem=sem.at[2 * n], recv_sem=sem.at[2 * n + 1],
            device_id=target, device_id_type=MESH)

    swap = remote(grads.at[pl.ds(other * half, half)], pair_got, 0, partner)
    swap.start()
    yield
    swap.wait()
    half_sum[...] = grads[pl.ds(core * half, half)] + pair_got[...]
    for n in range(1, regions):
        peer = lax.rem(my_r + n, regions)
        remote(half_sum.at[pl.ds(peer * per_r, per_r)], part_x.at[pl.ds(my_r * per_r, per_r)], 1,
               (peer, my_s)).start()
    yield
    far = (lax.rem(my_r + 1, regions), my_s)
    got = pl.ds(0, (regions - 1) * per_r)
    arrived = remote(half_sum.at[got], part_x.at[got], 1, far)
    arrived.wait_send()
    arrived.wait_recv()
    run = half_sum[pl.ds(my_r * per_r, per_r)]
    for n in range(1, regions):
        run = run + part_x[pl.ds(lax.rem(my_r + n, regions) * per_r, per_r)]
    x_sum[...] = run

    def spot(peer):
        return (my_r, 2 * peer + core)

    owns = place_ < used
    mine_at = jnp.minimum(place_, used - 1) * unit

    def start_sum(n, carry):
        peer = lax.rem(place_ + n, places)

        @pl.when(peer < used)
        def _():
            remote(x_sum.at[pl.ds(jnp.minimum(peer, used - 1) * unit, unit)],
                   part_p.at[pl.ds(place_ * unit, unit)], 2, spot(peer)).start()
        return carry

    lax.fori_loop(1, places, start_sum, 0)
    yield
    near = spot(lax.rem(place_ + 1, places))
    base = core * half + my_r * per_r
    out_at = base + mine_at

    def wait_sent(count, n, src):
        if count:
            remote(src.at[pl.ds(0, count * unit)], part_p.at[pl.ds(0, count * unit)], n,
                   near).wait_send()

    def wait_got(count, n, dst):
        if count:
            remote(dst.at[pl.ds(0, count * unit)], dst.at[pl.ds(0, count * unit)], n,
                   near).wait_recv()

    @pl.when(owns)
    def _():
        wait_sent(used - 1, 2, x_sum)
        wait_got(places - 1, 2, part_p)
        run = x_sum[pl.ds(mine_at, unit)]
        for n in range(1, places):
            run = run + part_p[pl.ds(lax.rem(place_ + n, places) * unit, unit)]
        mine[...] = run
        total_ref[pl.ds(out_at, unit)] = run

        def start_share(n, carry):
            remote(mine, total_ref.at[pl.ds(out_at, unit)], 3,
                   spot(lax.rem(place_ + n, places))).start()
            return carry

        lax.fori_loop(1, places, start_share, 0)

    @pl.when(jnp.logical_not(owns))
    def _():
        wait_sent(used, 2, x_sum)
    yield

    @pl.when(owns)
    def _():
        wait_sent(places - 1, 3, part_p)
        wait_got(used - 1, 3, total_ref)

    @pl.when(jnp.logical_not(owns))
    def _():
        wait_got(used, 3, total_ref)

    for n in range(1, regions):
        peer = lax.rem(my_r + n, regions)
        remote(total_ref.at[pl.ds(base, per_r)], total_ref.at[pl.ds(base, per_r)], 4,
               (peer, my_s)).start()
    yield
    gone = remote(total_ref.at[got], total_ref.at[got], 4, far)
    gone.wait_send()
    gone.wait_recv()
    own = pl.ds(core * half, half)
    remote(total_ref.at[own], total_ref.at[own], 5, partner).start()
    yield
    last = remote(total_ref.at[own], total_ref.at[pl.ds(other * half, half)], 5, partner)
    last.wait_send()
    last.wait_recv()


def result_kernel(slot_ref, made_ref, arr_ref, total_ref, grad_ref, out_ref, fine_ref, down_ref,
                  coarse_ref):
    out_ref[...] = jnp.zeros_like(out_ref)

    def put_block(s, carry):
        spot = slot_ref[s]

        @pl.when(spot >= 0)
        def _():
            out_ref[spot] = arr_ref[s]
        return carry

    lax.fori_loop(0, arr_ref.shape[0], put_block, 0, unroll=4)
    grad_ref[...] = made_ref[...]
    for tap in range(7):
        rows = total_ref[tap // 2 * 8:tap // 2 * 8 + 8].reshape(64, 128)
        fine_ref[tap] = rows[:, tap % 2 * 64:tap % 2 * 64 + 64]
    down_ref[...] = total_ref[32:96].reshape(512, 128)
    coarse_ref[...] = total_ref[96:112].reshape(128, 128)


def on_device(features, fine_weight, down_weight, coarse_weight, cotangent, face_source,
              face_requests, child_slot, parent_octant):
    regions = lax.axis_size("region")
    owners = lax.axis_size("space")
    count = regions * owners
    bricks, channels, volume = features.shape
    faces = bricks * 6
    parents, _, wide = cotangent.shape
    octant = volume // 8
    slots = parent_octant.shape[1]
    shape = jax.ShapeDtypeStruct
    vm = pltpu.VMEM
    dma = pltpu.SemaphoreType.DMA
    codes = face_source.reshape(faces)
    requests = face_requests.reshape(24)
    targets = parent_octant.reshape(slots)
    child_inv, face_inv, prev, last = pl.pallas_call(
        index_kernel,
        out_shape=(shape((slots,), jnp.int32), shape((24,), jnp.int32),
                   shape((faces + 24,), jnp.int32), shape((faces,), jnp.int32)),
        in_specs=[SMEM_SPEC] * 3,
        out_specs=(SMEM_SPEC,) * 4,
        name="index",
    )(codes, child_slot, requests)
    scale_fine = 1.0 / math.sqrt(bricks * count * volume)
    scale_coarse = 1.0 / math.sqrt(parents * count * volume)
    places = owners // 2
    per_r = 56 // regions
    unit = max(1, per_r // places)
    big = bricks * ROWS
    small = bricks * octant
    block = (slots, octant, wide)
    faces4 = (6, 4, 32, 128)
    made, arrived, totals = pl.pallas_call(
        functools.partial(main_kernel, regions, owners, scale_fine, scale_coarse),
        out_shape=(shape((bricks, channels, volume), BF), shape(block, BF),
                   shape((112, 8, 128), F32)),
        in_specs=[SMEM_SPEC] * 8 + [ANY_SPEC] * 4 + [VMEM_SPEC] * 4,
        out_specs=(VMEM_SPEC, ANY_SPEC, VMEM_SPEC),
        scratch_shapes=[
            vm((bricks, channels, volume), BF), vm(block, BF), vm((512, 512), BF),
            vm((512, 512), BF), vm((big, LANES), BF), vm((big, LANES), BF),
            vm((faces, 32, 128), BF), vm(faces4, BF), vm(faces4, BF), vm(block, BF), vm(block, BF),
            vm((1280, LANES), BF), vm((1280, LANES), BF), vm((big, 1280), BF),
            vm((small, 512), BF), vm((big, LANES), BF), vm((small, wide), BF),
            vm((small, wide), BF), vm((small, wide), BF),
            vm((bricks, octant, wide), BF), vm(block, BF), vm((big, LANES), F32),
            vm((small, wide), F32), vm((big, LANES), F32), vm((faces, 32, 128), BF),
            vm(faces4, BF), vm(faces4, BF), vm((faces + 25, 32, 128), F32),
            vm((GROUP, ROWS, 128), F32), vm((2 * GROUP, ROWS, 128), F32),
            vm((112, 8, 128), F32), vm((56, 8, 128), F32), vm((56, 8, 128), F32),
            vm((56, 8, 128), F32), vm((per_r, 8, 128), F32), vm((places * unit, 8, 128), F32),
            vm((unit, 8, 128), F32),
            dma((4,)), dma((6,)), dma((6,)), dma((6,)), dma((6,)), dma, dma((2,)), dma((2,)),
            dma((12,))],
        compiler_params=pltpu.CompilerParams(
            collective_id=0, has_side_effects=True, vmem_limit_bytes=60 * 2**20),
        name="main",
    )(codes, child_slot, requests, targets, child_inv, face_inv, prev, last, features,
      cotangent.reshape(parents * 8, octant, wide), jnp.asarray(ORDER_T), jnp.asarray(ORDER),
      jnp.asarray(FACE), fine_weight, down_weight.reshape(8 * channels, wide), coarse_weight)
    grad_in, coarse_out, fine, down, coarse = pl.pallas_call(
        result_kernel,
        out_shape=(shape((bricks, channels, volume), BF), shape((parents * 8, octant, wide), BF),
                   shape((7, channels, channels), F32), shape((8 * channels, wide), F32),
                   shape((wide, wide), F32)),
        in_specs=[SMEM_SPEC] + [VMEM_SPEC] * 3,
        out_specs=(VMEM_SPEC,) * 5,
        compiler_params=pltpu.CompilerParams(vmem_limit_bytes=60 * 2**20),
        name="result",
    )(targets, made, arrived, totals)
    return (grad_in, coarse_out.reshape(parents, volume, wide), fine,
            down.reshape(8, channels, wide), coarse)


def solution(mesh):
    both = ("region", "space")
    return jax.shard_map(
        on_device,
        mesh=mesh,
        in_specs=(P(both, None, None), P(), P(), P(), P(both, None, None), P(both, None),
                  P(both, None), P(both), P(both, None)),
        out_specs=(P(both, None, None), P(both, None, None), P(), P(), P()),
        check_vma=False,
    )
```

```python
import functools
import math

import jax
import jax.numpy as jnp
import numpy as np
from jax import lax
from jax.experimental import pallas as pl
from jax.experimental.pallas import tpu as pltpu
from jax.sharding import PartitionSpec as P

EDGE = 8
BF = jnp.bfloat16
F32 = jnp.float32
MESH = pl.DeviceIdType.MESH
NT = (((1,), (1,)), ((), ()))
TN = (((0,), (0,)), ((), ()))
VMEM_SPEC = pl.BlockSpec(memory_space=pltpu.VMEM)
SMEM_SPEC = pl.BlockSpec(memory_space=pltpu.SMEM)
ANY_SPEC = pl.BlockSpec(memory_space=pl.ANY)
ROWS = 128
LANES = 256
GROUP = 4


def row_of(i, j, k):
    return i * 16 + j * 4 + k


def make_tables():
    order = np.zeros((512, 512), np.float32)
    for i in range(8):
        for j in range(8):
            for k in range(8):
                q = (j % 2) * 2 + k % 2
                order[q * 128 + row_of(i, j // 2, k // 2), i * 64 + j * 8 + k] = 1
    face = np.zeros((128, 128), np.float32)
    for i in range(8):
        for m in range(4):
            face[i * 4 + m, row_of(i, 0, m)] = 1
            face[32 + i * 4 + m, row_of(i, 3, m)] = 1
            face[64 + i * 4 + m, row_of(i, m, 0)] = 1
            face[96 + i * 4 + m, row_of(i, m, 3)] = 1
    cast = lambda a: np.asarray(a, dtype=BF)
    return cast(order), cast(order.T), cast(face)


ORDER, ORDER_T, FACE = make_tables()


def dot(a, b, dims=(((1,), (0,)), ((), ()))):
    return lax.dot_general(a, b, dims, preferred_element_type=F32)


def neighbours(regions, owners):
    far = owners // 4
    return [(1, 0), (-1, 0), (0, 1), (0, -1), (0, far), (0, -far)]


def face_moves(regions, owners, my_r, my_s, backward):
    sign = -1 if backward else 1
    for k, (dr, ds) in enumerate(neighbours(regions, owners)):
        to_r, to_s = my_r + sign * dr, my_s + sign * ds
        from_r, from_s = my_r - sign * dr, my_s - sign * ds
        can_send = (to_r >= 0) & (to_r < regions) & (to_s >= 0) & (to_s < owners)
        can_take = (from_r >= 0) & (from_r < regions) & (from_s >= 0) & (from_s < owners)
        yield k, (to_r, to_s), can_send, can_take


def send_faces(regions, owners, my_r, my_s, backward, src, dst, send_sem, recv_sem):
    for k, target, can_send, can_take in face_moves(regions, owners, my_r, my_s, backward):
        copy = pltpu.make_async_remote_copy(
            src_ref=src.at[k], dst_ref=dst.at[k], send_sem=send_sem.at[k],
            recv_sem=recv_sem.at[k], device_id=target, device_id_type=MESH)

        @pl.when(can_send)
        def _():
            copy.start()


def wait_faces(regions, owners, my_r, my_s, backward, src, dst, send_sem, recv_sem):
    for k, target, can_send, can_take in face_moves(regions, owners, my_r, my_s, backward):
        copy = pltpu.make_async_remote_copy(
            src_ref=src.at[k], dst_ref=dst.at[k], send_sem=send_sem.at[k],
            recv_sem=recv_sem.at[k], device_id=target, device_id_type=MESH)

        @pl.when(can_send)
        def _():
            copy.wait_send()

        @pl.when(can_take)
        def _():
            copy.wait_recv()


def block_copy(my_r, peer, pair, take, land, src, dst, send_sem, recv_sem):
    return pltpu.make_async_remote_copy(
        src_ref=src.at[pl.ds(take * pair, pair)], dst_ref=dst.at[pl.ds(land * pair, pair)],
        send_sem=send_sem, recv_sem=recv_sem, device_id=(my_r, peer),
        device_id_type=MESH)


def start_blocks(owners, my_r, my_s, pair, first, end, src, dst, send_sem, recv_sem):
    def start(step, carry):
        peer = lax.rem(my_s + step, owners)
        block_copy(my_r, peer, pair, peer, my_s, src, dst, send_sem, recv_sem).start()
        return carry

    lax.fori_loop(first, end, start, 0)


def wait_blocks(owners, my_r, my_s, pair, src, dst, send_sem, recv_sem):
    count = (owners - 1) * pair
    copy = pltpu.make_async_remote_copy(
        src_ref=src.at[pl.ds(0, count)], dst_ref=dst.at[pl.ds(0, count)], send_sem=send_sem,
        recv_sem=recv_sem, device_id=(my_r, lax.rem(my_s + 1, owners)), device_id_type=MESH)
    copy.wait_send()
    copy.wait_recv()


def silu_parts(v):
    s = 1.0 / (1.0 + jnp.exp(-v))
    return v * s, s * (1.0 + v * (1.0 - s))


def place(w_ref, base, q_in, q_out, block):
    w_ref[base + q_in * 64:base + q_in * 64 + 64, q_out * 64:q_out * 64 + 64] = block


SWAP = (0, 2, 1, 3)


def fill_weights(fine_ref, w_ref, wt_ref):
    w_ref[...] = jnp.zeros_like(w_ref)
    wt_ref[...] = jnp.zeros_like(wt_ref)
    same = [(q, q) for q in range(4)]
    up_j = [(0, 2), (1, 3)]
    down_j = [(2, 0), (3, 1)]
    up_k = [(0, 1), (2, 3)]
    down_k = [(1, 0), (3, 2)]
    plan = [
        (0, 0, 0, same), (1, 1, 2, same), (2, 2, 1, same),
        (3, 0, 0, up_j), (3, 3, 3, down_j), (4, 0, 0, down_j), (4, 3, 3, up_j),
        (5, 0, 0, up_k), (5, 4, 4, down_k), (6, 0, 0, down_k), (6, 4, 4, up_k),
    ]
    for tap, fwd, bwd, pairs in plan:
        w = fine_ref[tap]
        wt = w.astype(F32).T.astype(BF)
        for q_in, q_out in pairs:
            place(w_ref, fwd * 256, SWAP[q_in] if fwd == 4 else q_in, q_out, w)
            place(wt_ref, bwd * 256, SWAP[q_out] if bwd == 4 else q_out, q_in, wt)
    return plan


def signal_peers(regions, owners, my_r, my_s):
    barrier = pltpu.get_barrier_semaphore()

    def greet(step, carry):
        peer = lax.rem(my_s + step, owners)
        pl.semaphore_signal(barrier, inc=1, device_id=(my_r, peer), device_id_type=MESH)
        return carry

    lax.fori_loop(1, owners, greet, 0)

    for step in range(1, regions):
        far_r = lax.rem(my_r + step, regions)
        pl.semaphore_signal(barrier, inc=1, device_id=(far_r, my_s), device_id_type=MESH)


def wait_peers(regions, owners):
    barrier = pltpu.get_barrier_semaphore()
    pl.semaphore_wait(barrier, owners - 1 + regions - 1)


def row_roll(v, by):
    return pltpu.roll(v, by % v.shape[0], 0)


def pieces8(v, start, step, count):
    return jnp.concatenate([v[start + n * step:start + n * step + 8] for n in range(count)], axis=0)


def main_kernel(regions, owners, scale_fine, scale_coarse,
                code_ref, slot_ref, req_ref, po_ref,
                feat_hbm, cot_hbm, order_t_hbm, order_hbm, face_ref, fine_ref, down_ref,
                coarse_ref,
                grad_ref, blocks_out, total_ref,
                feat, cot, order_t, order, x_ref, xk_ref, table, out_face, in_face, cots,
                got_cots, w_ref, wt_ref, taps_ref, act_ref, gh_ref, red_ref, cg_ref, ch_ref,
                co_ref, co_slots, slope_ref, cslope_ref, gin_ref, plane_ref, back_face, ans_ref,
                chain, halo_scr, g_scr,
                grads, pair_got, half_sum, part_x, x_sum, part_p, mine, lists_v, lists,
                load, lsem, fsend, frecv, hsend, hrecv, osem, bsem, csem, rsem):
    my_r = lax.axis_index("region")
    my_s = lax.axis_index("space")
    bricks = feat.shape[0]
    face_total = table.shape[0]
    slots = cots.shape[0]
    pair = slots // owners
    groups = bricks // GROUP
    wide_rows = GROUP * ROWS
    half_rows = GROUP * 64
    loads = [pltpu.make_async_copy(src, dst, load.at[n]) for n, (src, dst) in enumerate(
        [(feat_hbm, feat), (order_t_hbm, order_t), (cot_hbm, cot), (order_hbm, order)])]
    for copy in loads:
        copy.start()
    signal_peers(regions, owners, my_r, my_s)
    loads[2].wait()

    def gather_cot(s, carry):
        cots[s] = cot[jnp.maximum(po_ref[s], 0)]
        return carry

    lax.fori_loop(0, slots, gather_cot, 0, unroll=8)
    wait_peers(regions, owners)
    early = 1 + owners // 5
    start_blocks(owners, my_r, my_s, pair, 1, early, cots, got_cots, bsem.at[0], bsem.at[1])
    loads[0].wait()
    loads[1].wait()

    def turn(g, carry):
        block = feat[pl.ds(g * GROUP, GROUP)].reshape(half_rows, 512)
        moved = dot(block, order_t[...]).astype(BF)
        for n in range(GROUP):
            b = g * GROUP + n
            row = pl.multiple_of(b * ROWS, ROWS)
            part = moved[n * 64:(n + 1) * 64]
            q = [part[:, m * 128:(m + 1) * 128] for m in range(4)]
            x = jnp.concatenate(q, axis=0).T
            x_ref[pl.ds(row, ROWS), :] = x
            xk = jnp.concatenate([q[m] for m in SWAP], axis=0).T
            xk_ref[pl.ds(row, ROWS), :] = xk
            fj = dot(face_ref[0:64], x).astype(BF)
            fk = dot(face_ref[64:128], xk).astype(BF)
            base = b * 6
            table[base] = jnp.concatenate([x[0:16, 0:128], x[0:16, 128:256]], axis=0)
            table[base + 1] = jnp.concatenate([x[112:128, 0:128], x[112:128, 128:256]], axis=0)
            table[base + 2] = fj[0:32, 0:128]
            table[base + 3] = fj[32:64, 128:256]
            table[base + 4] = fk[0:32, 0:128]
            table[base + 5] = fk[32:64, 128:256]
        return carry

    lax.fori_loop(0, groups, turn, 0)
    for s in range(24):
        out_face[s // 4, s % 4] = table[jnp.maximum(req_ref[s], 0)]
    send_faces(regions, owners, my_r, my_s, False, out_face, in_face, fsend, frecv)
    start_blocks(owners, my_r, my_s, pair, early, owners, cots, got_cots, bsem.at[0], bsem.at[1])

    def code_of(n):
        return code_ref[lax.rem(n, 6), n // 6]

    none = face_total + 24
    lanes = lax.broadcasted_iota(jnp.int32, (8, 128), 1)
    child = jnp.zeros((8, 128), jnp.int32)
    for b in range(bricks):
        child = jnp.where(lanes == slot_ref[b], b, child)

    def enter(n, target, carry):
        targets, last = carry
        return jnp.where(lanes == n, target, targets), jnp.where(lanes == target, n, last)

    def own_entry(n, carry):
        code = code_of(n)
        plane = jnp.where(lanes == code - face_total, n, carry[0])
        return (plane,) + enter(n, jnp.where(code < face_total, code, -1), carry[1:])

    plane, targets, last = lax.fori_loop(
        0, face_total, own_entry,
        (jnp.zeros((8, 128), jnp.int32), jnp.full((8, 128), -2, jnp.int32),
         jnp.full((8, 128), none, jnp.int32)), unroll=8)
    for n in range(24):
        targets, last = enter(face_total + n, req_ref[n], (targets, last))

    def link(n, target, prev):
        return jnp.where(targets == target, jnp.where(lanes > n, n, prev), prev)

    def own_link(n, prev):
        code = code_of(n)
        return link(n, jnp.where(code < face_total, code, -1), prev)

    prev = lax.fori_loop(0, face_total, own_link, jnp.full((8, 128), none, jnp.int32), unroll=8)
    for n in range(24):
        prev = link(face_total + n, req_ref[n], prev)
    lists_v[...] = jnp.concatenate([child[0:1], plane[0:1], prev[0:1], last[0:1], child[0:4]], axis=0)
    move = pltpu.make_async_copy(lists_v, lists, lsem)
    move.start()
    move.wait()
    plan = fill_weights(fine_ref, w_ref, wt_ref)
    wait_faces(regions, owners, my_r, my_s, False, out_face, in_face, fsend, frecv)

    row8 = lax.broadcasted_iota(jnp.int32, (ROWS, 128), 0)
    first_j = lax.rem(row8, 16) < 4
    last_j = lax.rem(row8, 16) >= 12
    first_k = lax.rem(row8, 4) == 0
    last_k = lax.rem(row8, 4) == 3
    low4 = lax.rem(lax.broadcasted_iota(jnp.int32, (32, 128), 0), 8) < 4

    def halo(b, d):
        code = code_ref[d, b]
        own = table[jnp.clip(code, 0, face_total - 1)]
        slot = jnp.clip(code - face_total, 0, 23)
        got = in_face[slot // 4, lax.rem(slot, 4)]
        picked = jnp.where(code >= face_total, got, own)
        return jnp.where(code >= 0, picked, jnp.zeros_like(picked))

    def spread_j(slab, to_last):
        if to_last:
            even, odd = row_roll(slab, 4), slab
        else:
            even, odd = slab, row_roll(slab, -4)
        rows = []
        for i in range(8):
            piece = (even if i % 2 == 0 else odd)[(i // 2) * 8:(i // 2) * 8 + 8]
            rows += [piece, piece]
        return jnp.concatenate(rows, axis=0)

    def pick_j(values, from_last):
        if from_last:
            return jnp.where(low4, row_roll(pieces8(values, 8, 32, 4), -4),
                             pieces8(values, 24, 32, 4))
        return jnp.where(low4, pieces8(values, 0, 32, 4),
                         row_roll(pieces8(values, 16, 32, 4), 4))

    def forward_taps(g, n):
        b = g * GROUP + n
        row = pl.multiple_of(pl.multiple_of(g * wide_rows, wide_rows) + n * ROWS, ROWS)
        x = x_ref[pl.ds(row, ROWS), :]
        xk = xk_ref[pl.ds(row, ROWS), :].astype(F32)
        x32 = x.astype(F32)
        h = [halo(b, d) for d in range(6)]
        halo_scr[n, pl.ds(3, 32, stride=4), :] = h[5].astype(F32)
        halo_scr[n, pl.ds(0, 32, stride=4), :] = h[4].astype(F32)
        edge = halo_scr[n]
        out = pl.ds(row, ROWS)
        taps_ref[out, 0:256] = x
        taps_ref[out, 256:512] = jnp.concatenate(
            [jnp.concatenate([h[0][0:16], h[0][16:32]], axis=1), x[0:112]], axis=0)
        taps_ref[out, 512:768] = jnp.concatenate(
            [x[16:128], jnp.concatenate([h[1][0:16], h[1][16:32]], axis=1)], axis=0)
        taps_ref[out, 768:896] = jnp.where(
            last_j, spread_j(h[3].astype(F32), True), row_roll(x32[:, 0:128], -4)).astype(BF)
        taps_ref[out, 896:1024] = jnp.where(
            first_j, spread_j(h[2].astype(F32), False), row_roll(x32[:, 128:256], 4)).astype(BF)
        taps_ref[out, 1024:1152] = jnp.where(
            last_k, edge, row_roll(xk[:, 0:128], -1)).astype(BF)
        taps_ref[out, 1152:1280] = jnp.where(
            first_k, edge, row_roll(xk[:, 128:256], 1)).astype(BF)

    def forward(g, carry):
        row = pl.multiple_of(g * wide_rows, wide_rows)
        half = pl.multiple_of(g * half_rows, half_rows)
        forward_taps(g, 0)
        for n in range(GROUP):
            if n + 1 < GROUP:
                forward_taps(g, n + 1)
            part = pl.ds(pl.multiple_of(row + n * ROWS, ROWS), ROWS)
            hidden = dot(taps_ref[part, :], w_ref[...])
            act, slope = silu_parts(hidden)
            slope_ref[part, :] = slope
            act = act.astype(BF)
            dst = pl.ds(pl.multiple_of(half + n * 64, 64), 64)
            act_ref[dst, 0:256] = jnp.concatenate(
                [act[32 * m:32 * m + 16] for m in range(4)], axis=0)
            act_ref[dst, 256:512] = jnp.concatenate(
                [act[32 * m + 16:32 * m + 32] for m in range(4)], axis=0)
        out = pl.ds(half, half_rows)
        reduced = dot(act_ref[out, :], down_ref[...]).astype(BF)
        red_ref[out, :] = reduced
        c_out, c_slope = silu_parts(dot(reduced, coarse_ref[...]))
        co_ref[pl.ds(g * GROUP, GROUP)] = c_out.astype(BF).reshape(GROUP, 64, 128)
        cslope_ref[out, :] = c_slope
        return carry

    lax.fori_loop(0, groups, forward, 0)

    def gather_out(s, carry):
        co_slots[s] = co_ref[lists[0, s]]
        return carry

    lax.fori_loop(0, slots, gather_out, 0, unroll=8)
    wait_blocks(owners, my_r, my_s, pair, cots, got_cots, bsem.at[0], bsem.at[1])
    for u in range(pair):
        got_cots[my_s * pair + u] = cots[my_s * pair + u]
    cuts = (1, 1 + owners // 2, 1 + 3 * owners // 4, owners)

    def send_out(n):
        start_blocks(owners, my_r, my_s, pair, cuts[n], cuts[n + 1], co_slots, blocks_out,
                     csem.at[0], csem.at[1])

    send_out(0)
    keep = pltpu.make_async_copy(co_slots.at[pl.ds(my_s * pair, pair)],
                                 blocks_out.at[pl.ds(my_s * pair, pair)], osem)
    keep.start()

    def coarse_back(g, carry):
        row = pl.multiple_of(g * wide_rows, wide_rows)
        half = pl.multiple_of(g * half_rows, half_rows)
        out = pl.ds(half, half_rows)
        cot_rows = jnp.concatenate(
            [got_cots[slot_ref[g * GROUP + n]] for n in range(GROUP)], axis=0).astype(F32)
        c_grad = (cot_rows * cslope_ref[out, :]).astype(BF)
        cg_ref[out, :] = c_grad
        child = dot(c_grad, coarse_ref[...], NT).astype(BF)
        ch_ref[out, :] = child
        ga = dot(child, down_ref[...], NT)
        for n in range(GROUP * 4):
            for a in range(2):
                part = pl.ds(pl.multiple_of(row + n * 32 + a * 16, 16), 16)
                gh_ref[part, :] = (ga[16 * n:16 * n + 16, a * 256:a * 256 + 256]
                                   * slope_ref[part, :]).astype(BF)
        return carry

    lax.fori_loop(0, groups, coarse_back, 0)

    def put_rows(start, value):
        count = value.shape[0] // 8
        grads[start // 8:start // 8 + count] = value.reshape(count, 8, 128)

    turned = dot(gh_ref[...], taps_ref[...], TN) * scale_fine
    sums = [None] * 7
    for tap, fwd, bwd, pairs in plan:
        for q_in, q_out in pairs:
            spot = fwd * 256 + (SWAP[q_in] if fwd == 4 else q_in) * 64
            part = turned[q_out * 64:q_out * 64 + 64, spot:spot + 64]
            sums[tap] = part if sums[tap] is None else sums[tap] + part
    sums.append(jnp.zeros_like(sums[0]))
    for n in range(4):
        put_rows(n * 64, jnp.concatenate([sums[2 * n], sums[2 * n + 1]], axis=0).T)
    put_rows(256, dot(act_ref[...], ch_ref[...], TN) * scale_fine)
    put_rows(768, dot(red_ref[...], cg_ref[...], TN) * scale_coarse)
    phases = sum_phases(regions, owners, my_r, my_s, grads, pair_got, half_sum, part_x, x_sum,
                        part_p, mine, total_ref, rsem)
    next(phases)

    def backward(g):
        row = g * wide_rows
        bwd, f0, f1, fj, fk = [], [], [], [], []
        for n in range(GROUP):
            gh = gh_ref[row + n * ROWS:row + (n + 1) * ROWS, :]
            g32 = gh.astype(F32)
            low, high = g32[:, 0:128], g32[:, 128:256]
            zero = jnp.zeros_like(low)
            swapped = jnp.concatenate([gh[:, 0:64], gh[:, 128:192], gh[:, 64:128], gh[:, 192:256]],
                                      axis=1).astype(F32)
            k_low, k_high = swapped[:, 0:128], swapped[:, 128:256]
            blank = jnp.zeros((16, LANES), BF)
            bwd.append(jnp.concatenate([
                gh,
                jnp.concatenate([blank, gh[0:112]], axis=0),
                jnp.concatenate([gh[16:128], blank], axis=0),
                jnp.where(last_j, zero, row_roll(low, -4)).astype(BF),
                jnp.where(first_j, zero, row_roll(high, 4)).astype(BF),
                jnp.where(last_k, zero, row_roll(k_low, -1)).astype(BF),
                jnp.where(first_k, zero, row_roll(k_high, 1)).astype(BF)], axis=1))
            f0.append(gh[0:16])
            f1.append(gh[112:128])
            fj.append(jnp.concatenate([pick_j(low, False), pick_j(high, True)], axis=1).astype(BF))
            g_scr[2 * n] = k_low
            g_scr[2 * n + 1] = k_high
            fk.append(jnp.concatenate([g_scr[2 * n, pl.ds(0, 32, stride=4), :],
                                       g_scr[2 * n + 1, pl.ds(3, 32, stride=4), :]],
                                      axis=1).astype(BF))
        for n in range(GROUP):
            gin_ref[row + n * ROWS:row + (n + 1) * ROWS, :] = dot(bwd[n], wt_ref[...])
        p0 = dot(jnp.concatenate(f0, axis=0), wt_ref[512:768, :]).astype(BF)
        p1 = dot(jnp.concatenate(f1, axis=0), wt_ref[256:512, :]).astype(BF)
        pj = dot(jnp.concatenate(fj, axis=0), wt_ref[768:1024, :]).astype(BF)
        pk = dot(jnp.concatenate(fk, axis=0), wt_ref[1024:1280, :]).astype(BF)
        for n in range(GROUP):
            base = (g * GROUP + n) * 6
            a, c = p0[n * 16:n * 16 + 16], p1[n * 16:n * 16 + 16]
            j, k = pj[n * 32:n * 32 + 32], pk[n * 32:n * 32 + 32]
            plane_ref[base] = jnp.concatenate([a[:, 0:128], a[:, 128:256]], axis=0)
            plane_ref[base + 1] = jnp.concatenate([c[:, 0:128], c[:, 128:256]], axis=0)
            plane_ref[base + 2] = j[:, 128:256]
            plane_ref[base + 3] = j[:, 0:128]
            plane_ref[base + 4] = jnp.concatenate([k[:, 64:128], k[:, 192:256]], axis=1)
            plane_ref[base + 5] = jnp.concatenate([k[:, 0:64], k[:, 128:192]], axis=1)

    for g in range(groups):
        backward(g)
        if g == 0:
            next(phases)
    for s in range(24):
        back_face[s // 4, s % 4] = plane_ref[lists[1, s]]
    chain[face_total + 24] = jnp.zeros((32, 128), F32)
    send_faces(regions, owners, my_r, my_s, True, back_face, ans_ref, hsend, hrecv)

    def add_plane(n, carry):
        chain[n] = chain[lists[2, n]] + plane_ref[n].astype(F32)
        return carry

    lax.fori_loop(0, face_total, add_plane, 0, unroll=4)
    next(phases)
    send_out(1)
    wait_faces(regions, owners, my_r, my_s, True, back_face, ans_ref, hsend, hrecv)
    for s in range(24):
        chain[face_total + s] = (chain[lists[2, face_total + s]]
                                 + ans_ref[s // 4, s % 4].astype(F32))
    loads[3].wait()
    lane = lax.broadcasted_iota(jnp.int32, (ROWS, LANES), 1)
    edge_k = lax.rem(lax.broadcasted_iota(jnp.int32, (ROWS, LANES), 0), 4) == jnp.where(
        lax.rem(lane, 128) < 64, 0, 3)

    def finish(g, carry):
        wides = []
        for n in range(GROUP):
            b = g * GROUP + n
            f = [chain[lists[3, b * 6 + d]] for d in range(6)]
            zero = jnp.zeros((ROWS, 128), F32)
            add_j = jnp.concatenate([jnp.where(first_j, spread_j(f[2], False), zero),
                                     jnp.where(last_j, spread_j(f[3], True), zero)], axis=1)
            for side in range(2):
                k0 = f[4] if side == 0 else pltpu.roll(f[4], 64, 1)
                k3 = f[5] if side == 1 else pltpu.roll(f[5], 64, 1)
                g_scr[2 * n + side, pl.ds(0, 32, stride=4), :] = k0
                g_scr[2 * n + side, pl.ds(3, 32, stride=4), :] = k3
            add_k = jnp.where(edge_k, jnp.concatenate([g_scr[2 * n], g_scr[2 * n + 1]], axis=1),
                              jnp.zeros((ROWS, LANES), F32))
            total = gin_ref[pl.ds(pl.multiple_of(b * ROWS, ROWS), ROWS), :] + add_j + add_k
            low = jnp.concatenate([f[0][0:16], f[0][16:32]], axis=1)
            high = jnp.concatenate([f[1][0:16], f[1][16:32]], axis=1)
            total = jnp.concatenate(
                [total[0:16] + low, total[16:112], total[112:128] + high], axis=0).astype(BF)
            flipped = total.T
            wides.append(jnp.concatenate([flipped[q * 64:q * 64 + 64] for q in range(4)], axis=1))
        out = dot(jnp.concatenate(wides, axis=0), order[...]).astype(BF)
        grad_ref[pl.ds(g * GROUP, GROUP)] = out.reshape(GROUP, 64, 512)
        return carry

    lax.fori_loop(0, groups, finish, 0)
    next(phases)
    send_out(2)
    for _ in phases:
        pass
    keep.wait()
    wait_blocks(owners, my_r, my_s, pair, co_slots, blocks_out, csem.at[0], csem.at[1])


def sum_phases(regions, owners, my_r, my_s, grads, pair_got, half_sum, part_x, x_sum, part_p, mine,
               total_ref, sem):
    core = lax.rem(my_s, 2)
    other = 1 - core
    place_ = my_s // 2
    places = owners // 2
    half = pair_got.shape[0]
    per_r = half // regions
    unit = mine.shape[0]
    used = per_r // unit
    partner = (my_r, my_s + 1 - 2 * core)

    def remote(src, dst, n, target):
        return pltpu.make_async_remote_copy(
            src_ref=src, dst_ref=dst, send_sem=sem.at[2 * n], recv_sem=sem.at[2 * n + 1],
            device_id=target, device_id_type=MESH)

    swap = remote(grads.at[pl.ds(other * half, half)], pair_got, 0, partner)
    swap.start()
    yield
    swap.wait()
    half_sum[...] = grads[pl.ds(core * half, half)] + pair_got[...]
    for n in range(1, regions):
        peer = lax.rem(my_r + n, regions)
        remote(half_sum.at[pl.ds(peer * per_r, per_r)], part_x.at[pl.ds(my_r * per_r, per_r)], 1,
               (peer, my_s)).start()
    yield
    far = (lax.rem(my_r + 1, regions), my_s)
    got = pl.ds(0, (regions - 1) * per_r)
    arrived = remote(half_sum.at[got], part_x.at[got], 1, far)
    arrived.wait_send()
    arrived.wait_recv()
    run = half_sum[pl.ds(my_r * per_r, per_r)]
    for n in range(1, regions):
        run = run + part_x[pl.ds(lax.rem(my_r + n, regions) * per_r, per_r)]
    x_sum[...] = run

    def spot(peer):
        return (my_r, 2 * peer + core)

    owns = place_ < used
    mine_at = jnp.minimum(place_, used - 1) * unit

    def start_sum(n, carry):
        peer = lax.rem(place_ + n, places)

        @pl.when(peer < used)
        def _():
            remote(x_sum.at[pl.ds(jnp.minimum(peer, used - 1) * unit, unit)],
                   part_p.at[pl.ds(place_ * unit, unit)], 2, spot(peer)).start()
        return carry

    lax.fori_loop(1, places, start_sum, 0)
    yield
    near = spot(lax.rem(place_ + 1, places))
    base = core * half + my_r * per_r
    out_at = base + mine_at

    def wait_sent(count, n, src):
        if count:
            remote(src.at[pl.ds(0, count * unit)], src.at[pl.ds(0, count * unit)], n,
                   near).wait_send()

    def wait_got(count, n, dst):
        if count:
            remote(dst.at[pl.ds(0, count * unit)], dst.at[pl.ds(0, count * unit)], n,
                   near).wait_recv()

    @pl.when(owns)
    def _():
        wait_sent(used - 1, 2, x_sum)
        wait_got(places - 1, 2, part_p)
        run = x_sum[pl.ds(mine_at, unit)]
        for n in range(1, places):
            run = run + part_p[pl.ds(lax.rem(place_ + n, places) * unit, unit)]
        mine[...] = run.astype(BF)
        total_ref[pl.ds(out_at, unit)] = run.astype(BF)

        def start_share(n, carry):
            remote(mine, total_ref.at[pl.ds(out_at, unit)], 3,
                   spot(lax.rem(place_ + n, places))).start()
            return carry

        lax.fori_loop(1, places, start_share, 0)

    @pl.when(jnp.logical_not(owns))
    def _():
        wait_sent(used, 2, x_sum)
    yield

    @pl.when(owns)
    def _():
        wait_sent(places - 1, 3, total_ref)
        wait_got(used - 1, 3, total_ref)

    @pl.when(jnp.logical_not(owns))
    def _():
        wait_got(used, 3, total_ref)

    for n in range(1, regions):
        peer = lax.rem(my_r + n, regions)
        remote(total_ref.at[pl.ds(base, per_r)], total_ref.at[pl.ds(base, per_r)], 4,
               (peer, my_s)).start()
    yield
    gone = remote(total_ref.at[got], total_ref.at[got], 4, far)
    gone.wait_send()
    gone.wait_recv()
    own = pl.ds(core * half, half)
    remote(total_ref.at[own], total_ref.at[own], 5, partner).start()
    yield
    last = remote(total_ref.at[own], total_ref.at[pl.ds(other * half, half)], 5, partner)
    last.wait_send()
    last.wait_recv()


def result_kernel(slot_ref, made_ref, arr_ref, total_ref, grad_ref, out_ref, fine_ref, down_ref,
                  coarse_ref, made, arrived, out, sem):
    loads = [pltpu.make_async_copy(arr_ref, arrived, sem.at[0]),
             pltpu.make_async_copy(made_ref, made, sem.at[1])]
    for copy in loads:
        copy.start()
    out[...] = jnp.zeros_like(out)
    for tap in range(7):
        rows = total_ref[tap // 2 * 8:tap // 2 * 8 + 8].astype(F32).reshape(64, 128)
        fine_ref[tap] = rows[:, tap % 2 * 64:tap % 2 * 64 + 64]
    down_ref[...] = total_ref[32:96].astype(F32).reshape(512, 128)
    coarse_ref[...] = total_ref[96:112].astype(F32).reshape(128, 128)
    loads[0].wait()

    def put_block(s, carry):
        spot = slot_ref[s]

        @pl.when(spot >= 0)
        def _():
            out[spot] = arrived[s]
        return carry

    lax.fori_loop(0, arr_ref.shape[0], put_block, 0, unroll=4)
    stores = [pltpu.make_async_copy(out, out_ref, sem.at[2]),
              pltpu.make_async_copy(made, grad_ref, sem.at[3])]
    stores[0].start()
    loads[1].wait()
    stores[1].start()
    for copy in stores:
        copy.wait()


def on_device(features, fine_weight, down_weight, coarse_weight, cotangent, face_source,
              face_requests, child_slot, parent_octant):
    regions = lax.axis_size("region")
    owners = lax.axis_size("space")
    count = regions * owners
    bricks, channels, volume = features.shape
    faces = bricks * 6
    parents, _, wide = cotangent.shape
    octant = volume // 8
    slots = parent_octant.shape[1]
    shape = jax.ShapeDtypeStruct
    vm = pltpu.VMEM
    dma = pltpu.SemaphoreType.DMA
    requests = face_requests.reshape(24)
    targets = parent_octant.reshape(slots)
    scale_fine = 1.0 / math.sqrt(bricks * count * volume)
    scale_coarse = 1.0 / math.sqrt(parents * count * volume)
    places = owners // 2
    per_r = 56 // regions
    unit = max(1, per_r // places)
    big = bricks * ROWS
    small = bricks * octant
    block = (slots, octant, wide)
    faces4 = (6, 4, 32, 128)
    made, arrived, totals = pl.pallas_call(
        functools.partial(main_kernel, regions, owners, scale_fine, scale_coarse),
        out_shape=(shape((bricks, channels, volume), BF), shape(block, BF),
                   shape((112, 8, 128), BF)),
        in_specs=[SMEM_SPEC] * 4 + [ANY_SPEC] * 4 + [VMEM_SPEC] * 4,
        out_specs=(VMEM_SPEC, ANY_SPEC, VMEM_SPEC),
        scratch_shapes=[
            vm((bricks, channels, volume), BF), vm(block, BF), vm((512, 512), BF),
            vm((512, 512), BF), vm((big, LANES), BF), vm((big, LANES), BF),
            vm((faces, 32, 128), BF), vm(faces4, BF), vm(faces4, BF), vm(block, BF), vm(block, BF),
            vm((1280, LANES), BF), vm((1280, LANES), BF), vm((big, 1280), BF),
            vm((small, 512), BF), vm((big, LANES), BF), vm((small, wide), BF),
            vm((small, wide), BF), vm((small, wide), BF),
            vm((bricks, octant, wide), BF), vm(block, BF), vm((big, LANES), F32),
            vm((small, wide), F32), vm((big, LANES), F32), vm((faces, 32, 128), BF),
            vm(faces4, BF), vm(faces4, BF), vm((faces + 25, 32, 128), F32),
            vm((GROUP, ROWS, 128), F32), vm((2 * GROUP, ROWS, 128), F32),
            vm((112, 8, 128), F32), vm((56, 8, 128), F32), vm((56, 8, 128), F32),
            vm((56, 8, 128), F32), vm((per_r, 8, 128), F32), vm((places * unit, 8, 128), F32),
            vm((unit, 8, 128), BF), vm((8, 128), jnp.int32), pltpu.SMEM((8, 128), jnp.int32),
            dma((4,)), dma, dma((6,)), dma((6,)), dma((6,)), dma((6,)), dma, dma((2,)), dma((2,)),
            dma((12,))],
        compiler_params=pltpu.CompilerParams(
            collective_id=0, has_side_effects=True, vmem_limit_bytes=60 * 2**20),
        name="main",
    )(face_source.T, child_slot, requests, targets, features,
      cotangent.reshape(parents * 8, octant, wide), jnp.asarray(ORDER_T), jnp.asarray(ORDER),
      jnp.asarray(FACE), fine_weight, down_weight.reshape(8 * channels, wide), coarse_weight)
    grad_in, coarse_out, fine, down, coarse = pl.pallas_call(
        result_kernel,
        out_shape=(shape((bricks, channels, volume), BF), shape((parents * 8, octant, wide), BF),
                   shape((7, channels, channels), F32), shape((8 * channels, wide), F32),
                   shape((wide, wide), F32)),
        in_specs=[SMEM_SPEC, ANY_SPEC, ANY_SPEC, VMEM_SPEC],
        out_specs=(ANY_SPEC,) * 2 + (VMEM_SPEC,) * 3,
        scratch_shapes=[vm((bricks, channels, volume), BF), vm(block, BF),
                        vm((parents * 8, octant, wide), BF), dma((4,))],
        compiler_params=pltpu.CompilerParams(vmem_limit_bytes=60 * 2**20),
        name="result",
    )(targets, made, arrived, totals)
    return (grad_in, coarse_out.reshape(parents, volume, wide), fine,
            down.reshape(8, channels, wide), coarse)


def solution(mesh):
    both = ("region", "space")
    return jax.shard_map(
        on_device,
        mesh=mesh,
        in_specs=(P(both, None, None), P(), P(), P(), P(both, None, None), P(both, None),
                  P(both, None), P(both), P(both, None)),
        out_specs=(P(both, None, None), P(both, None, None), P(), P(), P()),
        check_vma=False,
    )
```

```python
import functools
import math

import jax
import jax.numpy as jnp
import numpy as np
from jax import lax
from jax.experimental import pallas as pl
from jax.experimental.pallas import tpu as pltpu
from jax.sharding import PartitionSpec as P

EDGE = 8
BF = jnp.bfloat16
F32 = jnp.float32
MESH = pl.DeviceIdType.MESH
NT = (((1,), (1,)), ((), ()))
TN = (((0,), (0,)), ((), ()))
VMEM_SPEC = pl.BlockSpec(memory_space=pltpu.VMEM)
SMEM_SPEC = pl.BlockSpec(memory_space=pltpu.SMEM)
ANY_SPEC = pl.BlockSpec(memory_space=pl.ANY)
ROWS = 128
LANES = 256
GROUP = 4


def row_of(i, j, k):
    return i * 16 + j * 4 + k


def make_tables():
    order = np.zeros((512, 512), np.float32)
    for i in range(8):
        for j in range(8):
            for k in range(8):
                q = (j % 2) * 2 + k % 2
                order[q * 128 + row_of(i, j // 2, k // 2), i * 64 + j * 8 + k] = 1
    face = np.zeros((128, 128), np.float32)
    for i in range(8):
        for m in range(4):
            face[i * 4 + m, row_of(i, 0, m)] = 1
            face[32 + i * 4 + m, row_of(i, 3, m)] = 1
            face[64 + i * 4 + m, row_of(i, m, 0)] = 1
            face[96 + i * 4 + m, row_of(i, m, 3)] = 1
    cast = lambda a: np.asarray(a, dtype=BF)
    return cast(order), cast(order.T), cast(face)


ORDER, ORDER_T, FACE = make_tables()


def dot(a, b, dims=(((1,), (0,)), ((), ()))):
    return lax.dot_general(a, b, dims, preferred_element_type=F32)


def neighbours(regions, owners):
    far = owners // 4
    return [(1, 0), (-1, 0), (0, 1), (0, -1), (0, far), (0, -far)]


def face_moves(regions, owners, my_r, my_s, backward):
    sign = -1 if backward else 1
    for k, (dr, ds) in enumerate(neighbours(regions, owners)):
        to_r, to_s = my_r + sign * dr, my_s + sign * ds
        from_r, from_s = my_r - sign * dr, my_s - sign * ds
        can_send = (to_r >= 0) & (to_r < regions) & (to_s >= 0) & (to_s < owners)
        can_take = (from_r >= 0) & (from_r < regions) & (from_s >= 0) & (from_s < owners)
        yield k, (to_r, to_s), can_send, can_take


def send_faces(regions, owners, my_r, my_s, backward, src, dst, send_sem, recv_sem):
    for k, target, can_send, can_take in face_moves(regions, owners, my_r, my_s, backward):
        copy = pltpu.make_async_remote_copy(
            src_ref=src.at[k], dst_ref=dst.at[k], send_sem=send_sem.at[k],
            recv_sem=recv_sem.at[k], device_id=target, device_id_type=MESH)

        @pl.when(can_send)
        def _():
            copy.start()


def wait_faces(regions, owners, my_r, my_s, backward, src, dst, send_sem, recv_sem):
    for k, target, can_send, can_take in face_moves(regions, owners, my_r, my_s, backward):
        copy = pltpu.make_async_remote_copy(
            src_ref=src.at[k], dst_ref=dst.at[k], send_sem=send_sem.at[k],
            recv_sem=recv_sem.at[k], device_id=target, device_id_type=MESH)

        @pl.when(can_send)
        def _():
            copy.wait_send()

        @pl.when(can_take)
        def _():
            copy.wait_recv()


def block_copy(my_r, peer, pair, take, land, src, dst, send_sem, recv_sem):
    return pltpu.make_async_remote_copy(
        src_ref=src.at[pl.ds(take * pair, pair)], dst_ref=dst.at[pl.ds(land * pair, pair)],
        send_sem=send_sem, recv_sem=recv_sem, device_id=(my_r, peer),
        device_id_type=MESH)


def peer_order(owners):
    rows = owners // 8
    if rows < 4:
        return [(0, n // 2, n % 2) for n in range(1, owners)]
    far = [(2, 2), (2, 1), (1, 2), (2, 3), (3, 2), (1, 1), (3, 3), (1, 3), (3, 1), (2, 0), (0, 2),
           (1, 0), (0, 3), (3, 0), (0, 1)]
    return [(a, b, c) for a, b in far for c in (0, 1)] + [(0, 0, 1)]


def start_blocks(owners, my_r, my_s, pair, first, end, src, dst, send_sem, recv_sem):
    rows, line = max(1, owners // 8), min(4, owners // 2)
    z, y, core = my_s // (2 * line), lax.rem(my_s // 2, line), lax.rem(my_s, 2)
    for dz, dy, dc in peer_order(owners)[first:end]:
        peer = (lax.rem(z + dz, rows) * line + lax.rem(y + dy, line)) * 2 + lax.rem(core + dc, 2)
        block_copy(my_r, peer, pair, peer, my_s, src, dst, send_sem, recv_sem).start()


def wait_blocks(owners, my_r, my_s, pair, src, dst, send_sem, recv_sem):
    count = (owners - 1) * pair
    copy = pltpu.make_async_remote_copy(
        src_ref=src.at[pl.ds(0, count)], dst_ref=dst.at[pl.ds(0, count)], send_sem=send_sem,
        recv_sem=recv_sem, device_id=(my_r, lax.rem(my_s + 1, owners)), device_id_type=MESH)
    copy.wait_send()
    copy.wait_recv()


def silu_parts(v):
    s = 1.0 / (1.0 + jnp.exp(-v))
    return v * s, s * (1.0 + v * (1.0 - s))


def place(w_ref, base, q_in, q_out, block):
    w_ref[base + q_in * 64:base + q_in * 64 + 64, q_out * 64:q_out * 64 + 64] = block


SWAP = (0, 2, 1, 3)


def fill_weights(fine_ref, w_ref, wt_ref):
    w_ref[...] = jnp.zeros_like(w_ref)
    wt_ref[...] = jnp.zeros_like(wt_ref)
    same = [(q, q) for q in range(4)]
    up_j = [(0, 2), (1, 3)]
    down_j = [(2, 0), (3, 1)]
    up_k = [(0, 1), (2, 3)]
    down_k = [(1, 0), (3, 2)]
    plan = [
        (0, 0, 0, same), (1, 1, 2, same), (2, 2, 1, same),
        (3, 0, 0, up_j), (3, 3, 3, down_j), (4, 0, 0, down_j), (4, 3, 3, up_j),
        (5, 0, 0, up_k), (5, 4, 4, down_k), (6, 0, 0, down_k), (6, 4, 4, up_k),
    ]
    for tap, fwd, bwd, pairs in plan:
        w = fine_ref[tap]
        wt = w.astype(F32).T.astype(BF)
        for q_in, q_out in pairs:
            place(w_ref, fwd * 256, SWAP[q_in] if fwd == 4 else q_in, q_out, w)
            place(wt_ref, bwd * 256, SWAP[q_out] if bwd == 4 else q_out, q_in, wt)
    return plan


def signal_peers(regions, owners, my_r, my_s):
    barrier = pltpu.get_barrier_semaphore()

    def greet(step, carry):
        peer = lax.rem(my_s + step, owners)
        pl.semaphore_signal(barrier, inc=1, device_id=(my_r, peer), device_id_type=MESH)
        return carry

    lax.fori_loop(1, owners, greet, 0)

    core = lax.rem(my_s, 2)

    def greet_far(place_, carry):
        for step in range(1, regions):
            far_r = lax.rem(my_r + step, regions)
            pl.semaphore_signal(barrier, inc=1, device_id=(far_r, 2 * place_ + core),
                                device_id_type=MESH)
        return carry

    lax.fori_loop(0, owners // 2, greet_far, 0)


def wait_peers(regions, owners):
    barrier = pltpu.get_barrier_semaphore()
    pl.semaphore_wait(barrier, owners - 1 + (regions - 1) * (owners // 2))


def row_roll(v, by):
    return pltpu.roll(v, by % v.shape[0], 0)


def pieces8(v, start, step, count):
    return jnp.concatenate([v[start + n * step:start + n * step + 8] for n in range(count)], axis=0)


def main_kernel(regions, owners, scale_fine, scale_coarse,
                code_ref, slot_ref, req_ref, po_ref,
                feat_hbm, cot_hbm, order_t_hbm, order_hbm, face_ref, fine_ref, down_ref,
                coarse_ref,
                grad_ref, blocks_out, total_ref,
                feat, cot, order_t, order, x_ref, xk_ref, table, out_face, in_face, cots,
                got_cots, w_ref, wt_ref, taps_ref, act_ref, gh_ref, red_ref, cg_ref, ch_ref,
                co_ref, co_slots, slope_ref, cslope_ref, gin_ref, plane_ref, back_face, ans_ref,
                chain, halo_scr, g_scr,
                grads, pair_got, half_sum, part_p, mine, lists_v, lists,
                load, lsem, fsend, frecv, hsend, hrecv, osem, bsem, csem, rsem):
    my_r = lax.axis_index("region")
    my_s = lax.axis_index("space")
    bricks = feat.shape[0]
    face_total = table.shape[0]
    slots = cots.shape[0]
    pair = slots // owners
    groups = bricks // GROUP
    wide_rows = GROUP * ROWS
    half_rows = GROUP * 64
    loads = [pltpu.make_async_copy(src, dst, load.at[n]) for n, (src, dst) in enumerate(
        [(feat_hbm, feat), (order_t_hbm, order_t), (cot_hbm, cot), (order_hbm, order)])]
    for copy in loads:
        copy.start()
    signal_peers(regions, owners, my_r, my_s)
    loads[2].wait()

    def gather_cot(s, carry):
        cots[s] = cot[jnp.maximum(po_ref[s], 0)]
        return carry

    lax.fori_loop(0, slots, gather_cot, 0, unroll=8)
    wait_peers(regions, owners)
    early = owners // 5
    start_blocks(owners, my_r, my_s, pair, 0, early, cots, got_cots, bsem.at[0], bsem.at[1])
    loads[0].wait()
    loads[1].wait()

    def turn(g, carry):
        block = feat[pl.ds(g * GROUP, GROUP)].reshape(half_rows, 512)
        moved = dot(block, order_t[...]).astype(BF)
        for n in range(GROUP):
            b = g * GROUP + n
            row = pl.multiple_of(b * ROWS, ROWS)
            part = moved[n * 64:(n + 1) * 64]
            q = [part[:, m * 128:(m + 1) * 128] for m in range(4)]
            x = jnp.concatenate(q, axis=0).T
            x_ref[pl.ds(row, ROWS), :] = x
            xk = jnp.concatenate([q[m] for m in SWAP], axis=0).T
            xk_ref[pl.ds(row, ROWS), :] = xk
            fj = dot(face_ref[0:64], x).astype(BF)
            fk = dot(face_ref[64:128], xk).astype(BF)
            base = b * 6
            table[base] = jnp.concatenate([x[0:16, 0:128], x[0:16, 128:256]], axis=0)
            table[base + 1] = jnp.concatenate([x[112:128, 0:128], x[112:128, 128:256]], axis=0)
            table[base + 2] = fj[0:32, 0:128]
            table[base + 3] = fj[32:64, 128:256]
            table[base + 4] = fk[0:32, 0:128]
            table[base + 5] = fk[32:64, 128:256]
        return carry

    lax.fori_loop(0, groups, turn, 0)
    for s in range(24):
        out_face[s // 4, s % 4] = table[jnp.maximum(req_ref[s], 0)]
    send_faces(regions, owners, my_r, my_s, False, out_face, in_face, fsend, frecv)
    start_blocks(owners, my_r, my_s, pair, early, owners - 1, cots, got_cots, bsem.at[0], bsem.at[1])

    none = face_total + 24
    lanes = lax.broadcasted_iota(jnp.int32, (8, 128), 1)
    child = jnp.zeros((8, 128), jnp.int32)
    for b in range(bricks):
        child = jnp.where(lanes == slot_ref[b], b, child)

    def enter(n, target, carry):
        targets, last = carry
        return jnp.where(lanes == n, target, targets), jnp.where(lanes == target, n, last)

    def own_entry(b, carry):
        plane, state = carry[0], carry[1:]
        for d in range(6):
            code = code_ref[d, b]
            plane = jnp.where(lanes == code - face_total, b * 6 + d, plane)
            state = enter(b * 6 + d, jnp.where(code < face_total, code, -1), state)
        return (plane,) + state

    plane, targets, last = lax.fori_loop(
        0, bricks, own_entry,
        (jnp.zeros((8, 128), jnp.int32), jnp.full((8, 128), -2, jnp.int32),
         jnp.full((8, 128), none, jnp.int32)), unroll=2)
    for n in range(24):
        targets, last = enter(face_total + n, req_ref[n], (targets, last))

    def link(n, target, prev):
        return jnp.where(targets == target, jnp.where(lanes > n, n, prev), prev)

    def own_link(b, prev):
        for d in range(6):
            code = code_ref[d, b]
            prev = link(b * 6 + d, jnp.where(code < face_total, code, -1), prev)
        return prev

    prev = lax.fori_loop(0, bricks, own_link, jnp.full((8, 128), none, jnp.int32), unroll=2)
    for n in range(24):
        prev = link(face_total + n, req_ref[n], prev)
    lists_v[...] = jnp.concatenate([child[0:1], plane[0:1], prev[0:1], last[0:1], child[0:4]], axis=0)
    move = pltpu.make_async_copy(lists_v, lists, lsem)
    move.start()
    move.wait()
    plan = fill_weights(fine_ref, w_ref, wt_ref)
    wait_faces(regions, owners, my_r, my_s, False, out_face, in_face, fsend, frecv)

    row8 = lax.broadcasted_iota(jnp.int32, (ROWS, 128), 0)
    first_j = lax.rem(row8, 16) < 4
    last_j = lax.rem(row8, 16) >= 12
    first_k = lax.rem(row8, 4) == 0
    last_k = lax.rem(row8, 4) == 3
    low4 = lax.rem(lax.broadcasted_iota(jnp.int32, (32, 128), 0), 8) < 4

    def halo(b, d):
        code = code_ref[d, b]
        own = table[jnp.clip(code, 0, face_total - 1)]
        slot = jnp.clip(code - face_total, 0, 23)
        got = in_face[slot // 4, lax.rem(slot, 4)]
        picked = jnp.where(code >= face_total, got, own)
        return jnp.where(code >= 0, picked, jnp.zeros_like(picked))

    def spread_j(slab, to_last):
        if to_last:
            even, odd = row_roll(slab, 4), slab
        else:
            even, odd = slab, row_roll(slab, -4)
        rows = []
        for i in range(8):
            piece = (even if i % 2 == 0 else odd)[(i // 2) * 8:(i // 2) * 8 + 8]
            rows += [piece, piece]
        return jnp.concatenate(rows, axis=0)

    def pick_j(values, from_last):
        if from_last:
            return jnp.where(low4, row_roll(pieces8(values, 8, 32, 4), -4),
                             pieces8(values, 24, 32, 4))
        return jnp.where(low4, pieces8(values, 0, 32, 4),
                         row_roll(pieces8(values, 16, 32, 4), 4))

    def forward_taps(g, n):
        b = g * GROUP + n
        row = pl.multiple_of(pl.multiple_of(g * wide_rows, wide_rows) + n * ROWS, ROWS)
        x = x_ref[pl.ds(row, ROWS), :]
        xk = xk_ref[pl.ds(row, ROWS), :].astype(F32)
        x32 = x.astype(F32)
        h = [halo(b, d) for d in range(6)]
        halo_scr[n, pl.ds(3, 32, stride=4), :] = h[5].astype(F32)
        halo_scr[n, pl.ds(0, 32, stride=4), :] = h[4].astype(F32)
        edge = halo_scr[n]
        out = pl.ds(row, ROWS)
        taps_ref[out, 0:256] = x
        taps_ref[out, 256:512] = jnp.concatenate(
            [jnp.concatenate([h[0][0:16], h[0][16:32]], axis=1), x[0:112]], axis=0)
        taps_ref[out, 512:768] = jnp.concatenate(
            [x[16:128], jnp.concatenate([h[1][0:16], h[1][16:32]], axis=1)], axis=0)
        taps_ref[out, 768:896] = jnp.where(
            last_j, spread_j(h[3].astype(F32), True), row_roll(x32[:, 0:128], -4)).astype(BF)
        taps_ref[out, 896:1024] = jnp.where(
            first_j, spread_j(h[2].astype(F32), False), row_roll(x32[:, 128:256], 4)).astype(BF)
        taps_ref[out, 1024:1152] = jnp.where(
            last_k, edge, row_roll(xk[:, 0:128], -1)).astype(BF)
        taps_ref[out, 1152:1280] = jnp.where(
            first_k, edge, row_roll(xk[:, 128:256], 1)).astype(BF)

    def forward(g, carry):
        row = pl.multiple_of(g * wide_rows, wide_rows)
        half = pl.multiple_of(g * half_rows, half_rows)
        forward_taps(g, 0)
        for n in range(GROUP):
            if n + 1 < GROUP:
                forward_taps(g, n + 1)
            part = pl.ds(pl.multiple_of(row + n * ROWS, ROWS), ROWS)
            hidden = dot(taps_ref[part, :], w_ref[...])
            act, slope = silu_parts(hidden)
            slope_ref[part, :] = slope
            act = act.astype(BF)
            dst = pl.ds(pl.multiple_of(half + n * 64, 64), 64)
            act_ref[dst, 0:256] = jnp.concatenate(
                [act[32 * m:32 * m + 16] for m in range(4)], axis=0)
            act_ref[dst, 256:512] = jnp.concatenate(
                [act[32 * m + 16:32 * m + 32] for m in range(4)], axis=0)
        out = pl.ds(half, half_rows)
        reduced = dot(act_ref[out, :], down_ref[...]).astype(BF)
        red_ref[out, :] = reduced
        c_out, c_slope = silu_parts(dot(reduced, coarse_ref[...]))
        co_ref[pl.ds(g * GROUP, GROUP)] = c_out.astype(BF).reshape(GROUP, 64, 128)
        cslope_ref[out, :] = c_slope
        return carry

    lax.fori_loop(0, groups, forward, 0)

    def gather_out(s, carry):
        co_slots[s] = co_ref[lists[0, s]]
        return carry

    lax.fori_loop(0, slots, gather_out, 0, unroll=8)
    wait_blocks(owners, my_r, my_s, pair, cots, got_cots, bsem.at[0], bsem.at[1])
    for u in range(pair):
        got_cots[my_s * pair + u] = cots[my_s * pair + u]
    cuts = (0, owners // 2, owners - 1)

    def send_out(n):
        start_blocks(owners, my_r, my_s, pair, cuts[n], cuts[n + 1], co_slots, blocks_out,
                     csem.at[0], csem.at[1])

    send_out(0)
    keep = pltpu.make_async_copy(co_slots.at[pl.ds(my_s * pair, pair)],
                                 blocks_out.at[pl.ds(my_s * pair, pair)], osem)
    keep.start()

    def coarse_back(g, carry):
        row = pl.multiple_of(g * wide_rows, wide_rows)
        half = pl.multiple_of(g * half_rows, half_rows)
        out = pl.ds(half, half_rows)
        cot_rows = jnp.concatenate(
            [got_cots[slot_ref[g * GROUP + n]] for n in range(GROUP)], axis=0).astype(F32)
        c_grad = (cot_rows * cslope_ref[out, :]).astype(BF)
        cg_ref[out, :] = c_grad
        child = dot(c_grad, coarse_ref[...], NT).astype(BF)
        ch_ref[out, :] = child
        ga = dot(child, down_ref[...], NT)
        for n in range(GROUP * 4):
            for a in range(2):
                part = pl.ds(pl.multiple_of(row + n * 32 + a * 16, 16), 16)
                gh_ref[part, :] = (ga[16 * n:16 * n + 16, a * 256:a * 256 + 256]
                                   * slope_ref[part, :]).astype(BF)
        return carry

    lax.fori_loop(0, groups, coarse_back, 0)

    def put_rows(start, value):
        count = value.shape[0] // 8
        grads[start // 8:start // 8 + count] = value.reshape(count, 8, 128)

    turned = dot(gh_ref[...], taps_ref[...], TN) * scale_fine
    sums = [None] * 7
    for tap, fwd, bwd, pairs in plan:
        for q_in, q_out in pairs:
            spot = fwd * 256 + (SWAP[q_in] if fwd == 4 else q_in) * 64
            part = turned[q_out * 64:q_out * 64 + 64, spot:spot + 64]
            sums[tap] = part if sums[tap] is None else sums[tap] + part
    sums.append(jnp.zeros_like(sums[0]))
    for n in range(4):
        put_rows(n * 64, jnp.concatenate([sums[2 * n], sums[2 * n + 1]], axis=0).T)
    put_rows(256, dot(act_ref[...], ch_ref[...], TN) * scale_fine)
    put_rows(768, dot(red_ref[...], cg_ref[...], TN) * scale_coarse)
    phases = sum_phases(regions, owners, my_r, my_s, grads, pair_got, half_sum, part_p, mine,
                        total_ref, rsem)
    next(phases)

    def backward(g):
        row = g * wide_rows
        bwd, f0, f1, fj, fk = [], [], [], [], []
        for n in range(GROUP):
            gh = gh_ref[row + n * ROWS:row + (n + 1) * ROWS, :]
            g32 = gh.astype(F32)
            low, high = g32[:, 0:128], g32[:, 128:256]
            zero = jnp.zeros_like(low)
            swapped = jnp.concatenate([gh[:, 0:64], gh[:, 128:192], gh[:, 64:128], gh[:, 192:256]],
                                      axis=1).astype(F32)
            k_low, k_high = swapped[:, 0:128], swapped[:, 128:256]
            blank = jnp.zeros((16, LANES), BF)
            bwd.append(jnp.concatenate([
                gh,
                jnp.concatenate([blank, gh[0:112]], axis=0),
                jnp.concatenate([gh[16:128], blank], axis=0),
                jnp.where(last_j, zero, row_roll(low, -4)).astype(BF),
                jnp.where(first_j, zero, row_roll(high, 4)).astype(BF),
                jnp.where(last_k, zero, row_roll(k_low, -1)).astype(BF),
                jnp.where(first_k, zero, row_roll(k_high, 1)).astype(BF)], axis=1))
            f0.append(gh[0:16])
            f1.append(gh[112:128])
            fj.append(jnp.concatenate([pick_j(low, False), pick_j(high, True)], axis=1).astype(BF))
            g_scr[2 * n] = k_low
            g_scr[2 * n + 1] = k_high
            fk.append(jnp.concatenate([g_scr[2 * n, pl.ds(0, 32, stride=4), :],
                                       g_scr[2 * n + 1, pl.ds(3, 32, stride=4), :]],
                                      axis=1).astype(BF))
        for n in range(GROUP):
            gin_ref[row + n * ROWS:row + (n + 1) * ROWS, :] = dot(bwd[n], wt_ref[...])
        p0 = dot(jnp.concatenate(f0, axis=0), wt_ref[512:768, :]).astype(BF)
        p1 = dot(jnp.concatenate(f1, axis=0), wt_ref[256:512, :]).astype(BF)
        pj = dot(jnp.concatenate(fj, axis=0), wt_ref[768:1024, :]).astype(BF)
        pk = dot(jnp.concatenate(fk, axis=0), wt_ref[1024:1280, :]).astype(BF)
        for n in range(GROUP):
            base = (g * GROUP + n) * 6
            a, c = p0[n * 16:n * 16 + 16], p1[n * 16:n * 16 + 16]
            j, k = pj[n * 32:n * 32 + 32], pk[n * 32:n * 32 + 32]
            plane_ref[base] = jnp.concatenate([a[:, 0:128], a[:, 128:256]], axis=0)
            plane_ref[base + 1] = jnp.concatenate([c[:, 0:128], c[:, 128:256]], axis=0)
            plane_ref[base + 2] = j[:, 128:256]
            plane_ref[base + 3] = j[:, 0:128]
            plane_ref[base + 4] = jnp.concatenate([k[:, 64:128], k[:, 192:256]], axis=1)
            plane_ref[base + 5] = jnp.concatenate([k[:, 0:64], k[:, 128:192]], axis=1)

    for g in range(groups):
        backward(g)
        if g == 0:
            next(phases)
            send_out(1)
    for s in range(24):
        back_face[s // 4, s % 4] = plane_ref[lists[1, s]]
    chain[face_total + 24] = jnp.zeros((32, 128), F32)
    send_faces(regions, owners, my_r, my_s, True, back_face, ans_ref, hsend, hrecv)

    def add_plane(n, carry):
        chain[n] = chain[lists[2, n]] + plane_ref[n].astype(F32)
        return carry

    lax.fori_loop(0, face_total, add_plane, 0, unroll=4)
    next(phases)
    wait_faces(regions, owners, my_r, my_s, True, back_face, ans_ref, hsend, hrecv)
    for s in range(24):
        chain[face_total + s] = (chain[lists[2, face_total + s]]
                                 + ans_ref[s // 4, s % 4].astype(F32))
    loads[3].wait()
    lane = lax.broadcasted_iota(jnp.int32, (ROWS, LANES), 1)
    edge_k = lax.rem(lax.broadcasted_iota(jnp.int32, (ROWS, LANES), 0), 4) == jnp.where(
        lax.rem(lane, 128) < 64, 0, 3)

    def finish(g, carry):
        wides = []
        for n in range(GROUP):
            b = g * GROUP + n
            f = [chain[lists[3, b * 6 + d]] for d in range(6)]
            zero = jnp.zeros((ROWS, 128), F32)
            add_j = jnp.concatenate([jnp.where(first_j, spread_j(f[2], False), zero),
                                     jnp.where(last_j, spread_j(f[3], True), zero)], axis=1)
            for side in range(2):
                k0 = f[4] if side == 0 else pltpu.roll(f[4], 64, 1)
                k3 = f[5] if side == 1 else pltpu.roll(f[5], 64, 1)
                g_scr[2 * n + side, pl.ds(0, 32, stride=4), :] = k0
                g_scr[2 * n + side, pl.ds(3, 32, stride=4), :] = k3
            add_k = jnp.where(edge_k, jnp.concatenate([g_scr[2 * n], g_scr[2 * n + 1]], axis=1),
                              jnp.zeros((ROWS, LANES), F32))
            total = gin_ref[pl.ds(pl.multiple_of(b * ROWS, ROWS), ROWS), :] + add_j + add_k
            low = jnp.concatenate([f[0][0:16], f[0][16:32]], axis=1)
            high = jnp.concatenate([f[1][0:16], f[1][16:32]], axis=1)
            total = jnp.concatenate(
                [total[0:16] + low, total[16:112], total[112:128] + high], axis=0).astype(BF)
            flipped = total.T
            wides.append(jnp.concatenate([flipped[q * 64:q * 64 + 64] for q in range(4)], axis=1))
        out = dot(jnp.concatenate(wides, axis=0), order[...]).astype(BF)
        grad_ref[pl.ds(g * GROUP, GROUP)] = out.reshape(GROUP, 64, 512)
        return carry

    lax.fori_loop(0, groups, finish, 0)
    for _ in phases:
        pass
    keep.wait()
    wait_blocks(owners, my_r, my_s, pair, co_slots, blocks_out, csem.at[0], csem.at[1])


def sum_phases(regions, owners, my_r, my_s, grads, pair_got, half_sum, part_p, mine, total_ref, sem):
    core = lax.rem(my_s, 2)
    other = 1 - core
    width = owners // 2
    chips = regions * width
    chip = my_r * width + my_s // 2
    half = pair_got.shape[0]
    unit = mine.shape[0]
    used = half // unit
    partner = (my_r, my_s + 1 - 2 * core)

    def remote(src, dst, n, target):
        return pltpu.make_async_remote_copy(
            src_ref=src, dst_ref=dst, send_sem=sem.at[2 * n], recv_sem=sem.at[2 * n + 1],
            device_id=target, device_id_type=MESH)

    def spot(peer):
        return (peer // width, 2 * lax.rem(peer, width) + core)

    near = spot(lax.rem(chip + 1, chips))

    def sized(ref, count, n):
        part = ref.at[pl.ds(0, count * unit)]
        return remote(part, part, n, near)

    swap = remote(grads.at[pl.ds(other * half, half)], pair_got, 0, partner)
    swap.start()
    yield
    swap.wait()
    half_sum[...] = grads[pl.ds(core * half, half)] + pair_got[...]
    owns = chip < used
    mine_at = jnp.minimum(chip, used - 1) * unit

    def start_sum(n, carry):
        peer = lax.rem(chip + n, chips)

        @pl.when(peer < used)
        def _():
            remote(half_sum.at[pl.ds(jnp.minimum(peer, used - 1) * unit, unit)],
                   part_p.at[pl.ds(chip * unit, unit)], 1, spot(peer)).start()
        return carry

    lax.fori_loop(1, chips, start_sum, 0)
    yield
    out_at = core * half + mine_at

    @pl.when(owns)
    def _():
        sized(half_sum, used - 1, 1).wait_send()
        sized(part_p, chips - 1, 1).wait_recv()
        part_p[pl.ds(chip * unit, unit)] = half_sum[pl.ds(mine_at, unit)]
        run = part_p[0:unit]
        for n in range(1, chips):
            run = run + part_p[n * unit:n * unit + unit]
        mine[...] = run.astype(BF)
        total_ref[pl.ds(out_at, unit)] = run.astype(BF)

        def start_share(n, carry):
            remote(mine, total_ref.at[pl.ds(out_at, unit)], 2,
                   spot(lax.rem(chip + n, chips))).start()
            return carry

        lax.fori_loop(1, chips, start_share, 0)

    if used < chips:
        @pl.when(jnp.logical_not(owns))
        def _():
            sized(half_sum, used, 1).wait_send()
    yield

    @pl.when(owns)
    def _():
        sized(total_ref, chips - 1, 2).wait_send()
        sized(total_ref, used - 1, 2).wait_recv()

    if used < chips:
        @pl.when(jnp.logical_not(owns))
        def _():
            sized(total_ref, used, 2).wait_recv()

    own = pl.ds(core * half, half)
    remote(total_ref.at[own], total_ref.at[own], 3, partner).start()
    yield
    last = remote(total_ref.at[own], total_ref.at[pl.ds(other * half, half)], 3, partner)
    last.wait_send()
    last.wait_recv()


def result_kernel(slot_ref, made_ref, arr_ref, total_ref, grad_ref, out_ref, fine_ref, down_ref,
                  coarse_ref):
    out_ref[...] = jnp.zeros_like(out_ref)

    def put_block(s, carry):
        spot = slot_ref[s]

        @pl.when(spot >= 0)
        def _():
            out_ref[spot] = arr_ref[s]
        return carry

    lax.fori_loop(0, arr_ref.shape[0], put_block, 0, unroll=4)
    grad_ref[...] = made_ref[...]
    for tap in range(7):
        rows = total_ref[tap // 2 * 8:tap // 2 * 8 + 8].astype(F32).reshape(64, 128)
        fine_ref[tap] = rows[:, tap % 2 * 64:tap % 2 * 64 + 64]
    down_ref[...] = total_ref[32:96].astype(F32).reshape(512, 128)
    coarse_ref[...] = total_ref[96:112].astype(F32).reshape(128, 128)


def on_device(features, fine_weight, down_weight, coarse_weight, cotangent, face_source,
              face_requests, child_slot, parent_octant):
    regions = lax.axis_size("region")
    owners = lax.axis_size("space")
    count = regions * owners
    bricks, channels, volume = features.shape
    faces = bricks * 6
    parents, _, wide = cotangent.shape
    octant = volume // 8
    slots = parent_octant.shape[1]
    shape = jax.ShapeDtypeStruct
    vm = pltpu.VMEM
    dma = pltpu.SemaphoreType.DMA
    requests = face_requests.reshape(24)
    targets = parent_octant.reshape(slots)
    scale_fine = 1.0 / math.sqrt(bricks * count * volume)
    scale_coarse = 1.0 / math.sqrt(parents * count * volume)
    chips = count // 2
    unit = max(1, 56 // chips)
    big = bricks * ROWS
    small = bricks * octant
    block = (slots, octant, wide)
    faces4 = (6, 4, 32, 128)
    made, arrived, totals = pl.pallas_call(
        functools.partial(main_kernel, regions, owners, scale_fine, scale_coarse),
        out_shape=(shape((bricks, channels, volume), BF), shape(block, BF),
                   shape((112, 8, 128), BF)),
        in_specs=[SMEM_SPEC] * 4 + [ANY_SPEC] * 4 + [VMEM_SPEC] * 4,
        out_specs=(VMEM_SPEC, ANY_SPEC, VMEM_SPEC),
        scratch_shapes=[
            vm((bricks, channels, volume), BF), vm(block, BF), vm((512, 512), BF),
            vm((512, 512), BF), vm((big, LANES), BF), vm((big, LANES), BF),
            vm((faces, 32, 128), BF), vm(faces4, BF), vm(faces4, BF), vm(block, BF), vm(block, BF),
            vm((1280, LANES), BF), vm((1280, LANES), BF), vm((big, 1280), BF),
            vm((small, 512), BF), vm((big, LANES), BF), vm((small, wide), BF),
            vm((small, wide), BF), vm((small, wide), BF),
            vm((bricks, octant, wide), BF), vm(block, BF), vm((big, LANES), F32),
            vm((small, wide), F32), vm((big, LANES), F32), vm((faces, 32, 128), BF),
            vm(faces4, BF), vm(faces4, BF), vm((faces + 25, 32, 128), F32),
            vm((GROUP, ROWS, 128), F32), vm((2 * GROUP, ROWS, 128), F32),
            vm((112, 8, 128), F32), vm((56, 8, 128), F32), vm((56, 8, 128), F32),
            vm((chips * unit, 8, 128), F32),
            vm((unit, 8, 128), BF), vm((8, 128), jnp.int32), pltpu.SMEM((8, 128), jnp.int32),
            dma((4,)), dma, dma((6,)), dma((6,)), dma((6,)), dma((6,)), dma, dma((2,)), dma((2,)),
            dma((8,))],
        compiler_params=pltpu.CompilerParams(
            collective_id=0, has_side_effects=True, vmem_limit_bytes=60 * 2**20),
        name="main",
    )(face_source.T, child_slot, requests, targets, features,
      cotangent.reshape(parents * 8, octant, wide), jnp.asarray(ORDER_T), jnp.asarray(ORDER),
      jnp.asarray(FACE), fine_weight, down_weight.reshape(8 * channels, wide), coarse_weight)
    grad_in, coarse_out, fine, down, coarse = pl.pallas_call(
        result_kernel,
        out_shape=(shape((bricks, channels, volume), BF), shape((parents * 8, octant, wide), BF),
                   shape((7, channels, channels), F32), shape((8 * channels, wide), F32),
                   shape((wide, wide), F32)),
        in_specs=[SMEM_SPEC] + [VMEM_SPEC] * 3,
        out_specs=(VMEM_SPEC,) * 5,
        compiler_params=pltpu.CompilerParams(vmem_limit_bytes=60 * 2**20),
        name="result",
    )(targets, made, arrived, totals)
    return (grad_in, coarse_out.reshape(parents, volume, wide), fine,
            down.reshape(8, channels, wide), coarse)


def solution(mesh):
    both = ("region", "space")
    return jax.shard_map(
        on_device,
        mesh=mesh,
        in_specs=(P(both, None, None), P(), P(), P(), P(both, None, None), P(both, None),
                  P(both, None), P(both), P(both, None)),
        out_specs=(P(both, None, None), P(both, None, None), P(), P(), P()),
        check_vma=False,
    )
```

```python
import functools
import math

import jax
import jax.numpy as jnp
import numpy as np
from jax import lax
from jax.experimental import pallas as pl
from jax.experimental.pallas import tpu as pltpu
from jax.sharding import PartitionSpec as P

EDGE = 8
BF = jnp.bfloat16
F32 = jnp.float32
MESH = pl.DeviceIdType.MESH
NT = (((1,), (1,)), ((), ()))
TN = (((0,), (0,)), ((), ()))
VMEM_SPEC = pl.BlockSpec(memory_space=pltpu.VMEM)
SMEM_SPEC = pl.BlockSpec(memory_space=pltpu.SMEM)
ANY_SPEC = pl.BlockSpec(memory_space=pl.ANY)
ROWS = 128
LANES = 256
GROUP = 4


def row_of(i, j, k):
    return i * 16 + j * 4 + k


def make_tables():
    order = np.zeros((512, 512), np.float32)
    for i in range(8):
        for j in range(8):
            for k in range(8):
                q = (j % 2) * 2 + k % 2
                order[q * 128 + row_of(i, j // 2, k // 2), i * 64 + j * 8 + k] = 1
    face = np.zeros((128, 128), np.float32)
    for i in range(8):
        for m in range(4):
            face[i * 4 + m, row_of(i, 0, m)] = 1
            face[32 + i * 4 + m, row_of(i, 3, m)] = 1
            face[64 + i * 4 + m, row_of(i, m, 0)] = 1
            face[96 + i * 4 + m, row_of(i, m, 3)] = 1
    cast = lambda a: np.asarray(a, dtype=BF)
    return cast(order), cast(order.T), cast(face)


ORDER, ORDER_T, FACE = make_tables()


def dot(a, b, dims=(((1,), (0,)), ((), ()))):
    return lax.dot_general(a, b, dims, preferred_element_type=F32)


def neighbours(regions, owners):
    far = owners // 4
    return [(1, 0), (-1, 0), (0, 1), (0, -1), (0, far), (0, -far)]


def face_moves(regions, owners, my_r, my_s, backward):
    sign = -1 if backward else 1
    for k, (dr, ds) in enumerate(neighbours(regions, owners)):
        to_r, to_s = my_r + sign * dr, my_s + sign * ds
        from_r, from_s = my_r - sign * dr, my_s - sign * ds
        can_send = (to_r >= 0) & (to_r < regions) & (to_s >= 0) & (to_s < owners)
        can_take = (from_r >= 0) & (from_r < regions) & (from_s >= 0) & (from_s < owners)
        yield k, (to_r, to_s), can_send, can_take


def send_faces(regions, owners, my_r, my_s, backward, src, dst, send_sem, recv_sem):
    for k, target, can_send, can_take in face_moves(regions, owners, my_r, my_s, backward):
        copy = pltpu.make_async_remote_copy(
            src_ref=src.at[k], dst_ref=dst.at[k], send_sem=send_sem.at[k],
            recv_sem=recv_sem.at[k], device_id=target, device_id_type=MESH)

        @pl.when(can_send)
        def _():
            copy.start()


def wait_faces(regions, owners, my_r, my_s, backward, src, dst, send_sem, recv_sem):
    for k, target, can_send, can_take in face_moves(regions, owners, my_r, my_s, backward):
        copy = pltpu.make_async_remote_copy(
            src_ref=src.at[k], dst_ref=dst.at[k], send_sem=send_sem.at[k],
            recv_sem=recv_sem.at[k], device_id=target, device_id_type=MESH)

        @pl.when(can_send)
        def _():
            copy.wait_send()

        @pl.when(can_take)
        def _():
            copy.wait_recv()


def block_copy(my_r, peer, pair, take, land, src, dst, send_sem, recv_sem):
    return pltpu.make_async_remote_copy(
        src_ref=src.at[pl.ds(take * pair, pair)], dst_ref=dst.at[pl.ds(land * pair, pair)],
        send_sem=send_sem, recv_sem=recv_sem, device_id=(my_r, peer),
        device_id_type=MESH)


def peer_order(owners):
    rows = owners // 8
    if rows < 4:
        return [(0, n // 2, n % 2) for n in range(1, owners)]
    far = [(2, 2), (2, 1), (1, 2), (2, 3), (3, 2), (1, 1), (3, 3), (1, 3), (3, 1), (2, 0), (0, 2),
           (1, 0), (0, 3), (3, 0), (0, 1)]
    return [(a, b, c) for a, b in far for c in (0, 1)] + [(0, 0, 1)]


def start_blocks(owners, my_r, my_s, pair, first, end, src, dst, send_sem, recv_sem):
    rows, line = max(1, owners // 8), min(4, owners // 2)
    z, y, core = my_s // (2 * line), lax.rem(my_s // 2, line), lax.rem(my_s, 2)
    for dz, dy, dc in peer_order(owners)[first:end]:
        peer = (lax.rem(z + dz, rows) * line + lax.rem(y + dy, line)) * 2 + lax.rem(core + dc, 2)
        block_copy(my_r, peer, pair, peer, my_s, src, dst, send_sem, recv_sem).start()


def wait_blocks(owners, my_r, my_s, pair, src, dst, send_sem, recv_sem):
    count = (owners - 1) * pair
    copy = pltpu.make_async_remote_copy(
        src_ref=src.at[pl.ds(0, count)], dst_ref=dst.at[pl.ds(0, count)], send_sem=send_sem,
        recv_sem=recv_sem, device_id=(my_r, lax.rem(my_s + 1, owners)), device_id_type=MESH)
    copy.wait_send()
    copy.wait_recv()


def silu_parts(v):
    s = 1.0 / (1.0 + jnp.exp(-v))
    return v * s, s * (1.0 + v * (1.0 - s))


def place(w_ref, base, q_in, q_out, block):
    w_ref[base + q_in * 64:base + q_in * 64 + 64, q_out * 64:q_out * 64 + 64] = block


SWAP = (0, 2, 1, 3)


def fill_weights(fine_ref, w_ref, wt_ref):
    w_ref[...] = jnp.zeros_like(w_ref)
    wt_ref[...] = jnp.zeros_like(wt_ref)
    same = [(q, q) for q in range(4)]
    up_j = [(0, 2), (1, 3)]
    down_j = [(2, 0), (3, 1)]
    up_k = [(0, 1), (2, 3)]
    down_k = [(1, 0), (3, 2)]
    plan = [
        (0, 0, 0, same), (1, 1, 2, same), (2, 2, 1, same),
        (3, 0, 0, up_j), (3, 3, 3, down_j), (4, 0, 0, down_j), (4, 3, 3, up_j),
        (5, 0, 0, up_k), (5, 4, 4, down_k), (6, 0, 0, down_k), (6, 4, 4, up_k),
    ]
    for tap, fwd, bwd, pairs in plan:
        w = fine_ref[tap]
        wt = w.astype(F32).T.astype(BF)
        for q_in, q_out in pairs:
            place(w_ref, fwd * 256, SWAP[q_in] if fwd == 4 else q_in, q_out, w)
            place(wt_ref, bwd * 256, SWAP[q_out] if bwd == 4 else q_out, q_in, wt)
    return plan


def signal_peers(regions, owners, my_r, my_s):
    barrier = pltpu.get_barrier_semaphore()

    def greet(step, carry):
        peer = lax.rem(my_s + step, owners)
        pl.semaphore_signal(barrier, inc=1, device_id=(my_r, peer), device_id_type=MESH)
        return carry

    lax.fori_loop(1, owners, greet, 0)

    core = lax.rem(my_s, 2)

    def greet_far(place_, carry):
        for step in range(1, regions):
            far_r = lax.rem(my_r + step, regions)
            pl.semaphore_signal(barrier, inc=1, device_id=(far_r, 2 * place_ + core),
                                device_id_type=MESH)
        return carry

    lax.fori_loop(0, owners // 2, greet_far, 0)


def wait_peers(regions, owners):
    barrier = pltpu.get_barrier_semaphore()
    pl.semaphore_wait(barrier, owners - 1 + (regions - 1) * (owners // 2))


def row_roll(v, by):
    return pltpu.roll(v, by % v.shape[0], 0)


def pieces8(v, start, step, count):
    return jnp.concatenate([v[start + n * step:start + n * step + 8] for n in range(count)], axis=0)


def main_kernel(regions, owners, scale_fine, scale_coarse,
                code_ref, slot_ref, req_ref, po_ref,
                feat_hbm, cot_hbm, order_t_hbm, order_hbm, face_ref, fine_ref, down_ref,
                coarse_ref,
                grad_ref, blocks_out, total_ref,
                feat, cot, order_t, order, x_ref, xk_ref, table, out_face, in_face, cots,
                got_cots, w_ref, wt_ref, taps_ref, act_ref, gh_ref, red_ref, cg_ref, ch_ref,
                co_ref, co_slots, slope_ref, cslope_ref, gin_ref, plane_ref, back_face, ans_ref,
                chain, halo_scr, g_scr,
                grads, pair_got, half_sum, part_p, mine, lists_v, lists,
                load, lsem, fsend, frecv, hsend, hrecv, osem, bsem, csem, rsem):
    my_r = lax.axis_index("region")
    my_s = lax.axis_index("space")
    bricks = feat.shape[0]
    face_total = table.shape[0]
    slots = cots.shape[0]
    pair = slots // owners
    groups = bricks // GROUP
    wide_rows = GROUP * ROWS
    half_rows = GROUP * 64
    loads = [pltpu.make_async_copy(src, dst, load.at[n]) for n, (src, dst) in enumerate(
        [(feat_hbm, feat), (order_t_hbm, order_t), (cot_hbm, cot), (order_hbm, order)])]
    for copy in loads:
        copy.start()
    signal_peers(regions, owners, my_r, my_s)
    def turn(g, carry):
        block = feat[pl.ds(g * GROUP, GROUP)].reshape(half_rows, 512)
        moved = dot(block, order_t[...]).astype(BF)
        for n in range(GROUP):
            b = g * GROUP + n
            row = pl.multiple_of(b * ROWS, ROWS)
            part = moved[n * 64:(n + 1) * 64]
            q = [part[:, m * 128:(m + 1) * 128] for m in range(4)]
            x = jnp.concatenate(q, axis=0).T
            x_ref[pl.ds(row, ROWS), :] = x
            xk = jnp.concatenate([q[m] for m in SWAP], axis=0).T
            xk_ref[pl.ds(row, ROWS), :] = xk
            fj = dot(face_ref[0:64], x).astype(BF)
            fk = dot(face_ref[64:128], xk).astype(BF)
            base = b * 6
            table[base] = jnp.concatenate([x[0:16, 0:128], x[0:16, 128:256]], axis=0)
            table[base + 1] = jnp.concatenate([x[112:128, 0:128], x[112:128, 128:256]], axis=0)
            table[base + 2] = fj[0:32, 0:128]
            table[base + 3] = fj[32:64, 128:256]
            table[base + 4] = fk[0:32, 0:128]
            table[base + 5] = fk[32:64, 128:256]
        return carry

    def gather_cot(s, carry):
        cots[s] = cot[jnp.maximum(po_ref[s], 0)]
        return carry

    loads[0].wait()
    loads[1].wait()
    lax.fori_loop(0, groups // 2, turn, 0)
    loads[2].wait()
    lax.fori_loop(0, slots, gather_cot, 0, unroll=8)
    wait_peers(regions, owners)
    early = owners // 8
    start_blocks(owners, my_r, my_s, pair, 0, early, cots, got_cots, bsem.at[0], bsem.at[1])
    lax.fori_loop(groups // 2, groups, turn, 0)
    for s in range(24):
        out_face[s // 4, s % 4] = table[jnp.maximum(req_ref[s], 0)]
    send_faces(regions, owners, my_r, my_s, False, out_face, in_face, fsend, frecv)
    start_blocks(owners, my_r, my_s, pair, early, owners - 1, cots, got_cots, bsem.at[0], bsem.at[1])

    none = face_total + 24
    lanes = lax.broadcasted_iota(jnp.int32, (8, 128), 1)
    child = jnp.zeros((8, 128), jnp.int32)
    for b in range(bricks):
        child = jnp.where(lanes == slot_ref[b], b, child)

    def enter(n, target, carry):
        targets, last = carry
        return jnp.where(lanes == n, target, targets), jnp.where(lanes == target, n, last)

    def own_entry(b, carry):
        plane, state = carry[0], carry[1:]
        for d in range(6):
            code = code_ref[d, b]
            plane = jnp.where(lanes == code - face_total, b * 6 + d, plane)
            state = enter(b * 6 + d, jnp.where(code < face_total, code, -1), state)
        return (plane,) + state

    plane, targets, last = lax.fori_loop(
        0, bricks, own_entry,
        (jnp.zeros((8, 128), jnp.int32), jnp.full((8, 128), -2, jnp.int32),
         jnp.full((8, 128), none, jnp.int32)), unroll=2)
    for n in range(24):
        targets, last = enter(face_total + n, req_ref[n], (targets, last))

    def link(n, target, prev):
        return jnp.where(targets == target, jnp.where(lanes > n, n, prev), prev)

    def own_link(b, prev):
        for d in range(6):
            code = code_ref[d, b]
            prev = link(b * 6 + d, jnp.where(code < face_total, code, -1), prev)
        return prev

    prev = lax.fori_loop(0, bricks, own_link, jnp.full((8, 128), none, jnp.int32), unroll=2)
    for n in range(24):
        prev = link(face_total + n, req_ref[n], prev)
    lists_v[...] = jnp.concatenate([child[0:1], plane[0:1], prev[0:1], last[0:1], child[0:4]], axis=0)
    move = pltpu.make_async_copy(lists_v, lists, lsem)
    move.start()
    move.wait()
    plan = fill_weights(fine_ref, w_ref, wt_ref)
    wait_faces(regions, owners, my_r, my_s, False, out_face, in_face, fsend, frecv)

    row8 = lax.broadcasted_iota(jnp.int32, (ROWS, 128), 0)
    first_j = lax.rem(row8, 16) < 4
    last_j = lax.rem(row8, 16) >= 12
    first_k = lax.rem(row8, 4) == 0
    last_k = lax.rem(row8, 4) == 3
    low4 = lax.rem(lax.broadcasted_iota(jnp.int32, (32, 128), 0), 8) < 4

    def halo(b, d):
        code = code_ref[d, b]
        own = table[jnp.clip(code, 0, face_total - 1)]
        slot = jnp.clip(code - face_total, 0, 23)
        got = in_face[slot // 4, lax.rem(slot, 4)]
        picked = jnp.where(code >= face_total, got, own)
        return jnp.where(code >= 0, picked, jnp.zeros_like(picked))

    def spread_j(slab, to_last):
        if to_last:
            even, odd = row_roll(slab, 4), slab
        else:
            even, odd = slab, row_roll(slab, -4)
        rows = []
        for i in range(8):
            piece = (even if i % 2 == 0 else odd)[(i // 2) * 8:(i // 2) * 8 + 8]
            rows += [piece, piece]
        return jnp.concatenate(rows, axis=0)

    def pick_j(values, from_last):
        if from_last:
            return jnp.where(low4, row_roll(pieces8(values, 8, 32, 4), -4),
                             pieces8(values, 24, 32, 4))
        return jnp.where(low4, pieces8(values, 0, 32, 4),
                         row_roll(pieces8(values, 16, 32, 4), 4))

    def forward_taps(g, n):
        b = g * GROUP + n
        row = pl.multiple_of(pl.multiple_of(g * wide_rows, wide_rows) + n * ROWS, ROWS)
        x = x_ref[pl.ds(row, ROWS), :]
        xk = xk_ref[pl.ds(row, ROWS), :].astype(F32)
        x32 = x.astype(F32)
        h = [halo(b, d) for d in range(6)]
        halo_scr[n, pl.ds(3, 32, stride=4), :] = h[5].astype(F32)
        halo_scr[n, pl.ds(0, 32, stride=4), :] = h[4].astype(F32)
        edge = halo_scr[n]
        out = pl.ds(row, ROWS)
        taps_ref[out, 0:256] = x
        taps_ref[out, 256:512] = jnp.concatenate(
            [jnp.concatenate([h[0][0:16], h[0][16:32]], axis=1), x[0:112]], axis=0)
        taps_ref[out, 512:768] = jnp.concatenate(
            [x[16:128], jnp.concatenate([h[1][0:16], h[1][16:32]], axis=1)], axis=0)
        taps_ref[out, 768:896] = jnp.where(
            last_j, spread_j(h[3].astype(F32), True), row_roll(x32[:, 0:128], -4)).astype(BF)
        taps_ref[out, 896:1024] = jnp.where(
            first_j, spread_j(h[2].astype(F32), False), row_roll(x32[:, 128:256], 4)).astype(BF)
        taps_ref[out, 1024:1152] = jnp.where(
            last_k, edge, row_roll(xk[:, 0:128], -1)).astype(BF)
        taps_ref[out, 1152:1280] = jnp.where(
            first_k, edge, row_roll(xk[:, 128:256], 1)).astype(BF)

    def forward(g, carry):
        row = pl.multiple_of(g * wide_rows, wide_rows)
        half = pl.multiple_of(g * half_rows, half_rows)
        forward_taps(g, 0)
        for n in range(GROUP):
            if n + 1 < GROUP:
                forward_taps(g, n + 1)
            part = pl.ds(pl.multiple_of(row + n * ROWS, ROWS), ROWS)
            hidden = dot(taps_ref[part, :], w_ref[...])
            act, slope = silu_parts(hidden)
            slope_ref[part, :] = slope
            act = act.astype(BF)
            dst = pl.ds(pl.multiple_of(half + n * 64, 64), 64)
            act_ref[dst, 0:256] = jnp.concatenate(
                [act[32 * m:32 * m + 16] for m in range(4)], axis=0)
            act_ref[dst, 256:512] = jnp.concatenate(
                [act[32 * m + 16:32 * m + 32] for m in range(4)], axis=0)
        out = pl.ds(half, half_rows)
        reduced = dot(act_ref[out, :], down_ref[...]).astype(BF)
        red_ref[out, :] = reduced
        c_out, c_slope = silu_parts(dot(reduced, coarse_ref[...]))
        co_ref[pl.ds(g * GROUP, GROUP)] = c_out.astype(BF).reshape(GROUP, 64, 128)
        cslope_ref[out, :] = c_slope
        return carry

    lax.fori_loop(0, groups, forward, 0)

    def gather_out(s, carry):
        co_slots[s] = co_ref[lists[0, s]]
        return carry

    lax.fori_loop(0, slots, gather_out, 0, unroll=8)
    wait_blocks(owners, my_r, my_s, pair, cots, got_cots, bsem.at[0], bsem.at[1])
    for u in range(pair):
        got_cots[my_s * pair + u] = cots[my_s * pair + u]
    cuts = (0, owners // 2, owners - 1)

    def send_out(n):
        start_blocks(owners, my_r, my_s, pair, cuts[n], cuts[n + 1], co_slots, blocks_out,
                     csem.at[0], csem.at[1])

    send_out(0)
    keep = pltpu.make_async_copy(co_slots.at[pl.ds(my_s * pair, pair)],
                                 blocks_out.at[pl.ds(my_s * pair, pair)], osem)
    keep.start()

    def coarse_back(g, carry):
        row = pl.multiple_of(g * wide_rows, wide_rows)
        half = pl.multiple_of(g * half_rows, half_rows)
        out = pl.ds(half, half_rows)
        cot_rows = jnp.concatenate(
            [got_cots[slot_ref[g * GROUP + n]] for n in range(GROUP)], axis=0).astype(F32)
        c_grad = (cot_rows * cslope_ref[out, :]).astype(BF)
        cg_ref[out, :] = c_grad
        child = dot(c_grad, coarse_ref[...], NT).astype(BF)
        ch_ref[out, :] = child
        ga = dot(child, down_ref[...], NT)
        for n in range(GROUP * 4):
            for a in range(2):
                part = pl.ds(pl.multiple_of(row + n * 32 + a * 16, 16), 16)
                gh_ref[part, :] = (ga[16 * n:16 * n + 16, a * 256:a * 256 + 256]
                                   * slope_ref[part, :]).astype(BF)
        return carry

    lax.fori_loop(0, groups, coarse_back, 0)

    def put_rows(start, value):
        count = value.shape[0] // 8
        grads[start // 8:start // 8 + count] = value.reshape(count, 8, 128)

    turned = dot(gh_ref[...], taps_ref[...], TN) * scale_fine
    sums = [None] * 7
    for tap, fwd, bwd, pairs in plan:
        for q_in, q_out in pairs:
            spot = fwd * 256 + (SWAP[q_in] if fwd == 4 else q_in) * 64
            part = turned[q_out * 64:q_out * 64 + 64, spot:spot + 64]
            sums[tap] = part if sums[tap] is None else sums[tap] + part
    sums.append(jnp.zeros_like(sums[0]))
    for n in range(4):
        put_rows(n * 64, jnp.concatenate([sums[2 * n], sums[2 * n + 1]], axis=0).T)
    put_rows(256, dot(act_ref[...], ch_ref[...], TN) * scale_fine)
    put_rows(768, dot(red_ref[...], cg_ref[...], TN) * scale_coarse)
    phases = sum_phases(regions, owners, my_r, my_s, grads, pair_got, half_sum, part_p, mine,
                        total_ref, rsem)
    next(phases)

    def backward(g):
        row = g * wide_rows
        bwd, f0, f1, fj, fk = [], [], [], [], []
        for n in range(GROUP):
            gh = gh_ref[row + n * ROWS:row + (n + 1) * ROWS, :]
            g32 = gh.astype(F32)
            low, high = g32[:, 0:128], g32[:, 128:256]
            zero = jnp.zeros_like(low)
            swapped = jnp.concatenate([gh[:, 0:64], gh[:, 128:192], gh[:, 64:128], gh[:, 192:256]],
                                      axis=1).astype(F32)
            k_low, k_high = swapped[:, 0:128], swapped[:, 128:256]
            blank = jnp.zeros((16, LANES), BF)
            bwd.append(jnp.concatenate([
                gh,
                jnp.concatenate([blank, gh[0:112]], axis=0),
                jnp.concatenate([gh[16:128], blank], axis=0),
                jnp.where(last_j, zero, row_roll(low, -4)).astype(BF),
                jnp.where(first_j, zero, row_roll(high, 4)).astype(BF),
                jnp.where(last_k, zero, row_roll(k_low, -1)).astype(BF),
                jnp.where(first_k, zero, row_roll(k_high, 1)).astype(BF)], axis=1))
            f0.append(gh[0:16])
            f1.append(gh[112:128])
            fj.append(jnp.concatenate([pick_j(low, False), pick_j(high, True)], axis=1).astype(BF))
            g_scr[2 * n] = k_low
            g_scr[2 * n + 1] = k_high
            fk.append(jnp.concatenate([g_scr[2 * n, pl.ds(0, 32, stride=4), :],
                                       g_scr[2 * n + 1, pl.ds(3, 32, stride=4), :]],
                                      axis=1).astype(BF))
        for n in range(GROUP):
            gin_ref[row + n * ROWS:row + (n + 1) * ROWS, :] = dot(bwd[n], wt_ref[...])
        p0 = dot(jnp.concatenate(f0, axis=0), wt_ref[512:768, :]).astype(BF)
        p1 = dot(jnp.concatenate(f1, axis=0), wt_ref[256:512, :]).astype(BF)
        pj = dot(jnp.concatenate(fj, axis=0), wt_ref[768:1024, :]).astype(BF)
        pk = dot(jnp.concatenate(fk, axis=0), wt_ref[1024:1280, :]).astype(BF)
        for n in range(GROUP):
            base = (g * GROUP + n) * 6
            a, c = p0[n * 16:n * 16 + 16], p1[n * 16:n * 16 + 16]
            j, k = pj[n * 32:n * 32 + 32], pk[n * 32:n * 32 + 32]
            plane_ref[base] = jnp.concatenate([a[:, 0:128], a[:, 128:256]], axis=0)
            plane_ref[base + 1] = jnp.concatenate([c[:, 0:128], c[:, 128:256]], axis=0)
            plane_ref[base + 2] = j[:, 128:256]
            plane_ref[base + 3] = j[:, 0:128]
            plane_ref[base + 4] = jnp.concatenate([k[:, 64:128], k[:, 192:256]], axis=1)
            plane_ref[base + 5] = jnp.concatenate([k[:, 0:64], k[:, 128:192]], axis=1)

    for g in range(groups):
        backward(g)
        if g == 0:
            next(phases)
            send_out(1)
    for s in range(24):
        back_face[s // 4, s % 4] = plane_ref[lists[1, s]]
    chain[face_total + 24] = jnp.zeros((32, 128), F32)
    send_faces(regions, owners, my_r, my_s, True, back_face, ans_ref, hsend, hrecv)

    def add_plane(n, carry):
        chain[n] = chain[lists[2, n]] + plane_ref[n].astype(F32)
        return carry

    lax.fori_loop(0, face_total, add_plane, 0, unroll=4)
    next(phases)
    wait_faces(regions, owners, my_r, my_s, True, back_face, ans_ref, hsend, hrecv)
    for s in range(24):
        chain[face_total + s] = (chain[lists[2, face_total + s]]
                                 + ans_ref[s // 4, s % 4].astype(F32))
    loads[3].wait()
    lane = lax.broadcasted_iota(jnp.int32, (ROWS, LANES), 1)
    edge_k = lax.rem(lax.broadcasted_iota(jnp.int32, (ROWS, LANES), 0), 4) == jnp.where(
        lax.rem(lane, 128) < 64, 0, 3)

    def finish(g, carry):
        wides = []
        for n in range(GROUP):
            b = g * GROUP + n
            f = [chain[lists[3, b * 6 + d]] for d in range(6)]
            zero = jnp.zeros((ROWS, 128), F32)
            add_j = jnp.concatenate([jnp.where(first_j, spread_j(f[2], False), zero),
                                     jnp.where(last_j, spread_j(f[3], True), zero)], axis=1)
            for side in range(2):
                k0 = f[4] if side == 0 else pltpu.roll(f[4], 64, 1)
                k3 = f[5] if side == 1 else pltpu.roll(f[5], 64, 1)
                g_scr[2 * n + side, pl.ds(0, 32, stride=4), :] = k0
                g_scr[2 * n + side, pl.ds(3, 32, stride=4), :] = k3
            add_k = jnp.where(edge_k, jnp.concatenate([g_scr[2 * n], g_scr[2 * n + 1]], axis=1),
                              jnp.zeros((ROWS, LANES), F32))
            total = gin_ref[pl.ds(pl.multiple_of(b * ROWS, ROWS), ROWS), :] + add_j + add_k
            low = jnp.concatenate([f[0][0:16], f[0][16:32]], axis=1)
            high = jnp.concatenate([f[1][0:16], f[1][16:32]], axis=1)
            total = jnp.concatenate(
                [total[0:16] + low, total[16:112], total[112:128] + high], axis=0).astype(BF)
            flipped = total.T
            wides.append(jnp.concatenate([flipped[q * 64:q * 64 + 64] for q in range(4)], axis=1))
        out = dot(jnp.concatenate(wides, axis=0), order[...]).astype(BF)
        feat[pl.ds(g * GROUP, GROUP)] = out.reshape(GROUP, 64, 512)
        return carry

    lax.fori_loop(0, groups, finish, 0)
    leave = pltpu.make_async_copy(feat, grad_ref, lsem)
    leave.start()
    for _ in phases:
        pass
    leave.wait()
    keep.wait()
    wait_blocks(owners, my_r, my_s, pair, co_slots, blocks_out, csem.at[0], csem.at[1])


def sum_phases(regions, owners, my_r, my_s, grads, pair_got, half_sum, part_p, mine, total_ref, sem):
    core = lax.rem(my_s, 2)
    other = 1 - core
    width = owners // 2
    chips = regions * width
    chip = my_r * width + my_s // 2
    half = pair_got.shape[0]
    unit = mine.shape[0]
    used = half // unit
    partner = (my_r, my_s + 1 - 2 * core)

    def remote(src, dst, n, target):
        return pltpu.make_async_remote_copy(
            src_ref=src, dst_ref=dst, send_sem=sem.at[2 * n], recv_sem=sem.at[2 * n + 1],
            device_id=target, device_id_type=MESH)

    def spot(peer):
        return (peer // width, 2 * lax.rem(peer, width) + core)

    near = spot(lax.rem(chip + 1, chips))

    def sized(ref, count, n):
        part = ref.at[pl.ds(0, count * unit)]
        return remote(part, part, n, near)

    swap = remote(grads.at[pl.ds(other * half, half)], pair_got, 0, partner)
    swap.start()
    yield
    swap.wait()
    half_sum[...] = grads[pl.ds(core * half, half)] + pair_got[...]
    owns = chip < used
    mine_at = jnp.minimum(chip, used - 1) * unit

    def start_sum(n, carry):
        peer = lax.rem(chip + n, chips)

        @pl.when(peer < used)
        def _():
            remote(half_sum.at[pl.ds(jnp.minimum(peer, used - 1) * unit, unit)],
                   part_p.at[pl.ds(chip * unit, unit)], 1, spot(peer)).start()
        return carry

    lax.fori_loop(1, chips, start_sum, 0)
    yield
    out_at = core * half + mine_at

    @pl.when(owns)
    def _():
        sized(half_sum, used - 1, 1).wait_send()
        sized(part_p, chips - 1, 1).wait_recv()
        part_p[pl.ds(chip * unit, unit)] = half_sum[pl.ds(mine_at, unit)]
        run = part_p[0:unit]
        for n in range(1, chips):
            run = run + part_p[n * unit:n * unit + unit]
        mine[...] = run.astype(BF)
        total_ref[pl.ds(out_at, unit)] = run.astype(BF)

        def start_share(n, carry):
            remote(mine, total_ref.at[pl.ds(out_at, unit)], 2,
                   spot(lax.rem(chip + n, chips))).start()
            return carry

        lax.fori_loop(1, chips, start_share, 0)

    if used < chips:
        @pl.when(jnp.logical_not(owns))
        def _():
            sized(half_sum, used, 1).wait_send()
    yield

    @pl.when(owns)
    def _():
        sized(total_ref, chips - 1, 2).wait_send()
        sized(total_ref, used - 1, 2).wait_recv()

    if used < chips:
        @pl.when(jnp.logical_not(owns))
        def _():
            sized(total_ref, used, 2).wait_recv()

    own = pl.ds(core * half, half)
    remote(total_ref.at[own], total_ref.at[own], 3, partner).start()
    yield
    last = remote(total_ref.at[own], total_ref.at[pl.ds(other * half, half)], 3, partner)
    last.wait_send()
    last.wait_recv()


def result_kernel(slot_ref, made_ref, arr_ref, total_ref, grad_ref, out_ref, fine_ref, down_ref,
                  coarse_ref):
    out_ref[...] = jnp.zeros_like(out_ref)

    def put_block(s, carry):
        spot = slot_ref[s]

        @pl.when(spot >= 0)
        def _():
            out_ref[spot] = arr_ref[s]
        return carry

    lax.fori_loop(0, arr_ref.shape[0], put_block, 0, unroll=4)
    grad_ref[...] = made_ref[...]
    for tap in range(7):
        rows = total_ref[tap // 2 * 8:tap // 2 * 8 + 8].astype(F32).reshape(64, 128)
        fine_ref[tap] = rows[:, tap % 2 * 64:tap % 2 * 64 + 64]
    down_ref[...] = total_ref[32:96].astype(F32).reshape(512, 128)
    coarse_ref[...] = total_ref[96:112].astype(F32).reshape(128, 128)


def on_device(features, fine_weight, down_weight, coarse_weight, cotangent, face_source,
              face_requests, child_slot, parent_octant):
    regions = lax.axis_size("region")
    owners = lax.axis_size("space")
    count = regions * owners
    bricks, channels, volume = features.shape
    faces = bricks * 6
    parents, _, wide = cotangent.shape
    octant = volume // 8
    slots = parent_octant.shape[1]
    shape = jax.ShapeDtypeStruct
    vm = pltpu.VMEM
    dma = pltpu.SemaphoreType.DMA
    requests = face_requests.reshape(24)
    targets = parent_octant.reshape(slots)
    scale_fine = 1.0 / math.sqrt(bricks * count * volume)
    scale_coarse = 1.0 / math.sqrt(parents * count * volume)
    chips = count // 2
    unit = max(1, 56 // chips)
    big = bricks * ROWS
    small = bricks * octant
    block = (slots, octant, wide)
    faces4 = (6, 4, 32, 128)
    made, arrived, totals = pl.pallas_call(
        functools.partial(main_kernel, regions, owners, scale_fine, scale_coarse),
        out_shape=(shape((bricks, channels, volume), BF), shape(block, BF),
                   shape((112, 8, 128), BF)),
        in_specs=[SMEM_SPEC] * 4 + [ANY_SPEC] * 4 + [VMEM_SPEC] * 4,
        out_specs=(ANY_SPEC, ANY_SPEC, VMEM_SPEC),
        scratch_shapes=[
            vm((bricks, channels, volume), BF), vm(block, BF), vm((512, 512), BF),
            vm((512, 512), BF), vm((big, LANES), BF), vm((big, LANES), BF),
            vm((faces, 32, 128), BF), vm(faces4, BF), vm(faces4, BF), vm(block, BF), vm(block, BF),
            vm((1280, LANES), BF), vm((1280, LANES), BF), vm((big, 1280), BF),
            vm((small, 512), BF), vm((big, LANES), BF), vm((small, wide), BF),
            vm((small, wide), BF), vm((small, wide), BF),
            vm((bricks, octant, wide), BF), vm(block, BF), vm((big, LANES), F32),
            vm((small, wide), F32), vm((big, LANES), F32), vm((faces, 32, 128), BF),
            vm(faces4, BF), vm(faces4, BF), vm((faces + 25, 32, 128), F32),
            vm((GROUP, ROWS, 128), F32), vm((2 * GROUP, ROWS, 128), F32),
            vm((112, 8, 128), F32), vm((56, 8, 128), F32), vm((56, 8, 128), F32),
            vm((chips * unit, 8, 128), F32),
            vm((unit, 8, 128), BF), vm((8, 128), jnp.int32), pltpu.SMEM((8, 128), jnp.int32),
            dma((4,)), dma, dma((6,)), dma((6,)), dma((6,)), dma((6,)), dma, dma((2,)), dma((2,)),
            dma((8,))],
        compiler_params=pltpu.CompilerParams(
            collective_id=0, has_side_effects=True, vmem_limit_bytes=60 * 2**20),
        name="main",
    )(face_source.T, child_slot, requests, targets, features,
      cotangent.reshape(parents * 8, octant, wide), jnp.asarray(ORDER_T), jnp.asarray(ORDER),
      jnp.asarray(FACE), fine_weight, down_weight.reshape(8 * channels, wide), coarse_weight)
    grad_in, coarse_out, fine, down, coarse = pl.pallas_call(
        result_kernel,
        out_shape=(shape((bricks, channels, volume), BF), shape((parents * 8, octant, wide), BF),
                   shape((7, channels, channels), F32), shape((8 * channels, wide), F32),
                   shape((wide, wide), F32)),
        in_specs=[SMEM_SPEC] + [VMEM_SPEC] * 3,
        out_specs=(VMEM_SPEC,) * 5,
        compiler_params=pltpu.CompilerParams(vmem_limit_bytes=60 * 2**20),
        name="result",
    )(targets, made, arrived, totals)
    return (grad_in, coarse_out.reshape(parents, volume, wide), fine,
            down.reshape(8, channels, wide), coarse)


def solution(mesh):
    both = ("region", "space")
    return jax.shard_map(
        on_device,
        mesh=mesh,
        in_specs=(P(both, None, None), P(), P(), P(), P(both, None, None), P(both, None),
                  P(both, None), P(both), P(both, None)),
        out_specs=(P(both, None, None), P(both, None, None), P(), P(), P()),
        check_vma=False,
    )
```

```python
import functools
import math

import jax
import jax.numpy as jnp
import numpy as np
from jax import lax
from jax.experimental import pallas as pl
from jax.experimental.pallas import tpu as pltpu
from jax.sharding import PartitionSpec as P

EDGE = 8
BF = jnp.bfloat16
F32 = jnp.float32
MESH = pl.DeviceIdType.MESH
NT = (((1,), (1,)), ((), ()))
TN = (((0,), (0,)), ((), ()))
VMEM_SPEC = pl.BlockSpec(memory_space=pltpu.VMEM)
SMEM_SPEC = pl.BlockSpec(memory_space=pltpu.SMEM)
ANY_SPEC = pl.BlockSpec(memory_space=pl.ANY)
ROWS = 128
LANES = 256
GROUP = 4


def row_of(i, j, k):
    return i * 16 + j * 4 + k


def make_tables():
    order = np.zeros((512, 512), np.float32)
    for i in range(8):
        for j in range(8):
            for k in range(8):
                q = (j % 2) * 2 + k % 2
                order[q * 128 + row_of(i, j // 2, k // 2), i * 64 + j * 8 + k] = 1
    face = np.zeros((128, 128), np.float32)
    for i in range(8):
        for m in range(4):
            face[i * 4 + m, row_of(i, 0, m)] = 1
            face[32 + i * 4 + m, row_of(i, 3, m)] = 1
            face[64 + i * 4 + m, row_of(i, m, 0)] = 1
            face[96 + i * 4 + m, row_of(i, m, 3)] = 1
    cast = lambda a: np.asarray(a, dtype=BF)
    return cast(order), cast(order.T), cast(face)


ORDER, ORDER_T, FACE = make_tables()


def dot(a, b, dims=(((1,), (0,)), ((), ()))):
    return lax.dot_general(a, b, dims, preferred_element_type=F32)


def neighbours(regions, owners):
    far = owners // 4
    return [(1, 0), (-1, 0), (0, 1), (0, -1), (0, far), (0, -far)]


def face_moves(regions, owners, my_r, my_s, backward):
    sign = -1 if backward else 1
    for k, (dr, ds) in enumerate(neighbours(regions, owners)):
        to_r, to_s = my_r + sign * dr, my_s + sign * ds
        from_r, from_s = my_r - sign * dr, my_s - sign * ds
        can_send = (to_r >= 0) & (to_r < regions) & (to_s >= 0) & (to_s < owners)
        can_take = (from_r >= 0) & (from_r < regions) & (from_s >= 0) & (from_s < owners)
        yield k, (to_r, to_s), can_send, can_take


def send_faces(regions, owners, my_r, my_s, backward, src, dst, send_sem, recv_sem):
    for k, target, can_send, can_take in face_moves(regions, owners, my_r, my_s, backward):
        copy = pltpu.make_async_remote_copy(
            src_ref=src.at[k], dst_ref=dst.at[k], send_sem=send_sem.at[k],
            recv_sem=recv_sem.at[k], device_id=target, device_id_type=MESH)

        @pl.when(can_send)
        def _():
            copy.start()


def wait_faces(regions, owners, my_r, my_s, backward, src, dst, send_sem, recv_sem):
    for k, target, can_send, can_take in face_moves(regions, owners, my_r, my_s, backward):
        copy = pltpu.make_async_remote_copy(
            src_ref=src.at[k], dst_ref=dst.at[k], send_sem=send_sem.at[k],
            recv_sem=recv_sem.at[k], device_id=target, device_id_type=MESH)

        @pl.when(can_send)
        def _():
            copy.wait_send()

        @pl.when(can_take)
        def _():
            copy.wait_recv()


def block_copy(my_r, peer, pair, take, land, src, dst, send_sem, recv_sem):
    return pltpu.make_async_remote_copy(
        src_ref=src.at[pl.ds(take * pair, pair)], dst_ref=dst.at[pl.ds(land * pair, pair)],
        send_sem=send_sem, recv_sem=recv_sem, device_id=(my_r, peer),
        device_id_type=MESH)


def peer_order(owners):
    rows = owners // 8
    if rows < 4:
        return [(0, n // 2, n % 2) for n in range(1, owners)]
    far = [(2, 2), (2, 1), (1, 2), (2, 3), (3, 2), (1, 1), (3, 3), (1, 3), (3, 1), (2, 0), (0, 2),
           (1, 0), (0, 3), (3, 0), (0, 1)]
    return [(a, b, c) for a, b in far for c in (0, 1)] + [(0, 0, 1)]


def start_blocks(owners, my_r, my_s, pair, first, end, src, dst, send_sem, recv_sem):
    rows, line = max(1, owners // 8), min(4, owners // 2)
    z, y, core = my_s // (2 * line), lax.rem(my_s // 2, line), lax.rem(my_s, 2)
    for dz, dy, dc in peer_order(owners)[first:end]:
        peer = (lax.rem(z + dz, rows) * line + lax.rem(y + dy, line)) * 2 + lax.rem(core + dc, 2)
        block_copy(my_r, peer, pair, peer, my_s, src, dst, send_sem, recv_sem).start()


def wait_blocks(owners, my_r, my_s, pair, src, dst, send_sem, recv_sem):
    count = (owners - 1) * pair
    copy = pltpu.make_async_remote_copy(
        src_ref=src.at[pl.ds(0, count)], dst_ref=dst.at[pl.ds(0, count)], send_sem=send_sem,
        recv_sem=recv_sem, device_id=(my_r, lax.rem(my_s + 1, owners)), device_id_type=MESH)
    copy.wait_send()
    copy.wait_recv()


def silu_parts(v):
    s = 1.0 / (1.0 + jnp.exp(-v))
    return v * s, s * (1.0 + v * (1.0 - s))


def place(w_ref, base, q_in, q_out, block):
    w_ref[base + q_in * 64:base + q_in * 64 + 64, q_out * 64:q_out * 64 + 64] = block


SWAP = (0, 2, 1, 3)


def fill_weights(fine_ref, w_ref, wt_ref):
    w_ref[...] = jnp.zeros_like(w_ref)
    wt_ref[...] = jnp.zeros_like(wt_ref)
    same = [(q, q) for q in range(4)]
    up_j = [(0, 2), (1, 3)]
    down_j = [(2, 0), (3, 1)]
    up_k = [(0, 1), (2, 3)]
    down_k = [(1, 0), (3, 2)]
    plan = [
        (0, 0, 0, same), (1, 1, 2, same), (2, 2, 1, same),
        (3, 0, 0, up_j), (3, 3, 3, down_j), (4, 0, 0, down_j), (4, 3, 3, up_j),
        (5, 0, 0, up_k), (5, 4, 4, down_k), (6, 0, 0, down_k), (6, 4, 4, up_k),
    ]
    for tap, fwd, bwd, pairs in plan:
        w = fine_ref[tap]
        wt = w.astype(F32).T.astype(BF)
        for q_in, q_out in pairs:
            place(w_ref, fwd * 256, SWAP[q_in] if fwd == 4 else q_in, q_out, w)
            place(wt_ref, bwd * 256, SWAP[q_out] if bwd == 4 else q_out, q_in, wt)
    return plan


def signal_peers(regions, owners, my_r, my_s):
    barrier = pltpu.get_barrier_semaphore()

    def greet(step, carry):
        peer = lax.rem(my_s + step, owners)
        pl.semaphore_signal(barrier, inc=1, device_id=(my_r, peer), device_id_type=MESH)
        return carry

    lax.fori_loop(1, owners, greet, 0)

    core = lax.rem(my_s, 2)

    def greet_far(place_, carry):
        for step in range(1, regions):
            far_r = lax.rem(my_r + step, regions)
            pl.semaphore_signal(barrier, inc=1, device_id=(far_r, 2 * place_ + core),
                                device_id_type=MESH)
        return carry

    lax.fori_loop(0, owners // 2, greet_far, 0)


def wait_peers(regions, owners):
    barrier = pltpu.get_barrier_semaphore()
    pl.semaphore_wait(barrier, owners - 1 + (regions - 1) * (owners // 2))


def row_roll(v, by):
    return pltpu.roll(v, by % v.shape[0], 0)


def pieces8(v, start, step, count):
    return jnp.concatenate([v[start + n * step:start + n * step + 8] for n in range(count)], axis=0)


def main_kernel(regions, owners, scale_fine, scale_coarse,
                code_ref, slot_ref, req_ref, po_ref,
                feat_hbm, cot_hbm, order_t_hbm, order_hbm, face_ref, fine_ref, down_ref,
                coarse_ref,
                grad_ref, blocks_out, total_ref,
                feat, cot, order_t, order, x_ref, xk_ref, table, out_face, in_face, cots,
                got_cots, w_ref, wt_ref, taps_ref, act_ref, gh_ref, red_ref, cg_ref, ch_ref,
                co_ref, co_slots, slope_ref, cslope_ref, gin_ref, plane_ref, back_face, ans_ref,
                chain, halo_scr, g_scr,
                grads, pair_got, half_sum, part_p, mine, lists_v, lists,
                load, lsem, fsend, frecv, hsend, hrecv, osem, bsem, csem, rsem):
    my_r = lax.axis_index("region")
    my_s = lax.axis_index("space")
    bricks = feat.shape[0]
    face_total = table.shape[0]
    slots = cots.shape[0]
    pair = slots // owners
    groups = bricks // GROUP
    wide_rows = GROUP * ROWS
    half_rows = GROUP * 64
    loads = [pltpu.make_async_copy(src, dst, load.at[n]) for n, (src, dst) in enumerate(
        [(feat_hbm, feat), (order_t_hbm, order_t), (cot_hbm, cot), (order_hbm, order)])]
    for copy in loads:
        copy.start()
    signal_peers(regions, owners, my_r, my_s)
    def turn(g, carry):
        block = feat[pl.ds(g * GROUP, GROUP)].reshape(half_rows, 512)
        moved = dot(block, order_t[...]).astype(BF)
        for n in range(GROUP):
            b = g * GROUP + n
            row = pl.multiple_of(b * ROWS, ROWS)
            part = moved[n * 64:(n + 1) * 64]
            q = [part[:, m * 128:(m + 1) * 128] for m in range(4)]
            x = jnp.concatenate(q, axis=0).T
            x_ref[pl.ds(row, ROWS), :] = x
            xk = jnp.concatenate([q[m] for m in SWAP], axis=0).T
            xk_ref[pl.ds(row, ROWS), :] = xk
            fj = dot(face_ref[0:64], x).astype(BF)
            fk = dot(face_ref[64:128], xk).astype(BF)
            base = b * 6
            table[base] = jnp.concatenate([x[0:16, 0:128], x[0:16, 128:256]], axis=0)
            table[base + 1] = jnp.concatenate([x[112:128, 0:128], x[112:128, 128:256]], axis=0)
            table[base + 2] = fj[0:32, 0:128]
            table[base + 3] = fj[32:64, 128:256]
            table[base + 4] = fk[0:32, 0:128]
            table[base + 5] = fk[32:64, 128:256]
        return carry

    def gather_cot(s, carry):
        cots[s] = cot[jnp.maximum(po_ref[s], 0)]
        return carry

    loads[0].wait()
    loads[1].wait()
    lax.fori_loop(0, groups // 2, turn, 0)
    loads[2].wait()
    lax.fori_loop(0, slots, gather_cot, 0, unroll=8)
    wait_peers(regions, owners)
    early = owners // 8
    start_blocks(owners, my_r, my_s, pair, 0, early, cots, got_cots, bsem.at[0], bsem.at[1])
    lax.fori_loop(groups // 2, groups, turn, 0)
    for s in range(24):
        out_face[s // 4, s % 4] = table[jnp.maximum(req_ref[s], 0)]
    send_faces(regions, owners, my_r, my_s, False, out_face, in_face, fsend, frecv)
    start_blocks(owners, my_r, my_s, pair, early, owners - 1, cots, got_cots, bsem.at[0], bsem.at[1])

    none = face_total + 24
    lanes = lax.broadcasted_iota(jnp.int32, (8, 128), 1)
    child = jnp.zeros((8, 128), jnp.int32)
    for b in range(bricks):
        child = jnp.where(lanes == slot_ref[b], b, child)

    def enter(n, target, carry):
        targets, last = carry
        return jnp.where(lanes == n, target, targets), jnp.where(lanes == target, n, last)

    def own_entry(b, carry):
        plane, state = carry[0], carry[1:]
        for d in range(6):
            code = code_ref[d, b]
            plane = jnp.where(lanes == code - face_total, b * 6 + d, plane)
            state = enter(b * 6 + d, jnp.where(code < face_total, code, -1), state)
        return (plane,) + state

    plane, targets, last = lax.fori_loop(
        0, bricks, own_entry,
        (jnp.zeros((8, 128), jnp.int32), jnp.full((8, 128), -2, jnp.int32),
         jnp.full((8, 128), none, jnp.int32)), unroll=2)
    for n in range(24):
        targets, last = enter(face_total + n, req_ref[n], (targets, last))

    def link(n, target, prev):
        return jnp.where(targets == target, jnp.where(lanes > n, n, prev), prev)

    def own_link(b, prev):
        for d in range(6):
            code = code_ref[d, b]
            prev = link(b * 6 + d, jnp.where(code < face_total, code, -1), prev)
        return prev

    prev = lax.fori_loop(0, bricks, own_link, jnp.full((8, 128), none, jnp.int32), unroll=2)
    for n in range(24):
        prev = link(face_total + n, req_ref[n], prev)
    lists_v[...] = jnp.concatenate([child[0:1], plane[0:1], prev[0:1], last[0:1], child[0:4]], axis=0)
    move = pltpu.make_async_copy(lists_v, lists, lsem)
    move.start()
    move.wait()
    plan = fill_weights(fine_ref, w_ref, wt_ref)
    wait_faces(regions, owners, my_r, my_s, False, out_face, in_face, fsend, frecv)

    row8 = lax.broadcasted_iota(jnp.int32, (ROWS, 128), 0)
    first_j = lax.rem(row8, 16) < 4
    last_j = lax.rem(row8, 16) >= 12
    first_k = lax.rem(row8, 4) == 0
    last_k = lax.rem(row8, 4) == 3
    low4 = lax.rem(lax.broadcasted_iota(jnp.int32, (32, 128), 0), 8) < 4

    def halo(b, d):
        code = code_ref[d, b]
        own = table[jnp.clip(code, 0, face_total - 1)]
        slot = jnp.clip(code - face_total, 0, 23)
        got = in_face[slot // 4, lax.rem(slot, 4)]
        picked = jnp.where(code >= face_total, got, own)
        return jnp.where(code >= 0, picked, jnp.zeros_like(picked))

    def spread_j(slab, to_last):
        if to_last:
            even, odd = row_roll(slab, 4), slab
        else:
            even, odd = slab, row_roll(slab, -4)
        rows = []
        for i in range(8):
            piece = (even if i % 2 == 0 else odd)[(i // 2) * 8:(i // 2) * 8 + 8]
            rows += [piece, piece]
        return jnp.concatenate(rows, axis=0)

    def pick_j(values, from_last):
        if from_last:
            return jnp.where(low4, row_roll(pieces8(values, 8, 32, 4), -4),
                             pieces8(values, 24, 32, 4))
        return jnp.where(low4, pieces8(values, 0, 32, 4),
                         row_roll(pieces8(values, 16, 32, 4), 4))

    def forward_taps(g, n):
        b = g * GROUP + n
        row = pl.multiple_of(pl.multiple_of(g * wide_rows, wide_rows) + n * ROWS, ROWS)
        x = x_ref[pl.ds(row, ROWS), :]
        xk = xk_ref[pl.ds(row, ROWS), :].astype(F32)
        x32 = x.astype(F32)
        h = [halo(b, d) for d in range(6)]
        halo_scr[n, pl.ds(3, 32, stride=4), :] = h[5].astype(F32)
        halo_scr[n, pl.ds(0, 32, stride=4), :] = h[4].astype(F32)
        edge = halo_scr[n]
        out = pl.ds(row, ROWS)
        taps_ref[out, 0:256] = x
        taps_ref[out, 256:512] = jnp.concatenate(
            [jnp.concatenate([h[0][0:16], h[0][16:32]], axis=1), x[0:112]], axis=0)
        taps_ref[out, 512:768] = jnp.concatenate(
            [x[16:128], jnp.concatenate([h[1][0:16], h[1][16:32]], axis=1)], axis=0)
        taps_ref[out, 768:896] = jnp.where(
            last_j, spread_j(h[3].astype(F32), True), row_roll(x32[:, 0:128], -4)).astype(BF)
        taps_ref[out, 896:1024] = jnp.where(
            first_j, spread_j(h[2].astype(F32), False), row_roll(x32[:, 128:256], 4)).astype(BF)
        taps_ref[out, 1024:1152] = jnp.where(
            last_k, edge, row_roll(xk[:, 0:128], -1)).astype(BF)
        taps_ref[out, 1152:1280] = jnp.where(
            first_k, edge, row_roll(xk[:, 128:256], 1)).astype(BF)

    def forward(g, carry):
        row = pl.multiple_of(g * wide_rows, wide_rows)
        half = pl.multiple_of(g * half_rows, half_rows)
        forward_taps(g, 0)
        for n in range(GROUP):
            if n + 1 < GROUP:
                forward_taps(g, n + 1)
            part = pl.ds(pl.multiple_of(row + n * ROWS, ROWS), ROWS)
            hidden = dot(taps_ref[part, :], w_ref[...])
            act, slope = silu_parts(hidden)
            slope_ref[part, :] = slope
            act = act.astype(BF)
            dst = pl.ds(pl.multiple_of(half + n * 64, 64), 64)
            act_ref[dst, 0:256] = jnp.concatenate(
                [act[32 * m:32 * m + 16] for m in range(4)], axis=0)
            act_ref[dst, 256:512] = jnp.concatenate(
                [act[32 * m + 16:32 * m + 32] for m in range(4)], axis=0)
        out = pl.ds(half, half_rows)
        reduced = dot(act_ref[out, :], down_ref[...]).astype(BF)
        red_ref[out, :] = reduced
        c_out, c_slope = silu_parts(dot(reduced, coarse_ref[...]))
        co_ref[pl.ds(g * GROUP, GROUP)] = c_out.astype(BF).reshape(GROUP, 64, 128)
        cslope_ref[out, :] = c_slope
        return carry

    lax.fori_loop(0, groups, forward, 0)

    def gather_out(s, carry):
        co_slots[s] = co_ref[lists[0, s]]
        return carry

    lax.fori_loop(0, slots, gather_out, 0, unroll=8)
    wait_blocks(owners, my_r, my_s, pair, cots, got_cots, bsem.at[0], bsem.at[1])
    for u in range(pair):
        got_cots[my_s * pair + u] = cots[my_s * pair + u]
    cuts = (0, owners // 4, 7 * owners // 16, owners - 1)

    def send_out(n):
        start_blocks(owners, my_r, my_s, pair, cuts[n], cuts[n + 1], co_slots, blocks_out,
                     csem.at[0], csem.at[1])

    send_out(0)
    keep = pltpu.make_async_copy(co_slots.at[pl.ds(my_s * pair, pair)],
                                 blocks_out.at[pl.ds(my_s * pair, pair)], osem)
    keep.start()

    def coarse_back(g, carry):
        row = pl.multiple_of(g * wide_rows, wide_rows)
        half = pl.multiple_of(g * half_rows, half_rows)
        out = pl.ds(half, half_rows)
        cot_rows = jnp.concatenate(
            [got_cots[slot_ref[g * GROUP + n]] for n in range(GROUP)], axis=0).astype(F32)
        c_grad = (cot_rows * cslope_ref[out, :]).astype(BF)
        cg_ref[out, :] = c_grad
        child = dot(c_grad, coarse_ref[...], NT).astype(BF)
        ch_ref[out, :] = child
        ga = dot(child, down_ref[...], NT)
        for n in range(GROUP * 4):
            for a in range(2):
                part = pl.ds(pl.multiple_of(row + n * 32 + a * 16, 16), 16)
                gh_ref[part, :] = (ga[16 * n:16 * n + 16, a * 256:a * 256 + 256]
                                   * slope_ref[part, :]).astype(BF)
        return carry

    lax.fori_loop(0, groups, coarse_back, 0)

    def put_rows(start, value):
        count = value.shape[0] // 8
        grads[start // 8:start // 8 + count] = value.reshape(count, 8, 128)

    turned = dot(gh_ref[...], taps_ref[...], TN) * scale_fine
    sums = [None] * 7
    for tap, fwd, bwd, pairs in plan:
        for q_in, q_out in pairs:
            spot = fwd * 256 + (SWAP[q_in] if fwd == 4 else q_in) * 64
            part = turned[q_out * 64:q_out * 64 + 64, spot:spot + 64]
            sums[tap] = part if sums[tap] is None else sums[tap] + part
    sums.append(jnp.zeros_like(sums[0]))
    for n in range(4):
        put_rows(n * 64, jnp.concatenate([sums[2 * n], sums[2 * n + 1]], axis=0).T)
    put_rows(256, dot(act_ref[...], ch_ref[...], TN) * scale_fine)
    put_rows(768, dot(red_ref[...], cg_ref[...], TN) * scale_coarse)
    phases = sum_phases(regions, owners, my_r, my_s, grads, pair_got, half_sum, part_p, mine,
                        total_ref, rsem)
    next(phases)

    def backward(g):
        row = g * wide_rows
        bwd, f0, f1, fj, fk = [], [], [], [], []
        for n in range(GROUP):
            gh = gh_ref[row + n * ROWS:row + (n + 1) * ROWS, :]
            g32 = gh.astype(F32)
            low, high = g32[:, 0:128], g32[:, 128:256]
            zero = jnp.zeros_like(low)
            swapped = jnp.concatenate([gh[:, 0:64], gh[:, 128:192], gh[:, 64:128], gh[:, 192:256]],
                                      axis=1).astype(F32)
            k_low, k_high = swapped[:, 0:128], swapped[:, 128:256]
            blank = jnp.zeros((16, LANES), BF)
            bwd.append(jnp.concatenate([
                gh,
                jnp.concatenate([blank, gh[0:112]], axis=0),
                jnp.concatenate([gh[16:128], blank], axis=0),
                jnp.where(last_j, zero, row_roll(low, -4)).astype(BF),
                jnp.where(first_j, zero, row_roll(high, 4)).astype(BF),
                jnp.where(last_k, zero, row_roll(k_low, -1)).astype(BF),
                jnp.where(first_k, zero, row_roll(k_high, 1)).astype(BF)], axis=1))
            f0.append(gh[0:16])
            f1.append(gh[112:128])
            fj.append(jnp.concatenate([pick_j(low, False), pick_j(high, True)], axis=1).astype(BF))
            g_scr[2 * n] = k_low
            g_scr[2 * n + 1] = k_high
            fk.append(jnp.concatenate([g_scr[2 * n, pl.ds(0, 32, stride=4), :],
                                       g_scr[2 * n + 1, pl.ds(3, 32, stride=4), :]],
                                      axis=1).astype(BF))
        for n in range(GROUP):
            gin_ref[row + n * ROWS:row + (n + 1) * ROWS, :] = dot(bwd[n], wt_ref[...])
        p0 = dot(jnp.concatenate(f0, axis=0), wt_ref[512:768, :]).astype(BF)
        p1 = dot(jnp.concatenate(f1, axis=0), wt_ref[256:512, :]).astype(BF)
        pj = dot(jnp.concatenate(fj, axis=0), wt_ref[768:1024, :]).astype(BF)
        pk = dot(jnp.concatenate(fk, axis=0), wt_ref[1024:1280, :]).astype(BF)
        for n in range(GROUP):
            base = (g * GROUP + n) * 6
            a, c = p0[n * 16:n * 16 + 16], p1[n * 16:n * 16 + 16]
            j, k = pj[n * 32:n * 32 + 32], pk[n * 32:n * 32 + 32]
            plane_ref[base] = jnp.concatenate([a[:, 0:128], a[:, 128:256]], axis=0)
            plane_ref[base + 1] = jnp.concatenate([c[:, 0:128], c[:, 128:256]], axis=0)
            plane_ref[base + 2] = j[:, 128:256]
            plane_ref[base + 3] = j[:, 0:128]
            plane_ref[base + 4] = jnp.concatenate([k[:, 64:128], k[:, 192:256]], axis=1)
            plane_ref[base + 5] = jnp.concatenate([k[:, 0:64], k[:, 128:192]], axis=1)

    for g in range(groups):
        backward(g)
        if g == 0:
            next(phases)
            send_out(1)
    for s in range(24):
        back_face[s // 4, s % 4] = plane_ref[lists[1, s]]
    chain[face_total + 24] = jnp.zeros((32, 128), F32)
    send_faces(regions, owners, my_r, my_s, True, back_face, ans_ref, hsend, hrecv)

    def add_plane(n, carry):
        chain[n] = chain[lists[2, n]] + plane_ref[n].astype(F32)
        return carry

    lax.fori_loop(0, face_total, add_plane, 0, unroll=4)
    next(phases)
    send_out(2)
    wait_faces(regions, owners, my_r, my_s, True, back_face, ans_ref, hsend, hrecv)
    for s in range(24):
        chain[face_total + s] = (chain[lists[2, face_total + s]]
                                 + ans_ref[s // 4, s % 4].astype(F32))
    loads[3].wait()
    lane = lax.broadcasted_iota(jnp.int32, (ROWS, LANES), 1)
    edge_k = lax.rem(lax.broadcasted_iota(jnp.int32, (ROWS, LANES), 0), 4) == jnp.where(
        lax.rem(lane, 128) < 64, 0, 3)

    def finish(g, carry):
        wides = []
        for n in range(GROUP):
            b = g * GROUP + n
            f = [chain[lists[3, b * 6 + d]] for d in range(6)]
            zero = jnp.zeros((ROWS, 128), F32)
            add_j = jnp.concatenate([jnp.where(first_j, spread_j(f[2], False), zero),
                                     jnp.where(last_j, spread_j(f[3], True), zero)], axis=1)
            for side in range(2):
                k0 = f[4] if side == 0 else pltpu.roll(f[4], 64, 1)
                k3 = f[5] if side == 1 else pltpu.roll(f[5], 64, 1)
                g_scr[2 * n + side, pl.ds(0, 32, stride=4), :] = k0
                g_scr[2 * n + side, pl.ds(3, 32, stride=4), :] = k3
            add_k = jnp.where(edge_k, jnp.concatenate([g_scr[2 * n], g_scr[2 * n + 1]], axis=1),
                              jnp.zeros((ROWS, LANES), F32))
            total = gin_ref[pl.ds(pl.multiple_of(b * ROWS, ROWS), ROWS), :] + add_j + add_k
            low = jnp.concatenate([f[0][0:16], f[0][16:32]], axis=1)
            high = jnp.concatenate([f[1][0:16], f[1][16:32]], axis=1)
            total = jnp.concatenate(
                [total[0:16] + low, total[16:112], total[112:128] + high], axis=0).astype(BF)
            flipped = total.T
            wides.append(jnp.concatenate([flipped[q * 64:q * 64 + 64] for q in range(4)], axis=1))
        out = dot(jnp.concatenate(wides, axis=0), order[...]).astype(BF)
        feat[pl.ds(g * GROUP, GROUP)] = out.reshape(GROUP, 64, 512)
        return carry

    lax.fori_loop(0, groups, finish, 0)
    leave = pltpu.make_async_copy(feat, grad_ref, lsem)
    leave.start()
    for _ in phases:
        pass
    leave.wait()
    keep.wait()
    wait_blocks(owners, my_r, my_s, pair, co_slots, blocks_out, csem.at[0], csem.at[1])


def sum_phases(regions, owners, my_r, my_s, grads, pair_got, half_sum, part_p, mine, total_ref, sem):
    core = lax.rem(my_s, 2)
    other = 1 - core
    width = owners // 2
    chips = regions * width
    chip = my_r * width + my_s // 2
    half = pair_got.shape[0]
    unit = mine.shape[0]
    used = half // unit
    partner = (my_r, my_s + 1 - 2 * core)

    def remote(src, dst, n, target):
        return pltpu.make_async_remote_copy(
            src_ref=src, dst_ref=dst, send_sem=sem.at[2 * n], recv_sem=sem.at[2 * n + 1],
            device_id=target, device_id_type=MESH)

    def spot(peer):
        return (peer // width, 2 * lax.rem(peer, width) + core)

    near = spot(lax.rem(chip + 1, chips))

    def sized(ref, count, n):
        part = ref.at[pl.ds(0, count * unit)]
        return remote(part, part, n, near)

    swap = remote(grads.at[pl.ds(other * half, half)], pair_got, 0, partner)
    swap.start()
    yield
    swap.wait()
    half_sum[...] = grads[pl.ds(core * half, half)] + pair_got[...]
    owns = chip < used
    mine_at = jnp.minimum(chip, used - 1) * unit

    def start_sum(n, carry):
        peer = lax.rem(chip + n, chips)

        @pl.when(peer < used)
        def _():
            remote(half_sum.at[pl.ds(jnp.minimum(peer, used - 1) * unit, unit)],
                   part_p.at[pl.ds(chip * unit, unit)], 1, spot(peer)).start()
        return carry

    lax.fori_loop(1, chips, start_sum, 0)
    yield
    out_at = core * half + mine_at

    @pl.when(owns)
    def _():
        sized(half_sum, used - 1, 1).wait_send()
        sized(part_p, chips - 1, 1).wait_recv()
        part_p[pl.ds(chip * unit, unit)] = half_sum[pl.ds(mine_at, unit)]
        run = part_p[0:unit]
        for n in range(1, chips):
            run = run + part_p[n * unit:n * unit + unit]
        mine[...] = run.astype(BF)
        total_ref[pl.ds(out_at, unit)] = run.astype(BF)

        def start_share(n, carry):
            remote(mine, total_ref.at[pl.ds(out_at, unit)], 2,
                   spot(lax.rem(chip + n, chips))).start()
            return carry

        lax.fori_loop(1, chips, start_share, 0)

    if used < chips:
        @pl.when(jnp.logical_not(owns))
        def _():
            sized(half_sum, used, 1).wait_send()
    yield

    @pl.when(owns)
    def _():
        sized(total_ref, chips - 1, 2).wait_send()
        sized(total_ref, used - 1, 2).wait_recv()

    if used < chips:
        @pl.when(jnp.logical_not(owns))
        def _():
            sized(total_ref, used, 2).wait_recv()

    own = pl.ds(core * half, half)
    remote(total_ref.at[own], total_ref.at[own], 3, partner).start()
    yield
    last = remote(total_ref.at[own], total_ref.at[pl.ds(other * half, half)], 3, partner)
    last.wait_send()
    last.wait_recv()


def result_kernel(slot_ref, made_ref, arr_ref, total_ref, grad_ref, out_ref, fine_ref, down_ref,
                  coarse_ref):
    out_ref[...] = jnp.zeros_like(out_ref)

    def put_block(s, carry):
        spot = slot_ref[s]

        @pl.when(spot >= 0)
        def _():
            out_ref[spot] = arr_ref[s]
        return carry

    lax.fori_loop(0, arr_ref.shape[0], put_block, 0, unroll=4)
    grad_ref[...] = made_ref[...]
    for tap in range(7):
        rows = total_ref[tap // 2 * 8:tap // 2 * 8 + 8].astype(F32).reshape(64, 128)
        fine_ref[tap] = rows[:, tap % 2 * 64:tap % 2 * 64 + 64]
    down_ref[...] = total_ref[32:96].astype(F32).reshape(512, 128)
    coarse_ref[...] = total_ref[96:112].astype(F32).reshape(128, 128)


def on_device(features, fine_weight, down_weight, coarse_weight, cotangent, face_source,
              face_requests, child_slot, parent_octant):
    regions = lax.axis_size("region")
    owners = lax.axis_size("space")
    count = regions * owners
    bricks, channels, volume = features.shape
    faces = bricks * 6
    parents, _, wide = cotangent.shape
    octant = volume // 8
    slots = parent_octant.shape[1]
    shape = jax.ShapeDtypeStruct
    vm = pltpu.VMEM
    dma = pltpu.SemaphoreType.DMA
    requests = face_requests.reshape(24)
    targets = parent_octant.reshape(slots)
    scale_fine = 1.0 / math.sqrt(bricks * count * volume)
    scale_coarse = 1.0 / math.sqrt(parents * count * volume)
    chips = count // 2
    unit = max(1, 56 // chips)
    big = bricks * ROWS
    small = bricks * octant
    block = (slots, octant, wide)
    faces4 = (6, 4, 32, 128)
    made, arrived, totals = pl.pallas_call(
        functools.partial(main_kernel, regions, owners, scale_fine, scale_coarse),
        out_shape=(shape((bricks, channels, volume), BF), shape(block, BF),
                   shape((112, 8, 128), BF)),
        in_specs=[SMEM_SPEC] * 4 + [ANY_SPEC] * 4 + [VMEM_SPEC] * 4,
        out_specs=(ANY_SPEC, ANY_SPEC, VMEM_SPEC),
        scratch_shapes=[
            vm((bricks, channels, volume), BF), vm(block, BF), vm((512, 512), BF),
            vm((512, 512), BF), vm((big, LANES), BF), vm((big, LANES), BF),
            vm((faces, 32, 128), BF), vm(faces4, BF), vm(faces4, BF), vm(block, BF), vm(block, BF),
            vm((1280, LANES), BF), vm((1280, LANES), BF), vm((big, 1280), BF),
            vm((small, 512), BF), vm((big, LANES), BF), vm((small, wide), BF),
            vm((small, wide), BF), vm((small, wide), BF),
            vm((bricks, octant, wide), BF), vm(block, BF), vm((big, LANES), F32),
            vm((small, wide), F32), vm((big, LANES), F32), vm((faces, 32, 128), BF),
            vm(faces4, BF), vm(faces4, BF), vm((faces + 25, 32, 128), F32),
            vm((GROUP, ROWS, 128), F32), vm((2 * GROUP, ROWS, 128), F32),
            vm((112, 8, 128), F32), vm((56, 8, 128), F32), vm((56, 8, 128), F32),
            vm((chips * unit, 8, 128), F32),
            vm((unit, 8, 128), BF), vm((8, 128), jnp.int32), pltpu.SMEM((8, 128), jnp.int32),
            dma((4,)), dma, dma((6,)), dma((6,)), dma((6,)), dma((6,)), dma, dma((2,)), dma((2,)),
            dma((8,))],
        compiler_params=pltpu.CompilerParams(
            collective_id=0, has_side_effects=True, vmem_limit_bytes=60 * 2**20),
        name="main",
    )(face_source.T, child_slot, requests, targets, features,
      cotangent.reshape(parents * 8, octant, wide), jnp.asarray(ORDER_T), jnp.asarray(ORDER),
      jnp.asarray(FACE), fine_weight, down_weight.reshape(8 * channels, wide), coarse_weight)
    grad_in, coarse_out, fine, down, coarse = pl.pallas_call(
        result_kernel,
        out_shape=(shape((bricks, channels, volume), BF), shape((parents * 8, octant, wide), BF),
                   shape((7, channels, channels), F32), shape((8 * channels, wide), F32),
                   shape((wide, wide), F32)),
        in_specs=[SMEM_SPEC] + [VMEM_SPEC] * 3,
        out_specs=(VMEM_SPEC,) * 5,
        compiler_params=pltpu.CompilerParams(vmem_limit_bytes=60 * 2**20),
        name="result",
    )(targets, made, arrived, totals)
    return (grad_in, coarse_out.reshape(parents, volume, wide), fine,
            down.reshape(8, channels, wide), coarse)


def solution(mesh):
    both = ("region", "space")
    return jax.shard_map(
        on_device,
        mesh=mesh,
        in_specs=(P(both, None, None), P(), P(), P(), P(both, None, None), P(both, None),
                  P(both, None), P(both), P(both, None)),
        out_specs=(P(both, None, None), P(both, None, None), P(), P(), P()),
        check_vma=False,
    )
```
